256 devices in a mesh: mode: 4 (over z_lo), ty: 8 (over y, core), tx: 8 (over z_hi, x).
Axes of the slice: x: 4, y: 4, z: 8 (z_hi: 2, z_lo: 4; z = z_hi * 4 + z_lo), core: 2. Of those that a mesh axis runs over, the one named last changes fastest.
Arguments:
- object_slices: float32 [4, 2, 1024, 1024], P(None, None, 'ty', 'tx'), may hold values from -4.2 to 4.2
- probe_modes: float32 [16, 2, 128, 128], P('mode'), may hold values from -1.5 to 1.5
- positions: int32 [8, 8, 1, 2], P('ty', 'tx'), may hold values from 0 to 128
- measured: float32 [8, 8, 1, 128, 128], P('ty', 'tx'), may hold values from 0.3 to 3
Outputs:
- object_gradient: float32 [4, 2, 1024, 1024], P('mode', None, 'ty', 'tx')
The draws below stay inside these ranges and needn't reach their ends.
Inputs may be any that keep to these rules, and one draw needn't show every extreme that they name: `positions`: pattern k of tile (a, b) has its 128 x 128 window inside that tile's region, which reaches 64 pixels beyond the tile on every side.
All inputs are finite; a program needn't handle non-finite values.
Results may differ from the reference program's by a relative error of at most 0.00016.
Values sent between devices are 32-bit elements; how exact they have to be, the bound alone decides.
A program may use at most 64 MiB of HBM per device.

```python
import math
import jax
import jax.numpy as jnp
from jax import lax

DET = 128
MODES = 16
SLICES = 4
TILE = 128
MARGIN = 64
PAT_DEV = 1
EXT = 256
TILES_Y = 8
TILES_X = 8
NY = 1024
NX = 1024


def place_ends(drawn, rng, least, high):
    longest = drawn.shape.index(max(drawn.shape))
    spots = []
    for shift in (0, 1):
        where = [jax.random.randint(jax.random.fold_in(rng, axis), (), 0, length) for axis, length in enumerate(drawn.shape)]
        where[longest] = (where[longest] + shift) % drawn.shape[longest]
        spots.append(tuple(where))
    return drawn.at[spots[0]].set(least).at[spots[1]].set(high)


def levels(own_key, shape, pieces, smallest, high):
    level, own = 1.0, jax.random.fold_in(own_key, 6)
    for dim, parts in pieces:
        heights = jnp.exp(jax.random.uniform(jax.random.fold_in(own, dim), (parts,), jnp.float32, smallest / len(pieces), high / len(pieces)))
        level = level * jnp.repeat(heights, shape[dim] // parts).reshape([-1 if axis == dim else 1 for axis in range(len(shape))])
    return level


def noise(rng, extent, spread, reach, pieces=(), kind=jnp.bfloat16):
    gain = levels(rng, extent, pieces, -0.22, 0.18) if pieces else 1.0
    entries = jax.random.normal(rng, extent, jnp.float32) * spread * gain
    return jnp.minimum(jnp.maximum(entries, -reach), reach).astype(kind)


def setup_inputs(seed: int = 0) -> dict:
    key_of = jax.random.split(jax.random.key(seed), 5)
    return {
        "object_slices": noise(key_of[0], (SLICES, 2, NY, NX), 0.7, 4.2, ((2, 8), (3, 8)), jnp.float32),
        "probe_modes": noise(key_of[1], (MODES, 2, DET, DET), 0.25, 1.5, ((0, 4),), jnp.float32),
        "positions": place_ends(jax.random.randint(key_of[2], (TILES_Y, TILES_X, PAT_DEV, 2), 0, EXT - DET + 1), jax.random.fold_in(key_of[2], 1), 0, EXT - DET).astype(jnp.int32),
        "measured": jnp.clip(jnp.exp(math.log(3.0) - 2.3025851 * jax.random.uniform(key_of[3], (TILES_Y, TILES_X, PAT_DEV, DET, DET), jnp.float32) ** levels(key_of[3], (TILES_Y, TILES_X, PAT_DEV, DET, DET), ((0, 8), (1, 8)), -0.2, 0.2)), 0.3, 3.0),
    }


fresnel_rate = 0.3

def chirp_phase(length, kind):
    counter = jnp.arange(length)
    frequency = jnp.where(counter < length // 2, counter, counter - length).astype(kind)
    return fresnel_rate * (frequency[:, None] ** 2 + frequency[None, :] ** 2) / length

def forward_fourier(field):
    return jnp.fft.fft2(field, norm='ortho')

def inverse_fourier(field):
    return jnp.fft.ifft2(field, norm='ortho')

def reference(object_slices, probe_modes, positions, measured):
    transmission = lax.complex(object_slices[:, 0], object_slices[:, 1])
    transmission = jnp.pad(transmission, ((0, 0), (MARGIN, MARGIN), (MARGIN, MARGIN)))
    illumination = lax.complex(probe_modes[:, 0], probe_modes[:, 1])
    phase = chirp_phase(DET, jnp.float32)
    kernel = lax.complex(jnp.cos(phase), -jnp.sin(phase))
    row_start = (positions[..., 0] + TILE * jnp.arange(TILES_Y, dtype=jnp.int32)[:, None, None]).reshape(-1).astype(jnp.int32)
    col_start = (positions[..., 1] + TILE * jnp.arange(TILES_X, dtype=jnp.int32)[None, :, None]).reshape(-1).astype(jnp.int32)
    amplitudes = measured.reshape(-1, DET, DET)

    def accumulate(summed, item):
        row, column, amplitude = item
        anchor = (jnp.int32(0), row, column)
        window = lax.dynamic_slice(transmission, anchor, (SLICES, DET, DET))
        wavefield = illumination
        incident = []
        farfield = wavefield
        for layer_index in range(SLICES):
            incident.append(wavefield)
            leaving = wavefield * window[layer_index]
            if layer_index + 1 < SLICES:
                wavefield = inverse_fourier(kernel * forward_fourier(leaving))
            else:
                farfield = forward_fourier(leaving)
        intensity = lax.optimization_barrier(jnp.sum(jnp.real(farfield) ** 2 + jnp.imag(farfield) ** 2, axis=0))
        weight = 1.0 - amplitude / jnp.maximum(jnp.sqrt(intensity), 1.0)
        backward = inverse_fourier(weight * farfield)
        gradients = [None] * SLICES
        for layer_index in reversed(range(SLICES)):
            gradients[layer_index] = lax.optimization_barrier(jnp.sum(jnp.conj(incident[layer_index]) * backward, axis=0))
            if layer_index > 0:
                backward = inverse_fourier(jnp.conj(kernel) * forward_fourier(jnp.conj(window[layer_index]) * backward))
        update = jnp.stack(gradients)
        current = lax.dynamic_slice(summed, anchor, (SLICES, DET, DET))
        return (lax.dynamic_update_slice(summed, current + update, anchor), None)
    summed, ignored = lax.scan(accumulate, jnp.zeros_like(transmission), (row_start, col_start, amplitudes))
    inner = summed[:, MARGIN:MARGIN + NY, MARGIN:MARGIN + NX]
    return jnp.stack([jnp.real(inner), jnp.imag(inner)], axis=1)
```

```python
import functools

import numpy as np
import jax
import jax.numpy as jnp
from jax import lax
from jax.experimental import pallas as pl
from jax.experimental.pallas import tpu as pltpu
from jax.sharding import PartitionSpec as P

DET = 128
SLICES = 4
MARGIN = 64
LOCAL = 4
RATE = 0.3
F32 = jnp.float32
BF16 = jnp.bfloat16


def real_block(matrix):
    return np.block([[matrix.real, matrix.imag], [-matrix.imag, matrix.real]])


def tables():
    counter = np.arange(DET)
    fourier = np.exp(-2j * np.pi * (np.outer(counter, counter) % DET) / DET) / np.sqrt(DET)
    frequency = np.where(counter < DET // 2, counter, counter - DET).astype(np.float64)
    chirp = np.exp(-1j * RATE * frequency**2 / DET)
    step = fourier.conj() @ (chirp[:, None] * fourier)
    step = (step + step.T) / 2
    out = []
    for matrix in (step, step.conj(), fourier, fourier.conj()):
        block = real_block(matrix).astype(np.float32)
        high = block.astype(jnp.bfloat16)
        low = (block - high.astype(np.float32)).astype(jnp.bfloat16)
        out += [high, low]
    return np.stack(out)


STEP, STEP_BACK, FAR, FAR_BACK = range(4)
CONJ = {STEP: STEP_BACK, STEP_BACK: STEP, FAR: FAR_BACK, FAR_BACK: FAR}


def halves(x):
    high = x.astype(BF16)
    return high, (x - high.astype(F32)).astype(BF16)


def rows(m):
    return slice(m * DET, (m + 1) * DET)


def right_product(mats, which, real, imag):
    rh, rl = halves(real)
    ih, il = halves(imag)
    lhs = jnp.concatenate([rh, ih, rl, il, rh, ih], axis=1)
    high, low = mats[2 * which], mats[2 * which + 1]
    rhs = jnp.concatenate([high, high, low], axis=0)
    return jnp.dot(lhs, rhs, preferred_element_type=F32)


def left_product(mats, which, stacked):
    conj = CONJ[which]
    high, low = mats[2 * conj], mats[2 * conj + 1]
    lhs = jnp.concatenate([high, high, low], axis=1)
    rhs = jnp.concatenate([stacked, stacked[: 2 * DET]], axis=0)
    return jnp.dot(lhs, rhs, preferred_element_type=F32)


def two_sided(mats, which, fetch, deliver, mid):
    for m in range(LOCAL):
        real, imag = fetch(m)
        out = right_product(mats, which, real, imag)
        rh, rl = halves(out[:, :DET])
        ih, il = halves(out[:, DET:])
        for part, value in enumerate((rh, ih, rl, il)):
            mid[rows(part), rows(m)] = value
    for pair in range(LOCAL // 2):
        out = left_product(mats, which, mid[:, pair * 2 * DET : (pair + 1) * 2 * DET])
        for k in range(2):
            deliver(2 * pair + k, out[:DET, rows(k)], out[DET:, rows(k)])


def forward_kernel(pos_ref, ext_ref, probe_ref, mats, window_ref, psi_ref, far_ref, part_ref, mid):
    row, col = pos_ref[0], pos_ref[1]
    shift = lax.rem(2 * DET - col, 2 * DET)
    group = jnp.minimum(row // 8, DET // 8 - 1)
    lift = DET + 8 - (row - 8 * group)
    for s in range(SLICES):
        for c in range(2):
            band = ext_ref[s, c, pl.ds(pl.multiple_of(8 * group, 8), DET + 8), :]
            band = pltpu.roll(band, lift, 0)[:DET]
            window_ref[s, c] = pltpu.roll(band, shift, 1)[:, :DET]
    for s in range(SLICES):

        def fetch(m):
            if s == 0:
                real, imag = probe_ref[m, 0], probe_ref[m, 1]
            else:
                real, imag = psi_ref[s - 1, 0, rows(m)], psi_ref[s - 1, 1, rows(m)]
            wr, wi = window_ref[s, 0], window_ref[s, 1]
            return real * wr - imag * wi, real * wi + imag * wr

        def deliver(m, real, imag):
            if s + 1 < SLICES:
                psi_ref[s, 0, rows(m)] = real
                psi_ref[s, 1, rows(m)] = imag
            else:
                far_ref[0, rows(m)] = real
                far_ref[1, rows(m)] = imag
                power = real * real + imag * imag
                part_ref[...] = power if m == 0 else part_ref[...] + power

        two_sided(mats, STEP if s + 1 < SLICES else FAR, fetch, deliver, mid)


def backward_kernel(window_ref, psi_ref, far_ref, probe_ref, whole_ref, measured_ref, mats, term_ref, pulled, mid):
    weight = 1.0 - measured_ref[...] / jnp.maximum(jnp.sqrt(whole_ref[...]), 1.0)
    for s in reversed(range(SLICES)):

        def fetch(m):
            if s == SLICES - 1:
                return weight * far_ref[0, rows(m)], weight * far_ref[1, rows(m)]
            return pulled[0, rows(m)], pulled[1, rows(m)]

        def deliver(m, real, imag):
            if s == 0:
                pr, pi = probe_ref[m, 0], probe_ref[m, 1]
            else:
                pr, pi = psi_ref[s - 1, 0, rows(m)], psi_ref[s - 1, 1, rows(m)]
            tr, ti = pr * real + pi * imag, pr * imag - pi * real
            term_ref[s, 0] = tr if m == 0 else term_ref[s, 0] + tr
            term_ref[s, 1] = ti if m == 0 else term_ref[s, 1] + ti
            if s > 0:
                wr, wi = window_ref[s, 0], window_ref[s, 1]
                pulled[0, rows(m)] = wr * real + wi * imag
                pulled[1, rows(m)] = wr * imag - wi * real

        two_sided(mats, FAR_BACK if s == SLICES - 1 else STEP_BACK, fetch, deliver, mid)


VMEM = pl.BlockSpec(memory_space=pltpu.VMEM)
SMEM = pl.BlockSpec(memory_space=pltpu.SMEM)


def forward(pos, ext, probe, mats):
    return pl.pallas_call(
        forward_kernel,
        out_shape=(
            jax.ShapeDtypeStruct((SLICES, 2, DET, DET), F32),
            jax.ShapeDtypeStruct((SLICES - 1, 2, LOCAL * DET, DET), F32),
            jax.ShapeDtypeStruct((2, LOCAL * DET, DET), F32),
            jax.ShapeDtypeStruct((DET, DET), F32),
        ),
        in_specs=[SMEM, VMEM, VMEM, VMEM],
        out_specs=(VMEM,) * 4,
        scratch_shapes=[pltpu.VMEM((4 * DET, LOCAL * DET), BF16)],
        name="forward",
    )(pos, ext, probe, mats)


def backward(window, psi, far, probe, whole, measured, mats):
    return pl.pallas_call(
        backward_kernel,
        out_shape=jax.ShapeDtypeStruct((SLICES, 2, DET, DET), F32),
        in_specs=[VMEM] * 7,
        out_specs=VMEM,
        scratch_shapes=[pltpu.VMEM((2, LOCAL * DET, DET), F32), pltpu.VMEM((4 * DET, LOCAL * DET), BF16)],
        name="backward",
    )(window, psi, far, probe, whole, measured, mats)


def shifted(block, axis, distance):
    devices = range(lax.axis_size(axis))
    route = [(i - distance, i) for i in devices if i - distance in devices]
    return lax.ppermute(block, axis, route)


def extended(shard, sides, width):
    for axis, dim in sides:
        size, length = (lax.axis_size(axis), shard.shape[dim])
        up = [(i, (i + 1) % size) for i in range(size - 1)]
        down = [(j, i) for i, j in up]
        last = lax.slice_in_dim(shard, length - width, length, axis=dim)
        leading = lax.slice_in_dim(shard, 0, width, axis=dim)
        before = lax.ppermute(last, axis, up)
        after = lax.ppermute(leading, axis, down)
        shard = jnp.concatenate([before, shard, after], axis=dim)
    return shard


def border_sum(gradient):
    upper = gradient[:, :, :MARGIN, :]
    lower = gradient[:, :, -MARGIN:, :]
    from_next = shifted(upper, "ty", -1)
    from_prior = shifted(lower, "ty", 1)
    middle = gradient[:, :, MARGIN:-MARGIN, :]
    middle = middle.at[:, :, :MARGIN, :].add(from_prior)
    middle = middle.at[:, :, -MARGIN:, :].add(from_next)
    left_strip = middle[:, :, :, :MARGIN]
    right_strip = middle[:, :, :, -MARGIN:]
    from_right = shifted(left_strip, "tx", -1)
    from_left = shifted(right_strip, "tx", 1)
    interior = middle[:, :, :, MARGIN:-MARGIN]
    interior = interior.at[:, :, :, :MARGIN].add(from_left)
    interior = interior.at[:, :, :, -MARGIN:].add(from_right)
    return interior


def body(object_slices, probe_modes, positions, measured):
    mats = jnp.asarray(tables())
    pos = positions.reshape(2)
    ext = extended(object_slices, (("ty", 2), ("tx", 3)), MARGIN)
    window, psi, far, part = forward(pos, ext, probe_modes, mats)
    copies = jnp.broadcast_to(part, (lax.axis_size("mode"), DET, DET))
    whole = jnp.sum(lax.all_to_all(copies, "mode", split_axis=0, concat_axis=0, tiled=True), axis=0)
    terms = backward(window, psi, far, probe_modes, whole, measured[0, 0, 0], mats)
    arrived = lax.all_to_all(terms, "mode", split_axis=0, concat_axis=0, tiled=True)
    mine = jnp.sum(arrived.reshape(lax.axis_size("mode"), 1, 2, DET, DET), axis=0)
    gradient = jnp.zeros((1, 2, 2 * DET, 2 * DET), F32)
    gradient = lax.dynamic_update_slice(gradient, mine, (0, 0, pos[0], pos[1]))
    return border_sum(gradient)


def solution(mesh):
    return jax.shard_map(
        body,
        mesh=mesh,
        in_specs=(
            P(None, None, "ty", "tx"),
            P("mode", None, None, None),
            P("ty", "tx", None, None),
            P("ty", "tx", None, None, None),
        ),
        out_specs=P("mode", None, "ty", "tx"),
        check_vma=False,
    )
```

```python
import functools

import numpy as np
import jax
import jax.numpy as jnp
from jax import lax
from jax.experimental import pallas as pl
from jax.experimental.pallas import tpu as pltpu
from jax.sharding import PartitionSpec as P

DET = 128
SLICES = 4
MARGIN = 64
LOCAL = 4
RATE = 0.3
F32 = jnp.float32
BF16 = jnp.bfloat16


def real_block(matrix):
    return np.block([[matrix.real, matrix.imag], [-matrix.imag, matrix.real]])


def tables():
    counter = np.arange(DET)
    fourier = np.exp(-2j * np.pi * (np.outer(counter, counter) % DET) / DET) / np.sqrt(DET)
    frequency = np.where(counter < DET // 2, counter, counter - DET).astype(np.float64)
    chirp = np.exp(-1j * RATE * frequency**2 / DET)
    step = fourier.conj() @ (chirp[:, None] * fourier)
    step = (step + step.T) / 2
    out = []
    for matrix in (step, step.conj(), fourier, fourier.conj()):
        block = real_block(matrix).astype(np.float32)
        high = block.astype(jnp.bfloat16)
        low = (block - high.astype(np.float32)).astype(jnp.bfloat16)
        out += [high, low]
    return np.stack(out)


STEP, STEP_BACK, FAR, FAR_BACK = range(4)
CONJ = {STEP: STEP_BACK, STEP_BACK: STEP, FAR: FAR_BACK, FAR_BACK: FAR}


def halves(x):
    high = x.astype(BF16)
    return high, (x - high.astype(F32)).astype(BF16)


def rows(m):
    return slice(m * DET, (m + 1) * DET)


def right_product(mats, which, real, imag):
    rh, rl = halves(real)
    ih, il = halves(imag)
    lhs = jnp.concatenate([rh, ih, rl, il, rh, ih], axis=1)
    high, low = mats[2 * which], mats[2 * which + 1]
    rhs = jnp.concatenate([high, high, low], axis=0)
    return jnp.dot(lhs, rhs, preferred_element_type=F32)


def left_product(mats, which, stacked):
    conj = CONJ[which]
    high, low = mats[2 * conj], mats[2 * conj + 1]
    lhs = jnp.concatenate([high, high, low], axis=1)
    rhs = jnp.concatenate([stacked, stacked[: 2 * DET]], axis=0)
    return jnp.dot(lhs, rhs, preferred_element_type=F32)


def two_sided(mats, which, fetch, deliver, mid):
    for m in range(LOCAL):
        real, imag = fetch(m)
        out = right_product(mats, which, real, imag)
        rh, rl = halves(out[:, :DET])
        ih, il = halves(out[:, DET:])
        for part, value in enumerate((rh, ih, rl, il)):
            mid[rows(part), rows(m)] = value
    for pair in range(LOCAL // 2):
        out = left_product(mats, which, mid[:, pair * 2 * DET : (pair + 1) * 2 * DET])
        for k in range(2):
            deliver(2 * pair + k, out[:DET, rows(k)], out[DET:, rows(k)])


MESH = pl.DeviceIdType.MESH
HALF = DET // 2
BLOCK = HALF // 2


def lane_low(shape):
    return lax.broadcasted_iota(jnp.int32, shape, len(shape) - 1) < HALF


def turned(x):
    return pltpu.roll(x, HALF, x.ndim - 1)


def packed_edges(strip):
    first, second = strip[:BLOCK], strip[BLOCK:]
    low = lane_low(first.shape)
    left_edge = jnp.where(low, first, turned(second))
    right_edge = jnp.where(low, turned(first), second)
    return left_edge, right_edge


def unpacked_sides(from_left, from_right):
    low = lane_low(from_left.shape)
    first = jnp.where(low, from_right, turned(from_left))
    second = jnp.where(low, turned(from_right), from_left)
    return first, second


LEFT, RIGHT, UP, DOWN, UP_CORNER, DOWN_CORNER = range(6)


def kernel(
    pos_ref, obj, probe, measured, mats, out,
    pk, rs, vt, cr, ext, window, psi, far, part, others, mid, pulled, term, parts, grid, gv, middle, hp, gh,
    halo_send, halo_recv, mode_send, mode_recv, term_send, term_recv, grad_send, grad_recv,
):
    mode, ty, tx = lax.axis_index("mode"), lax.axis_index("ty"), lax.axis_index("tx")
    modes, tys, txs = lax.axis_size("mode"), lax.axis_size("ty"), lax.axis_size("tx")
    has = {LEFT: tx > 0, RIGHT: tx < txs - 1, UP: ty > 0, DOWN: ty < tys - 1}
    has[UP_CORNER], has[DOWN_CORNER] = has[UP], has[DOWN]
    cross_right, cross_left = tx == txs // 2 - 1, tx == txs // 2
    mirror = modes - 1 - mode
    left_mode = jnp.where(cross_left, mirror, mode)
    right_mode = jnp.where(cross_right, mirror, mode)
    target = {
        LEFT: {"mode": left_mode, "ty": ty, "tx": tx - 1},
        RIGHT: {"mode": right_mode, "ty": ty, "tx": tx + 1},
        UP: {"mode": mode, "ty": ty - 1, "tx": tx},
        DOWN: {"mode": mode, "ty": ty + 1, "tx": tx},
    }
    direct = {LEFT: {"mode": mode, "ty": ty, "tx": tx - 1}, RIGHT: {"mode": mode, "ty": ty, "tx": tx + 1}}

    def peer(step):
        return {"mode": lax.rem(mode + step, modes), "ty": ty, "tx": tx}

    for side in (LEFT, RIGHT):

        @pl.when(jnp.logical_not(has[side]))
        def _():
            rs[:, side] = jnp.zeros_like(rs[:, side])
            gh[side] = jnp.zeros_like(gh[side])

    for side in (UP, DOWN):

        @pl.when(jnp.logical_not(has[side]))
        def _():
            vt[:, side - UP] = jnp.zeros_like(vt[:, side - UP])
            cr[:, side - UP] = jnp.zeros_like(cr[:, side - UP])
            gv[side - UP] = jnp.zeros_like(gv[side - UP])

    for s in range(SLICES):
        for c in range(2):
            for b in range(2):
                left_edge, right_edge = packed_edges(obj[s, c, b * HALF : (b + 1) * HALF])
                pk[s, LEFT, c, b * BLOCK : (b + 1) * BLOCK] = left_edge
                pk[s, RIGHT, c, b * BLOCK : (b + 1) * BLOCK] = right_edge

    barrier = pltpu.get_barrier_semaphore()
    count = jnp.int32(modes - 1)
    for side in (LEFT, RIGHT, UP, DOWN):
        count = count + has[side].astype(jnp.int32)

        @pl.when(has[side])
        def _():
            pl.semaphore_signal(barrier, inc=1, device_id=target[side], device_id_type=MESH)

    for side, cross in ((LEFT, cross_left), (RIGHT, cross_right)):
        far_pair = jnp.logical_and(cross, has[side])
        count = count + far_pair.astype(jnp.int32)

        @pl.when(far_pair)
        def _():
            pl.semaphore_signal(barrier, inc=1, device_id=direct[side], device_id_type=MESH)

    for step in range(1, modes):
        pl.semaphore_signal(barrier, inc=1, device_id=peer(step), device_id_type=MESH)
    pl.semaphore_wait(barrier, count)

    opposite = {LEFT: RIGHT, RIGHT: LEFT, UP: DOWN, DOWN: UP, UP_CORNER: DOWN_CORNER, DOWN_CORNER: UP_CORNER}

    def landing(s, kind):
        if kind in (LEFT, RIGHT):
            return rs.at[s, kind]
        if kind in (UP, DOWN):
            return vt.at[s, kind - UP]
        return cr.at[s, kind - UP_CORNER]

    def source(s, kind):
        if kind in (LEFT, RIGHT):
            return pk.at[s, kind]
        if kind in (UP, DOWN):
            return obj.at[s, :, (kind - UP) * HALF : (kind - UP + 1) * HALF]
        return rs.at[s, :, :, (kind - UP_CORNER) * BLOCK : (kind - UP_CORNER + 1) * BLOCK]

    def halo_copy(s, kind):
        return pltpu.make_async_remote_copy(
            src_ref=source(s, kind),
            dst_ref=landing(s, opposite[kind]),
            send_sem=halo_send.at[s, kind],
            recv_sem=halo_recv.at[s, opposite[kind]],
            device_id=target[kind if kind < UP_CORNER else kind - 2],
            device_id_type=MESH,
        )

    def start_halo(s, kind):
        @pl.when(has[kind])
        def _():
            halo_copy(s, kind).start()

    def await_halo(s, kind):
        @pl.when(has[kind])
        def _():
            halo_copy(s, opposite[kind]).wait_recv()

    for s in range(SLICES):
        for kind in (LEFT, RIGHT, UP, DOWN):
            start_halo(s, kind)

    def relay_corners(s):
        await_halo(s, LEFT)
        await_halo(s, RIGHT)
        start_halo(s, UP_CORNER)
        start_halo(s, DOWN_CORNER)

    row, col = pos_ref[0], pos_ref[1]
    here, there = (lax.broadcasted_iota(jnp.int32, (DET, 2 * DET), d) for d in range(2))
    pick_rows = jnp.where(there == here + row, 1.0, 0.0).astype(BF16)
    offset = here + (col + 2 * DET - HALF)
    offset = jnp.where(offset >= 2 * DET, offset - 2 * DET, offset)
    pick_cols = jnp.where(there == offset, 1.0, 0.0).astype(BF16)
    here, there = (lax.broadcasted_iota(jnp.int32, (2 * DET, DET), d) for d in range(2))
    put_rows = jnp.where(here == there + row, 1.0, 0.0).astype(BF16)
    offset = there + (col + 2 * DET - HALF)
    offset = jnp.where(offset >= 2 * DET, offset - 2 * DET, offset)
    put_cols = jnp.where(here == offset, 1.0, 0.0).astype(BF16)

    def twice(x, axis):
        return jnp.concatenate([x, x], axis=axis)

    def both(x, axis):
        return jnp.concatenate(halves(x), axis=axis)

    def dot(x, y):
        return jnp.dot(x, y, preferred_element_type=F32)

    def build_window(s):
        for kind in (UP, DOWN, UP_CORNER, DOWN_CORNER):
            await_halo(s, kind)
        for c in range(2):
            for side in range(2):
                at = side * 3 * HALF
                ext[c, at : at + HALF, :DET] = vt[s, side, c]
                first, second = unpacked_sides(cr[s, side, LEFT, c], cr[s, side, RIGHT, c])
                ext[c, at : at + BLOCK, DET:] = first
                ext[c, at + BLOCK : at + HALF, DET:] = second
            ext[c, HALF : 3 * HALF, :DET] = obj[s, c]
            for b in range(2):
                block = slice(b * BLOCK, (b + 1) * BLOCK)
                first, second = unpacked_sides(rs[s, LEFT, c, block], rs[s, RIGHT, c, block])
                at = HALF + b * HALF
                ext[c, at : at + BLOCK, DET:] = first
                ext[c, at + BLOCK : at + HALF, DET:] = second
            band = dot(twice(pick_rows, 1), both(ext[c], 0))
            window[s, c] = dot(both(band, 1), twice(put_cols, 0))

    relay_corners(0)
    for s in range(SLICES):
        if s + 1 < SLICES:
            relay_corners(s + 1)
        build_window(s)

        def fetch(m):
            if s == 0:
                real, imag = probe[m, 0], probe[m, 1]
            else:
                real, imag = psi[s - 1, 0, rows(m)], psi[s - 1, 1, rows(m)]
            wr, wi = window[s, 0], window[s, 1]
            return real * wr - imag * wi, real * wi + imag * wr

        def deliver(m, real, imag):
            if s + 1 < SLICES:
                psi[s, 0, rows(m)] = real
                psi[s, 1, rows(m)] = imag
            else:
                far[0, rows(m)] = real
                far[1, rows(m)] = imag
                power = real * real + imag * imag
                part[...] = power if m == 0 else part[...] + power

        two_sided(mats, STEP if s + 1 < SLICES else FAR, fetch, deliver, mid)

    def mode_copy(step):
        return pltpu.make_async_remote_copy(
            src_ref=part,
            dst_ref=others.at[step - 1],
            send_sem=mode_send.at[step - 1],
            recv_sem=mode_recv.at[step - 1],
            device_id=peer(step),
            device_id_type=MESH,
        )

    for step in range(1, modes):
        mode_copy(step).start()
    whole = part[...]
    for step in range(1, modes):
        mode_copy(step).wait_recv()
        whole = whole + others[step - 1]
    weight = 1.0 - measured[0, 0, 0] / jnp.maximum(jnp.sqrt(whole), 1.0)

    def term_copy(s):
        slot = lax.rem(s - mode + modes, modes) - 1
        return pltpu.make_async_remote_copy(
            src_ref=term.at[s],
            dst_ref=parts.at[slot],
            send_sem=term_send.at[s],
            recv_sem=term_recv.at[slot],
            device_id={"mode": s, "ty": ty, "tx": tx},
            device_id_type=MESH,
        )

    for s in reversed(range(SLICES)):

        def fetch(m):
            if s == SLICES - 1:
                return weight * far[0, rows(m)], weight * far[1, rows(m)]
            return pulled[0, rows(m)], pulled[1, rows(m)]

        def deliver(m, real, imag):
            if s == 0:
                pr, pi = probe[m, 0], probe[m, 1]
            else:
                pr, pi = psi[s - 1, 0, rows(m)], psi[s - 1, 1, rows(m)]
            tr, ti = pr * real + pi * imag, pr * imag - pi * real
            term[s, 0] = tr if m == 0 else term[s, 0] + tr
            term[s, 1] = ti if m == 0 else term[s, 1] + ti
            if s > 0:
                wr, wi = window[s, 0], window[s, 1]
                pulled[0, rows(m)] = wr * real + wi * imag
                pulled[1, rows(m)] = wr * imag - wi * real

        two_sided(mats, FAR_BACK if s == SLICES - 1 else STEP_BACK, fetch, deliver, mid)

        @pl.when(mode != s)
        def _():
            term_copy(s).start()

    for step in range(1, modes):
        pltpu.make_async_remote_copy(
            src_ref=term.at[0],
            dst_ref=parts.at[step - 1],
            send_sem=term_send.at[0],
            recv_sem=term_recv.at[step - 1],
            device_id=peer(step),
            device_id_type=MESH,
        ).wait_recv()

    for c in range(2):
        mine = term[mode, c]
        for step in range(1, modes):
            mine = mine + parts[step - 1, c]
        tall = dot(twice(put_rows, 1), both(mine, 0))
        grid[c] = dot(both(tall, 1), twice(pick_cols, 0))

    def grad_copy(kind):
        if kind in (UP, DOWN):
            at = (kind - UP) * 3 * HALF
            src, dst = grid.at[:, at : at + HALF], gv.at[opposite[kind] - UP]
            where = target[kind]
        else:
            src, dst = hp.at[kind], gh.at[opposite[kind]]
            where = direct[kind]
        return pltpu.make_async_remote_copy(
            src_ref=src,
            dst_ref=dst,
            send_sem=grad_send.at[kind],
            recv_sem=grad_recv.at[opposite[kind]],
            device_id=where,
            device_id_type=MESH,
        )

    def exchange(kinds):
        for kind in kinds:

            @pl.when(has[kind])
            def _():
                grad_copy(kind).start()

        for kind in kinds:

            @pl.when(has[kind])
            def _():
                grad_copy(opposite[kind]).wait_recv()

    exchange((UP, DOWN))
    for c in range(2):
        for b in range(2):
            block = slice(b * HALF, (b + 1) * HALF)
            middle[c, block] = grid[c, HALF + b * HALF : 2 * HALF + b * HALF] + gv[b, c]
        upper, lower = middle[c, :HALF, DET:], middle[c, HALF:, DET:]
        low = lane_low(upper.shape)
        hp[RIGHT, c] = jnp.where(low, upper, turned(lower))
        hp[LEFT, c] = jnp.where(low, turned(upper), lower)
    exchange((LEFT, RIGHT))
    for c in range(2):
        low = lane_low(gh[LEFT, c].shape)
        out[0, c, :HALF] = middle[c, :HALF, :DET] + jnp.where(low, gh[LEFT, c], turned(gh[RIGHT, c]))
        out[0, c, HALF:] = middle[c, HALF:, :DET] + jnp.where(low, turned(gh[LEFT, c]), gh[RIGHT, c])

    for kind in range(6):

        @pl.when(has[kind])
        def _():
            for s in range(SLICES):
                halo_copy(s, kind).wait_send()
            if kind < UP_CORNER:
                grad_copy(kind).wait_send()

    for step in range(1, modes):
        mode_copy(step).wait_send()
    for s in range(SLICES):

        @pl.when(mode != s)
        def _():
            term_copy(s).wait_send()


VMEM = pl.BlockSpec(memory_space=pltpu.VMEM)
SMEM = pl.BlockSpec(memory_space=pltpu.SMEM)


def body(object_slices, probe_modes, positions, measured):
    mats = jnp.asarray(tables())
    modes = lax.axis_size("mode")
    dma = pltpu.SemaphoreType.DMA
    wave = (LOCAL * DET, DET)
    scratch = dict(
        pk=(SLICES, 2, 2, HALF, DET),
        rs=(SLICES, 2, 2, HALF, DET),
        vt=(SLICES, 2, 2, HALF, DET),
        cr=(SLICES, 2, 2, 2, BLOCK, DET),
        ext=(2, 2 * DET, 2 * DET),
        window=(SLICES, 2, DET, DET),
        psi=(SLICES - 1, 2, *wave),
        far=(2, *wave),
        part=(DET, DET),
        others=(modes - 1, DET, DET),
        mid=(4 * DET, LOCAL * DET),
        pulled=(2, *wave),
        term=(SLICES, 2, DET, DET),
        parts=(modes - 1, 2, DET, DET),
        grid=(2, 2 * DET, 2 * DET),
        gv=(2, 2, HALF, 2 * DET),
        middle=(2, DET, 2 * DET),
        hp=(2, 2, HALF, DET),
        gh=(2, 2, HALF, DET),
    )
    return pl.pallas_call(
        kernel,
        out_shape=jax.ShapeDtypeStruct((1, 2, DET, DET), F32),
        in_specs=[SMEM, VMEM, VMEM, VMEM, VMEM],
        out_specs=VMEM,
        scratch_shapes=[pltpu.VMEM(shape, BF16 if name == "mid" else F32) for name, shape in scratch.items()]
        + [dma((SLICES, 6)), dma((SLICES, 6))]
        + [dma((modes - 1,)), dma((modes - 1,))]
        + [dma((SLICES,)), dma((modes - 1,))]
        + [dma((4,)), dma((4,))],
        compiler_params=pltpu.CompilerParams(collective_id=0, has_side_effects=True),
        name="ptycho",
    )(positions.reshape(2), object_slices, probe_modes, measured, mats)


def solution(mesh):
    return jax.shard_map(
        body,
        mesh=mesh,
        in_specs=(
            P(None, None, "ty", "tx"),
            P("mode", None, None, None),
            P("ty", "tx", None, None),
            P("ty", "tx", None, None, None),
        ),
        out_specs=P("mode", None, "ty", "tx"),
        check_vma=False,
    )
```

```python
import functools

import numpy as np
import jax
import jax.numpy as jnp
from jax import lax
from jax.experimental import pallas as pl
from jax.experimental.pallas import tpu as pltpu
from jax.sharding import PartitionSpec as P

DET = 128
SLICES = 4
MARGIN = 64
LOCAL = 4
RATE = 0.3
F32 = jnp.float32
BF16 = jnp.bfloat16


def real_block(matrix):
    return np.block([[matrix.real, matrix.imag], [-matrix.imag, matrix.real]])


def tables():
    counter = np.arange(DET)
    fourier = np.exp(-2j * np.pi * (np.outer(counter, counter) % DET) / DET) / np.sqrt(DET)
    frequency = np.where(counter < DET // 2, counter, counter - DET).astype(np.float64)
    chirp = np.exp(-1j * RATE * frequency**2 / DET)
    step = fourier.conj() @ (chirp[:, None] * fourier)
    step = (step + step.T) / 2
    out = []
    for matrix in (step, step.conj(), fourier, fourier.conj()):
        block = real_block(matrix).astype(np.float32)
        high = block.astype(jnp.bfloat16)
        low = (block - high.astype(np.float32)).astype(jnp.bfloat16)
        out += [high, low]
    return np.stack(out)


STEP, STEP_BACK, FAR, FAR_BACK = range(4)
CONJ = {STEP: STEP_BACK, STEP_BACK: STEP, FAR: FAR_BACK, FAR_BACK: FAR}


def halves(x):
    high = x.astype(BF16)
    return high, (x - high.astype(F32)).astype(BF16)


def rows(m):
    return slice(m * DET, (m + 1) * DET)


def right_product(mats, which, real, imag):
    rh, rl = halves(real)
    ih, il = halves(imag)
    lhs = jnp.concatenate([rh, ih, rl, il, rh, ih], axis=1)
    high, low = mats[2 * which], mats[2 * which + 1]
    rhs = jnp.concatenate([high, high, low], axis=0)
    return jnp.dot(lhs, rhs, preferred_element_type=F32)


def left_product(mats, which, stacked):
    conj = CONJ[which]
    high, low = mats[2 * conj], mats[2 * conj + 1]
    main = jnp.dot(jnp.concatenate([high, low], axis=0), stacked[: 2 * DET], preferred_element_type=F32)
    rest = jnp.dot(high, stacked[2 * DET :], preferred_element_type=F32)
    return main[: 2 * DET] + main[2 * DET :] + rest


def two_sided(mats, which, fetch, deliver, mid):
    for m in range(LOCAL):
        real, imag = fetch(m)
        out = right_product(mats, which, real, imag)
        rh, rl = halves(out[:, :DET])
        ih, il = halves(out[:, DET:])
        for part, value in enumerate((rh, ih, rl, il)):
            mid[rows(part), rows(m)] = value
    for pair in range(LOCAL // 2):
        out = left_product(mats, which, mid[:, pair * 2 * DET : (pair + 1) * 2 * DET])
        for k in range(2):
            deliver(2 * pair + k, out[:DET, rows(k)], out[DET:, rows(k)])

MESH = pl.DeviceIdType.MESH
HALF = DET // 2
BLOCK = HALF // 2


def lane_low(shape):
    return lax.broadcasted_iota(jnp.int32, shape, len(shape) - 1) < HALF


def turned(x):
    return pltpu.roll(x, HALF, x.ndim - 1)


def packed_edges(strip):
    first, second = strip[:BLOCK], strip[BLOCK:]
    low = lane_low(first.shape)
    left_edge = jnp.where(low, first, turned(second))
    right_edge = jnp.where(low, turned(first), second)
    return left_edge, right_edge


def unpacked_sides(from_left, from_right):
    low = lane_low(from_left.shape)
    first = jnp.where(low, from_right, turned(from_left))
    second = jnp.where(low, turned(from_right), from_left)
    return first, second


LEFT, RIGHT, UP, DOWN, UP_CORNER, DOWN_CORNER = range(6)


def kernel(
    pos_ref, obj, probe_in, measured_in, mats_in, out,
    probe, measured, mats, pk, rs, rl, vt, cr, ext, window, psi, far, part, others, mid, pulled, term, parts, grid, gv, middle, hp, gh,
    load, halo_send, halo_recv, cross_send, cross_recv, relay_send, relay_recv, mode_send, mode_recv, term_send, term_recv, grad_send, grad_recv,
):
    mode, ty, tx = lax.axis_index("mode"), lax.axis_index("ty"), lax.axis_index("tx")
    modes, tys, txs = lax.axis_size("mode"), lax.axis_size("ty"), lax.axis_size("tx")
    has = {LEFT: tx > 0, RIGHT: tx < txs - 1, UP: ty > 0, DOWN: ty < tys - 1}
    has[UP_CORNER], has[DOWN_CORNER] = has[UP], has[DOWN]
    cross_right, cross_left = tx == txs // 2 - 1, tx == txs // 2
    mirror = modes - 1 - mode
    left_mode = jnp.where(cross_left, mirror, mode)
    right_mode = jnp.where(cross_right, mirror, mode)
    target = {
        LEFT: {"mode": left_mode, "ty": ty, "tx": tx - 1},
        RIGHT: {"mode": right_mode, "ty": ty, "tx": tx + 1},
        UP: {"mode": mode, "ty": ty - 1, "tx": tx},
        DOWN: {"mode": mode, "ty": ty + 1, "tx": tx},
    }
    crossing = {LEFT: cross_left, RIGHT: cross_right}
    relay_tx = {LEFT: 0, RIGHT: txs - 1}
    relaying = {LEFT: tx == relay_tx[LEFT], RIGHT: tx == relay_tx[RIGHT]}
    landing_tx = {LEFT: txs // 2 - 1, RIGHT: txs // 2}
    direct = {LEFT: {"mode": mode, "ty": ty, "tx": tx - 1}, RIGHT: {"mode": mode, "ty": ty, "tx": tx + 1}}

    def peer(step):
        return {"mode": lax.rem(mode + step, modes), "ty": ty, "tx": tx}

    loads = [pltpu.make_async_copy(src, dst, load.at[i]) for i, (src, dst) in enumerate(((probe_in, probe), (mats_in, mats), (measured_in, measured)))]
    for copy in loads:
        copy.start()

    for side in (LEFT, RIGHT):

        @pl.when(jnp.logical_not(has[side]))
        def _():
            rs[:, side] = jnp.zeros_like(rs[:, side])
            gh[side] = jnp.zeros_like(gh[side])

    for side in (UP, DOWN):

        @pl.when(jnp.logical_not(has[side]))
        def _():
            vt[:, side - UP] = jnp.zeros_like(vt[:, side - UP])
            cr[:, side - UP] = jnp.zeros_like(cr[:, side - UP])
            gv[side - UP] = jnp.zeros_like(gv[side - UP])

    for s in range(SLICES):
        for c in range(2):
            for b in range(2):
                left_edge, right_edge = packed_edges(obj[s, c, b * HALF : (b + 1) * HALF])
                pk[s, LEFT, c, b * BLOCK : (b + 1) * BLOCK] = left_edge
                pk[s, RIGHT, c, b * BLOCK : (b + 1) * BLOCK] = right_edge

    barrier = pltpu.get_barrier_semaphore()
    count = jnp.int32(modes - 1)
    for side in (LEFT, RIGHT, UP, DOWN):
        count = count + has[side].astype(jnp.int32)

        @pl.when(has[side])
        def _():
            pl.semaphore_signal(barrier, inc=1, device_id=target[side], device_id_type=MESH)

    for side, cross in ((LEFT, cross_left), (RIGHT, cross_right)):
        far_pair = jnp.logical_and(cross, has[side])
        count = count + far_pair.astype(jnp.int32)

        @pl.when(far_pair)
        def _():
            pl.semaphore_signal(barrier, inc=1, device_id=direct[side], device_id_type=MESH)

    for side in (LEFT, RIGHT):
        from_relay, from_landing = crossing[side], relaying[side]
        count = count + from_relay.astype(jnp.int32) + from_landing.astype(jnp.int32)

        @pl.when(relaying[side])
        def _():
            sender = {"mode": mirror, "ty": ty, "tx": landing_tx[1 - side]}
            pl.semaphore_signal(barrier, inc=1, device_id=sender, device_id_type=MESH)

        @pl.when(tx == landing_tx[side])
        def _():
            relay = {"mode": mode, "ty": ty, "tx": relay_tx[side]}
            pl.semaphore_signal(barrier, inc=1, device_id=relay, device_id_type=MESH)

    for step in range(1, modes):
        pl.semaphore_signal(barrier, inc=1, device_id=peer(step), device_id_type=MESH)
    pl.semaphore_wait(barrier, count)

    opposite = {LEFT: RIGHT, RIGHT: LEFT, UP: DOWN, DOWN: UP, UP_CORNER: DOWN_CORNER, DOWN_CORNER: UP_CORNER}

    def landing(s, kind):
        if kind in (LEFT, RIGHT):
            return rs.at[s, kind]
        if kind in (UP, DOWN):
            return vt.at[s, kind - UP]
        return cr.at[s, kind - UP_CORNER]

    def source(s, kind):
        if kind in (LEFT, RIGHT):
            return pk.at[s, kind]
        if kind in (UP, DOWN):
            return obj.at[s, :, (kind - UP) * HALF : (kind - UP + 1) * HALF]
        return rs.at[s, :, :, (kind - UP_CORNER) * BLOCK : (kind - UP_CORNER + 1) * BLOCK]

    def halo_copy(s, kind):
        return pltpu.make_async_remote_copy(
            src_ref=source(s, kind),
            dst_ref=landing(s, opposite[kind]),
            send_sem=halo_send.at[s, kind],
            recv_sem=halo_recv.at[s, opposite[kind]],
            device_id=target[kind if kind < UP_CORNER else kind - 2],
            device_id_type=MESH,
        )

    def straight_copy(s, kind):
        return pltpu.make_async_remote_copy(
            src_ref=pk.at[s, kind, 0],
            dst_ref=rs.at[s, opposite[kind], 0],
            send_sem=cross_send.at[s, 0],
            recv_sem=cross_recv.at[s, 0],
            device_id=target[kind],
            device_id_type=MESH,
        )

    def detour_copy(s, kind):
        return pltpu.make_async_remote_copy(
            src_ref=pk.at[s, kind, 1],
            dst_ref=rl.at[s],
            send_sem=cross_send.at[s, 1],
            recv_sem=relay_recv.at[s],
            device_id={"mode": mirror, "ty": ty, "tx": relay_tx[kind]},
            device_id_type=MESH,
        )

    def onward_copy(s, kind):
        return pltpu.make_async_remote_copy(
            src_ref=rl.at[s],
            dst_ref=rs.at[s, opposite[kind], 1],
            send_sem=relay_send.at[s],
            recv_sem=cross_recv.at[s, 1],
            device_id={"mode": mode, "ty": ty, "tx": landing_tx[kind]},
            device_id_type=MESH,
        )

    def near(kind):
        return jnp.logical_and(has[kind], jnp.logical_not(crossing[kind])) if kind in crossing else has[kind]

    def start_halo(s, kind):
        @pl.when(near(kind))
        def _():
            halo_copy(s, kind).start()

        if kind in crossing:

            @pl.when(crossing[kind])
            def _():
                straight_copy(s, kind).start()
                detour_copy(s, kind).start()

    def await_halo(s, kind):
        @pl.when(near(kind))
        def _():
            halo_copy(s, opposite[kind]).wait_recv()

        if kind in crossing:

            @pl.when(crossing[kind])
            def _():
                straight_copy(s, opposite[kind]).wait_recv()
                onward_copy(s, opposite[kind]).wait_recv()

    def relay(s):
        for kind in (LEFT, RIGHT):

            @pl.when(relaying[kind])
            def _():
                detour_copy(s, kind).wait_recv()
                onward_copy(s, kind).start()

    for s in range(SLICES):
        for kind in (LEFT, RIGHT, UP, DOWN):
            start_halo(s, kind)

    def relay_corners(s):
        await_halo(s, LEFT)
        await_halo(s, RIGHT)
        start_halo(s, UP_CORNER)
        start_halo(s, DOWN_CORNER)

    row, col = pos_ref[0], pos_ref[1]
    here, there = (lax.broadcasted_iota(jnp.int32, (DET, 2 * DET), d) for d in range(2))
    pick_rows = jnp.where(there == here + row, 1.0, 0.0).astype(BF16)
    offset = here + (col + 2 * DET - HALF)
    offset = jnp.where(offset >= 2 * DET, offset - 2 * DET, offset)
    pick_cols = jnp.where(there == offset, 1.0, 0.0).astype(BF16)
    here, there = (lax.broadcasted_iota(jnp.int32, (2 * DET, DET), d) for d in range(2))
    put_rows = jnp.where(here == there + row, 1.0, 0.0).astype(BF16)
    offset = there + (col + 2 * DET - HALF)
    offset = jnp.where(offset >= 2 * DET, offset - 2 * DET, offset)
    put_cols = jnp.where(here == offset, 1.0, 0.0).astype(BF16)

    def twice(x, axis):
        return jnp.concatenate([x, x], axis=axis)

    def both(x, axis):
        return jnp.concatenate(halves(x), axis=axis)

    def dot(x, y):
        return jnp.dot(x, y, preferred_element_type=F32)

    def build_window(s):
        for kind in (UP, DOWN, UP_CORNER, DOWN_CORNER):
            await_halo(s, kind)
        for c in range(2):
            for side in range(2):
                at = side * 3 * HALF
                ext[c, at : at + HALF, :DET] = vt[s, side, c]
                first, second = unpacked_sides(cr[s, side, LEFT, c], cr[s, side, RIGHT, c])
                ext[c, at : at + BLOCK, DET:] = first
                ext[c, at + BLOCK : at + HALF, DET:] = second
            ext[c, HALF : 3 * HALF, :DET] = obj[s, c]
            for b in range(2):
                block = slice(b * BLOCK, (b + 1) * BLOCK)
                first, second = unpacked_sides(rs[s, LEFT, c, block], rs[s, RIGHT, c, block])
                at = HALF + b * HALF
                ext[c, at : at + BLOCK, DET:] = first
                ext[c, at + BLOCK : at + HALF, DET:] = second
            band = dot(twice(pick_rows, 1), both(ext[c], 0))
            window[s, c] = dot(both(band, 1), twice(put_cols, 0))

    relay_corners(0)
    relay(0)
    for s in range(SLICES):
        if s + 1 < SLICES:
            relay_corners(s + 1)
        for ahead in range(2 * s, min(2 * s + 2, SLICES)):
            if ahead:
                relay(ahead)
        build_window(s)
        if s == 0:
            for copy in loads:
                copy.wait()

        def fetch(m):
            if s == 0:
                real, imag = probe[m, 0], probe[m, 1]
            else:
                real, imag = psi[s - 1, 0, rows(m)], psi[s - 1, 1, rows(m)]
            wr, wi = window[s, 0], window[s, 1]
            return real * wr - imag * wi, real * wi + imag * wr

        def deliver(m, real, imag):
            if s + 1 < SLICES:
                psi[s, 0, rows(m)] = real
                psi[s, 1, rows(m)] = imag
            else:
                far[0, rows(m)] = real
                far[1, rows(m)] = imag
                power = real * real + imag * imag
                part[...] = power if m == 0 else part[...] + power

        two_sided(mats, STEP if s + 1 < SLICES else FAR, fetch, deliver, mid)

    def mode_copy(step):
        return pltpu.make_async_remote_copy(
            src_ref=part,
            dst_ref=others.at[step - 1],
            send_sem=mode_send.at[step - 1],
            recv_sem=mode_recv.at[step - 1],
            device_id=peer(step),
            device_id_type=MESH,
        )

    for step in range(1, modes):
        mode_copy(step).start()
    whole = part[...]
    for step in range(1, modes):
        mode_copy(step).wait_recv()
        whole = whole + others[step - 1]
    weight = 1.0 - measured[0, 0, 0] / jnp.maximum(jnp.sqrt(whole), 1.0)

    def term_copy(s):
        slot = lax.rem(s - mode + modes, modes) - 1
        return pltpu.make_async_remote_copy(
            src_ref=term.at[s],
            dst_ref=parts.at[slot],
            send_sem=term_send.at[s],
            recv_sem=term_recv.at[slot],
            device_id={"mode": s, "ty": ty, "tx": tx},
            device_id_type=MESH,
        )

    for s in reversed(range(SLICES)):

        def fetch(m):
            if s == SLICES - 1:
                return weight * far[0, rows(m)], weight * far[1, rows(m)]
            return pulled[0, rows(m)], pulled[1, rows(m)]

        def deliver(m, real, imag):
            if s == 0:
                pr, pi = probe[m, 0], probe[m, 1]
            else:
                pr, pi = psi[s - 1, 0, rows(m)], psi[s - 1, 1, rows(m)]
            tr, ti = pr * real + pi * imag, pr * imag - pi * real
            term[s, 0] = tr if m == 0 else term[s, 0] + tr
            term[s, 1] = ti if m == 0 else term[s, 1] + ti
            if s > 0:
                wr, wi = window[s, 0], window[s, 1]
                pulled[0, rows(m)] = wr * real + wi * imag
                pulled[1, rows(m)] = wr * imag - wi * real

        two_sided(mats, FAR_BACK if s == SLICES - 1 else STEP_BACK, fetch, deliver, mid)

        @pl.when(mode != s)
        def _():
            term_copy(s).start()

    for step in range(1, modes):
        pltpu.make_async_remote_copy(
            src_ref=term.at[0],
            dst_ref=parts.at[step - 1],
            send_sem=term_send.at[0],
            recv_sem=term_recv.at[step - 1],
            device_id=peer(step),
            device_id_type=MESH,
        ).wait_recv()

    for c in range(2):
        mine = term[mode, c]
        for step in range(1, modes):
            mine = mine + parts[step - 1, c]
        tall = dot(twice(put_rows, 1), both(mine, 0))
        grid[c] = dot(both(tall, 1), twice(pick_cols, 0))

    def grad_copy(kind):
        if kind in (UP, DOWN):
            at = (kind - UP) * 3 * HALF
            src, dst = grid.at[:, at : at + HALF], gv.at[opposite[kind] - UP]
            where = target[kind]
        else:
            src, dst = hp.at[kind], gh.at[opposite[kind]]
            where = direct[kind]
        return pltpu.make_async_remote_copy(
            src_ref=src,
            dst_ref=dst,
            send_sem=grad_send.at[kind],
            recv_sem=grad_recv.at[opposite[kind]],
            device_id=where,
            device_id_type=MESH,
        )

    def exchange(kinds):
        for kind in kinds:

            @pl.when(has[kind])
            def _():
                grad_copy(kind).start()

        for kind in kinds:

            @pl.when(has[kind])
            def _():
                grad_copy(opposite[kind]).wait_recv()

    exchange((UP, DOWN))
    for c in range(2):
        for b in range(2):
            block = slice(b * HALF, (b + 1) * HALF)
            middle[c, block] = grid[c, HALF + b * HALF : 2 * HALF + b * HALF] + gv[b, c]
        upper, lower = middle[c, :HALF, DET:], middle[c, HALF:, DET:]
        low = lane_low(upper.shape)
        hp[RIGHT, c] = jnp.where(low, upper, turned(lower))
        hp[LEFT, c] = jnp.where(low, turned(upper), lower)
    exchange((LEFT, RIGHT))
    for c in range(2):
        low = lane_low(gh[LEFT, c].shape)
        out[0, c, :HALF] = middle[c, :HALF, :DET] + jnp.where(low, gh[LEFT, c], turned(gh[RIGHT, c]))
        out[0, c, HALF:] = middle[c, HALF:, :DET] + jnp.where(low, turned(gh[LEFT, c]), gh[RIGHT, c])

    for kind in range(6):

        @pl.when(near(kind))
        def _():
            for s in range(SLICES):
                halo_copy(s, kind).wait_send()

        if kind < UP_CORNER:

            @pl.when(has[kind])
            def _():
                grad_copy(kind).wait_send()

    for kind in (LEFT, RIGHT):

        @pl.when(crossing[kind])
        def _():
            for s in range(SLICES):
                straight_copy(s, kind).wait_send()
                detour_copy(s, kind).wait_send()

        @pl.when(relaying[kind])
        def _():
            for s in range(SLICES):
                onward_copy(s, kind).wait_send()

    for step in range(1, modes):
        mode_copy(step).wait_send()
    for s in range(SLICES):

        @pl.when(mode != s)
        def _():
            term_copy(s).wait_send()


VMEM = pl.BlockSpec(memory_space=pltpu.VMEM)
SMEM = pl.BlockSpec(memory_space=pltpu.SMEM)
ANY = pl.BlockSpec(memory_space=pl.ANY)


def body(object_slices, probe_modes, positions, measured):
    mats = jnp.asarray(tables())
    modes = lax.axis_size("mode")
    dma = pltpu.SemaphoreType.DMA
    wave = (LOCAL * DET, DET)
    scratch = dict(
        probe=(LOCAL, 2, DET, DET),
        measured=(1, 1, 1, DET, DET),
        mats=(8, 2 * DET, 2 * DET),
        pk=(SLICES, 2, 2, HALF, DET),
        rs=(SLICES, 2, 2, HALF, DET),
        rl=(SLICES, HALF, DET),
        vt=(SLICES, 2, 2, HALF, DET),
        cr=(SLICES, 2, 2, 2, BLOCK, DET),
        ext=(2, 2 * DET, 2 * DET),
        window=(SLICES, 2, DET, DET),
        psi=(SLICES - 1, 2, *wave),
        far=(2, *wave),
        part=(DET, DET),
        others=(modes - 1, DET, DET),
        mid=(4 * DET, LOCAL * DET),
        pulled=(2, *wave),
        term=(SLICES, 2, DET, DET),
        parts=(modes - 1, 2, DET, DET),
        grid=(2, 2 * DET, 2 * DET),
        gv=(2, 2, HALF, 2 * DET),
        middle=(2, DET, 2 * DET),
        hp=(2, 2, HALF, DET),
        gh=(2, 2, HALF, DET),
    )
    return pl.pallas_call(
        kernel,
        out_shape=jax.ShapeDtypeStruct((1, 2, DET, DET), F32),
        in_specs=[SMEM, VMEM, ANY, ANY, ANY],
        out_specs=VMEM,
        scratch_shapes=[pltpu.VMEM(shape, BF16 if name in ("mid", "mats") else F32) for name, shape in scratch.items()]
        + [dma((3,))]
        + [dma((SLICES, 6)), dma((SLICES, 6))]
        + [dma((SLICES, 2)), dma((SLICES, 2)), dma((SLICES,)), dma((SLICES,))]
        + [dma((modes - 1,)), dma((modes - 1,))]
        + [dma((SLICES,)), dma((modes - 1,))]
        + [dma((4,)), dma((4,))],
        compiler_params=pltpu.CompilerParams(collective_id=0, has_side_effects=True),
        name="ptycho",
    )(positions.reshape(2), object_slices, probe_modes, measured, mats)


def solution(mesh):
    return jax.shard_map(
        body,
        mesh=mesh,
        in_specs=(
            P(None, None, "ty", "tx"),
            P("mode", None, None, None),
            P("ty", "tx", None, None),
            P("ty", "tx", None, None, None),
        ),
        out_specs=P("mode", None, "ty", "tx"),
        check_vma=False,
    )
```

```python
import functools

import numpy as np
import jax
import jax.numpy as jnp
from jax import lax
from jax.experimental import pallas as pl
from jax.experimental.pallas import tpu as pltpu
from jax.sharding import PartitionSpec as P

DET = 128
SLICES = 4
MARGIN = 64
LOCAL = 4
RATE = 0.3
F32 = jnp.float32
BF16 = jnp.bfloat16


def real_block(matrix):
    return np.block([[matrix.real, matrix.imag], [-matrix.imag, matrix.real]])


def tables():
    counter = np.arange(DET)
    fourier = np.exp(-2j * np.pi * (np.outer(counter, counter) % DET) / DET) / np.sqrt(DET)
    frequency = np.where(counter < DET // 2, counter, counter - DET).astype(np.float64)
    chirp = np.exp(-1j * RATE * frequency**2 / DET)
    step = fourier.conj() @ (chirp[:, None] * fourier)
    step = (step + step.T) / 2
    out = []
    for matrix in (step, step.conj(), fourier, fourier.conj()):
        block = real_block(matrix).astype(np.float32)
        high = block.astype(jnp.bfloat16)
        low = (block - high.astype(np.float32)).astype(jnp.bfloat16)
        out += [high, low]
    return np.stack(out)


STEP, STEP_BACK, FAR, FAR_BACK = range(4)
CONJ = {STEP: STEP_BACK, STEP_BACK: STEP, FAR: FAR_BACK, FAR_BACK: FAR}


def halves(x):
    high = x.astype(BF16)
    return high, (x - high.astype(F32)).astype(BF16)


def rows(m):
    return slice(m * DET, (m + 1) * DET)


def right_product(mats, which, real, imag):
    rh, rl = halves(real)
    ih, il = halves(imag)
    lhs = jnp.concatenate([rh, ih, rl, il, rh, ih], axis=1)
    high, low = mats[2 * which], mats[2 * which + 1]
    rhs = jnp.concatenate([high, high, low], axis=0)
    return jnp.dot(lhs, rhs, preferred_element_type=F32)


def left_product(mats, which, stacked):
    conj = CONJ[which]
    high, low = mats[2 * conj], mats[2 * conj + 1]
    main = jnp.dot(jnp.concatenate([high, low], axis=0), stacked[: 2 * DET], preferred_element_type=F32)
    rest = jnp.dot(high, stacked[2 * DET :], preferred_element_type=F32)
    return main[: 2 * DET] + main[2 * DET :] + rest


def two_sided(mats, which, fetch, deliver, mid):
    for m in range(LOCAL):
        real, imag = fetch(m)
        out = right_product(mats, which, real, imag)
        rh, rl = halves(out[:, :DET])
        ih, il = halves(out[:, DET:])
        for part, value in enumerate((rh, ih, rl, il)):
            mid[rows(part), rows(m)] = value
    for pair in range(LOCAL // 2):
        out = left_product(mats, which, mid[:, pair * 2 * DET : (pair + 1) * 2 * DET])
        for k in range(2):
            deliver(2 * pair + k, out[:DET, rows(k)], out[DET:, rows(k)])

MESH = pl.DeviceIdType.MESH
HALF = DET // 2
BLOCK = HALF // 2


def lane_low(shape):
    return lax.broadcasted_iota(jnp.int32, shape, len(shape) - 1) < HALF


def turned(x):
    return pltpu.roll(x, HALF, x.ndim - 1)


def packed_edges(strip):
    first, second = strip[:BLOCK], strip[BLOCK:]
    low = lane_low(first.shape)
    left_edge = jnp.where(low, first, turned(second))
    right_edge = jnp.where(low, turned(first), second)
    return left_edge, right_edge


def unpacked_sides(from_left, from_right):
    low = lane_low(from_left.shape)
    first = jnp.where(low, from_right, turned(from_left))
    second = jnp.where(low, turned(from_right), from_left)
    return first, second


LEFT, RIGHT, UP, DOWN, UP_CORNER, DOWN_CORNER = range(6)


def kernel(
    pos_ref, obj, probe_in, measured_in, mats_in, out,
    probe, measured, mats, pk, rs, rl, vt, cr, ext, window, psi, far, part, others, mid, pulled, term, parts, grid, gv, middle, hp, gh,
    load, halo_send, halo_recv, cross_send, cross_recv, relay_send, relay_recv, mode_send, mode_recv, term_send, term_recv, grad_send, grad_recv,
):
    mode, ty, tx = lax.axis_index("mode"), lax.axis_index("ty"), lax.axis_index("tx")
    modes, tys, txs = lax.axis_size("mode"), lax.axis_size("ty"), lax.axis_size("tx")
    has = {LEFT: tx > 0, RIGHT: tx < txs - 1, UP: ty > 0, DOWN: ty < tys - 1}
    has[UP_CORNER], has[DOWN_CORNER] = has[UP], has[DOWN]
    cross_right, cross_left = tx == txs // 2 - 1, tx == txs // 2
    mirror = modes - 1 - mode
    left_mode = jnp.where(cross_left, mirror, mode)
    right_mode = jnp.where(cross_right, mirror, mode)
    target = {
        LEFT: {"mode": left_mode, "ty": ty, "tx": tx - 1},
        RIGHT: {"mode": right_mode, "ty": ty, "tx": tx + 1},
        UP: {"mode": mode, "ty": ty - 1, "tx": tx},
        DOWN: {"mode": mode, "ty": ty + 1, "tx": tx},
    }
    crossing = {LEFT: cross_left, RIGHT: cross_right}
    relay_tx = {LEFT: txs - 1, RIGHT: 0}
    relaying = {LEFT: tx == relay_tx[LEFT], RIGHT: tx == relay_tx[RIGHT]}
    landing_tx = {LEFT: txs // 2 - 1, RIGHT: txs // 2}
    direct = {LEFT: {"mode": mode, "ty": ty, "tx": tx - 1}, RIGHT: {"mode": mode, "ty": ty, "tx": tx + 1}}

    def peer(step):
        return {"mode": lax.rem(mode + step, modes), "ty": ty, "tx": tx}

    loads = [pltpu.make_async_copy(src, dst, load.at[i]) for i, (src, dst) in enumerate(((probe_in, probe), (mats_in, mats), (measured_in, measured)))]
    for copy in loads:
        copy.start()

    for side in (LEFT, RIGHT):

        @pl.when(jnp.logical_not(has[side]))
        def _():
            rs[:, side] = jnp.zeros_like(rs[:, side])
            gh[side] = jnp.zeros_like(gh[side])

    for side in (UP, DOWN):

        @pl.when(jnp.logical_not(has[side]))
        def _():
            vt[:, side - UP] = jnp.zeros_like(vt[:, side - UP])
            cr[:, side - UP] = jnp.zeros_like(cr[:, side - UP])
            gv[side - UP] = jnp.zeros_like(gv[side - UP])

    for s in range(SLICES):
        for c in range(2):
            for b in range(2):
                left_edge, right_edge = packed_edges(obj[s, c, b * HALF : (b + 1) * HALF])
                pk[s, LEFT, c, b * BLOCK : (b + 1) * BLOCK] = left_edge
                pk[s, RIGHT, c, b * BLOCK : (b + 1) * BLOCK] = right_edge

    barrier = pltpu.get_barrier_semaphore()
    count = jnp.int32(modes - 1)
    for side in (LEFT, RIGHT, UP, DOWN):
        count = count + has[side].astype(jnp.int32)

        @pl.when(has[side])
        def _():
            pl.semaphore_signal(barrier, inc=1, device_id=target[side], device_id_type=MESH)

    for side, cross in ((LEFT, cross_left), (RIGHT, cross_right)):
        far_pair = jnp.logical_and(cross, has[side])
        count = count + far_pair.astype(jnp.int32)

        @pl.when(far_pair)
        def _():
            pl.semaphore_signal(barrier, inc=1, device_id=direct[side], device_id_type=MESH)

    for side in (LEFT, RIGHT):
        from_relay, from_landing = crossing[side], relaying[side]
        count = count + from_relay.astype(jnp.int32) + from_landing.astype(jnp.int32)

        @pl.when(relaying[side])
        def _():
            sender = {"mode": mode, "ty": ty, "tx": landing_tx[1 - side]}
            pl.semaphore_signal(barrier, inc=1, device_id=sender, device_id_type=MESH)

        @pl.when(tx == landing_tx[side])
        def _():
            relay = {"mode": mirror, "ty": ty, "tx": relay_tx[side]}
            pl.semaphore_signal(barrier, inc=1, device_id=relay, device_id_type=MESH)

    for step in range(1, modes):
        pl.semaphore_signal(barrier, inc=1, device_id=peer(step), device_id_type=MESH)
    pl.semaphore_wait(barrier, count)

    opposite = {LEFT: RIGHT, RIGHT: LEFT, UP: DOWN, DOWN: UP, UP_CORNER: DOWN_CORNER, DOWN_CORNER: UP_CORNER}

    def landing(s, kind):
        if kind in (LEFT, RIGHT):
            return rs.at[s, kind]
        if kind in (UP, DOWN):
            return vt.at[s, kind - UP]
        return cr.at[s, kind - UP_CORNER]

    def source(s, kind):
        if kind in (LEFT, RIGHT):
            return pk.at[s, kind]
        if kind in (UP, DOWN):
            return obj.at[s, :, (kind - UP) * HALF : (kind - UP + 1) * HALF]
        return rs.at[s, :, :, (kind - UP_CORNER) * BLOCK : (kind - UP_CORNER + 1) * BLOCK]

    def halo_copy(s, kind):
        return pltpu.make_async_remote_copy(
            src_ref=source(s, kind),
            dst_ref=landing(s, opposite[kind]),
            send_sem=halo_send.at[s, kind],
            recv_sem=halo_recv.at[s, opposite[kind]],
            device_id=target[kind if kind < UP_CORNER else kind - 2],
            device_id_type=MESH,
        )

    def straight_copy(s, kind):
        return pltpu.make_async_remote_copy(
            src_ref=pk.at[s, kind, 0],
            dst_ref=rs.at[s, opposite[kind], 0],
            send_sem=cross_send.at[s, 0],
            recv_sem=cross_recv.at[s, 0],
            device_id=target[kind],
            device_id_type=MESH,
        )

    def detour_copy(s, kind):
        return pltpu.make_async_remote_copy(
            src_ref=pk.at[s, kind, 1],
            dst_ref=rl.at[s],
            send_sem=cross_send.at[s, 1],
            recv_sem=relay_recv.at[s],
            device_id={"mode": mode, "ty": ty, "tx": relay_tx[kind]},
            device_id_type=MESH,
        )

    def onward_copy(s, kind):
        return pltpu.make_async_remote_copy(
            src_ref=rl.at[s],
            dst_ref=rs.at[s, opposite[kind], 1],
            send_sem=relay_send.at[s],
            recv_sem=cross_recv.at[s, 1],
            device_id={"mode": mirror, "ty": ty, "tx": landing_tx[kind]},
            device_id_type=MESH,
        )

    def near(kind):
        return jnp.logical_and(has[kind], jnp.logical_not(crossing[kind])) if kind in crossing else has[kind]

    def start_halo(s, kind):
        @pl.when(near(kind))
        def _():
            halo_copy(s, kind).start()

        if kind in crossing:

            @pl.when(crossing[kind])
            def _():
                straight_copy(s, kind).start()
                detour_copy(s, kind).start()

    def await_halo(s, kind):
        @pl.when(near(kind))
        def _():
            halo_copy(s, opposite[kind]).wait_recv()

        if kind in crossing:

            @pl.when(crossing[kind])
            def _():
                straight_copy(s, opposite[kind]).wait_recv()
                onward_copy(s, opposite[kind]).wait_recv()

    def relay(s):
        for kind in (LEFT, RIGHT):

            @pl.when(relaying[kind])
            def _():
                detour_copy(s, kind).wait_recv()
                onward_copy(s, kind).start()

    for s in range(SLICES):
        for kind in (LEFT, RIGHT, UP, DOWN):
            start_halo(s, kind)

    def relay_corners(s):
        await_halo(s, LEFT)
        await_halo(s, RIGHT)
        start_halo(s, UP_CORNER)
        start_halo(s, DOWN_CORNER)

    row, col = pos_ref[0], pos_ref[1]
    here, there = (lax.broadcasted_iota(jnp.int32, (DET, 2 * DET), d) for d in range(2))
    pick_rows = jnp.where(there == here + row, 1.0, 0.0).astype(BF16)
    offset = here + (col + 2 * DET - HALF)
    offset = jnp.where(offset >= 2 * DET, offset - 2 * DET, offset)
    pick_cols = jnp.where(there == offset, 1.0, 0.0).astype(BF16)
    here, there = (lax.broadcasted_iota(jnp.int32, (2 * DET, DET), d) for d in range(2))
    put_rows = jnp.where(here == there + row, 1.0, 0.0).astype(BF16)
    offset = there + (col + 2 * DET - HALF)
    offset = jnp.where(offset >= 2 * DET, offset - 2 * DET, offset)
    put_cols = jnp.where(here == offset, 1.0, 0.0).astype(BF16)

    def twice(x, axis):
        return jnp.concatenate([x, x], axis=axis)

    def both(x, axis):
        return jnp.concatenate(halves(x), axis=axis)

    def dot(x, y):
        return jnp.dot(x, y, preferred_element_type=F32)

    def build_window(s):
        for kind in (UP, DOWN, UP_CORNER, DOWN_CORNER):
            await_halo(s, kind)
        for c in range(2):
            for side in range(2):
                at = side * 3 * HALF
                ext[c, at : at + HALF, :DET] = vt[s, side, c]
                first, second = unpacked_sides(cr[s, side, LEFT, c], cr[s, side, RIGHT, c])
                ext[c, at : at + BLOCK, DET:] = first
                ext[c, at + BLOCK : at + HALF, DET:] = second
            ext[c, HALF : 3 * HALF, :DET] = obj[s, c]
            for b in range(2):
                block = slice(b * BLOCK, (b + 1) * BLOCK)
                first, second = unpacked_sides(rs[s, LEFT, c, block], rs[s, RIGHT, c, block])
                at = HALF + b * HALF
                ext[c, at : at + BLOCK, DET:] = first
                ext[c, at + BLOCK : at + HALF, DET:] = second
            band = dot(twice(pick_rows, 1), both(ext[c], 0))
            window[s, c] = dot(both(band, 1), twice(put_cols, 0))

    relay_corners(0)
    relay(0)
    for s in range(SLICES):
        if s + 1 < SLICES:
            relay_corners(s + 1)
        for ahead in range(2 * s, min(2 * s + 2, SLICES)):
            if ahead:
                relay(ahead)
        build_window(s)
        if s == 0:
            for copy in loads:
                copy.wait()

        def fetch(m):
            if s == 0:
                real, imag = probe[m, 0], probe[m, 1]
            else:
                real, imag = psi[s - 1, 0, rows(m)], psi[s - 1, 1, rows(m)]
            wr, wi = window[s, 0], window[s, 1]
            return real * wr - imag * wi, real * wi + imag * wr

        def deliver(m, real, imag):
            if s + 1 < SLICES:
                psi[s, 0, rows(m)] = real
                psi[s, 1, rows(m)] = imag
            else:
                far[0, rows(m)] = real
                far[1, rows(m)] = imag
                power = real * real + imag * imag
                part[...] = power if m == 0 else part[...] + power

        two_sided(mats, STEP if s + 1 < SLICES else FAR, fetch, deliver, mid)

    def mode_copy(step):
        return pltpu.make_async_remote_copy(
            src_ref=part,
            dst_ref=others.at[step - 1],
            send_sem=mode_send.at[step - 1],
            recv_sem=mode_recv.at[step - 1],
            device_id=peer(step),
            device_id_type=MESH,
        )

    for step in range(1, modes):
        mode_copy(step).start()
    whole = part[...]
    for step in range(1, modes):
        mode_copy(step).wait_recv()
        whole = whole + others[step - 1]
    weight = 1.0 - measured[0, 0, 0] / jnp.maximum(jnp.sqrt(whole), 1.0)

    def term_copy(s):
        slot = lax.rem(s - mode + modes, modes) - 1
        return pltpu.make_async_remote_copy(
            src_ref=term.at[s],
            dst_ref=parts.at[slot],
            send_sem=term_send.at[s],
            recv_sem=term_recv.at[slot],
            device_id={"mode": s, "ty": ty, "tx": tx},
            device_id_type=MESH,
        )

    for s in reversed(range(SLICES)):

        def fetch(m):
            if s == SLICES - 1:
                return weight * far[0, rows(m)], weight * far[1, rows(m)]
            return pulled[0, rows(m)], pulled[1, rows(m)]

        def deliver(m, real, imag):
            if s == 0:
                pr, pi = probe[m, 0], probe[m, 1]
            else:
                pr, pi = psi[s - 1, 0, rows(m)], psi[s - 1, 1, rows(m)]
            tr, ti = pr * real + pi * imag, pr * imag - pi * real
            term[s, 0] = tr if m == 0 else term[s, 0] + tr
            term[s, 1] = ti if m == 0 else term[s, 1] + ti
            if s > 0:
                wr, wi = window[s, 0], window[s, 1]
                pulled[0, rows(m)] = wr * real + wi * imag
                pulled[1, rows(m)] = wr * imag - wi * real

        two_sided(mats, FAR_BACK if s == SLICES - 1 else STEP_BACK, fetch, deliver, mid)

        @pl.when(mode != s)
        def _():
            term_copy(s).start()

    for step in range(1, modes):
        pltpu.make_async_remote_copy(
            src_ref=term.at[0],
            dst_ref=parts.at[step - 1],
            send_sem=term_send.at[0],
            recv_sem=term_recv.at[step - 1],
            device_id=peer(step),
            device_id_type=MESH,
        ).wait_recv()

    for c in range(2):
        mine = term[mode, c]
        for step in range(1, modes):
            mine = mine + parts[step - 1, c]
        tall = dot(twice(put_rows, 1), both(mine, 0))
        grid[c] = dot(both(tall, 1), twice(pick_cols, 0))

    def grad_copy(kind):
        if kind in (UP, DOWN):
            at = (kind - UP) * 3 * HALF
            src, dst = grid.at[:, at : at + HALF], gv.at[opposite[kind] - UP]
            where = target[kind]
        else:
            src, dst = hp.at[kind], gh.at[opposite[kind]]
            where = direct[kind]
        return pltpu.make_async_remote_copy(
            src_ref=src,
            dst_ref=dst,
            send_sem=grad_send.at[kind],
            recv_sem=grad_recv.at[opposite[kind]],
            device_id=where,
            device_id_type=MESH,
        )

    def exchange(kinds):
        for kind in kinds:

            @pl.when(has[kind])
            def _():
                grad_copy(kind).start()

        for kind in kinds:

            @pl.when(has[kind])
            def _():
                grad_copy(opposite[kind]).wait_recv()

    exchange((UP, DOWN))
    for c in range(2):
        for b in range(2):
            block = slice(b * HALF, (b + 1) * HALF)
            middle[c, block] = grid[c, HALF + b * HALF : 2 * HALF + b * HALF] + gv[b, c]
        upper, lower = middle[c, :HALF, DET:], middle[c, HALF:, DET:]
        low = lane_low(upper.shape)
        hp[RIGHT, c] = jnp.where(low, upper, turned(lower))
        hp[LEFT, c] = jnp.where(low, turned(upper), lower)
    exchange((LEFT, RIGHT))
    for c in range(2):
        low = lane_low(gh[LEFT, c].shape)
        out[0, c, :HALF] = middle[c, :HALF, :DET] + jnp.where(low, gh[LEFT, c], turned(gh[RIGHT, c]))
        out[0, c, HALF:] = middle[c, HALF:, :DET] + jnp.where(low, turned(gh[LEFT, c]), gh[RIGHT, c])

    for kind in range(6):

        @pl.when(near(kind))
        def _():
            for s in range(SLICES):
                halo_copy(s, kind).wait_send()

        if kind < UP_CORNER:

            @pl.when(has[kind])
            def _():
                grad_copy(kind).wait_send()

    for kind in (LEFT, RIGHT):

        @pl.when(crossing[kind])
        def _():
            for s in range(SLICES):
                straight_copy(s, kind).wait_send()
                detour_copy(s, kind).wait_send()

        @pl.when(relaying[kind])
        def _():
            for s in range(SLICES):
                onward_copy(s, kind).wait_send()

    for step in range(1, modes):
        mode_copy(step).wait_send()
    for s in range(SLICES):

        @pl.when(mode != s)
        def _():
            term_copy(s).wait_send()


VMEM = pl.BlockSpec(memory_space=pltpu.VMEM)
SMEM = pl.BlockSpec(memory_space=pltpu.SMEM)
ANY = pl.BlockSpec(memory_space=pl.ANY)


def body(object_slices, probe_modes, positions, measured):
    mats = jnp.asarray(tables())
    modes = lax.axis_size("mode")
    dma = pltpu.SemaphoreType.DMA
    wave = (LOCAL * DET, DET)
    scratch = dict(
        probe=(LOCAL, 2, DET, DET),
        measured=(1, 1, 1, DET, DET),
        mats=(8, 2 * DET, 2 * DET),
        pk=(SLICES, 2, 2, HALF, DET),
        rs=(SLICES, 2, 2, HALF, DET),
        rl=(SLICES, HALF, DET),
        vt=(SLICES, 2, 2, HALF, DET),
        cr=(SLICES, 2, 2, 2, BLOCK, DET),
        ext=(2, 2 * DET, 2 * DET),
        window=(SLICES, 2, DET, DET),
        psi=(SLICES - 1, 2, *wave),
        far=(2, *wave),
        part=(DET, DET),
        others=(modes - 1, DET, DET),
        mid=(4 * DET, LOCAL * DET),
        pulled=(2, *wave),
        term=(SLICES, 2, DET, DET),
        parts=(modes - 1, 2, DET, DET),
        grid=(2, 2 * DET, 2 * DET),
        gv=(2, 2, HALF, 2 * DET),
        middle=(2, DET, 2 * DET),
        hp=(2, 2, HALF, DET),
        gh=(2, 2, HALF, DET),
    )
    return pl.pallas_call(
        kernel,
        out_shape=jax.ShapeDtypeStruct((1, 2, DET, DET), F32),
        in_specs=[SMEM, VMEM, ANY, ANY, ANY],
        out_specs=VMEM,
        scratch_shapes=[pltpu.VMEM(shape, BF16 if name in ("mid", "mats") else F32) for name, shape in scratch.items()]
        + [dma((3,))]
        + [dma((SLICES, 6)), dma((SLICES, 6))]
        + [dma((SLICES, 2)), dma((SLICES, 2)), dma((SLICES,)), dma((SLICES,))]
        + [dma((modes - 1,)), dma((modes - 1,))]
        + [dma((SLICES,)), dma((modes - 1,))]
        + [dma((4,)), dma((4,))],
        compiler_params=pltpu.CompilerParams(collective_id=0, has_side_effects=True),
        name="ptycho",
    )(positions.reshape(2), object_slices, probe_modes, measured, mats)


def solution(mesh):
    return jax.shard_map(
        body,
        mesh=mesh,
        in_specs=(
            P(None, None, "ty", "tx"),
            P("mode", None, None, None),
            P("ty", "tx", None, None),
            P("ty", "tx", None, None, None),
        ),
        out_specs=P("mode", None, "ty", "tx"),
        check_vma=False,
    )
```

```python
import functools

import numpy as np
import jax
import jax.numpy as jnp
from jax import lax
from jax.experimental import pallas as pl
from jax.experimental.pallas import tpu as pltpu
from jax.sharding import PartitionSpec as P

DET = 128
SLICES = 4
MARGIN = 64
LOCAL = 4
RATE = 0.3
F32 = jnp.float32
BF16 = jnp.bfloat16


def real_block(matrix):
    return np.block([[matrix.real, matrix.imag], [-matrix.imag, matrix.real]])


def tables():
    counter = np.arange(DET)
    fourier = np.exp(-2j * np.pi * (np.outer(counter, counter) % DET) / DET) / np.sqrt(DET)
    frequency = np.where(counter < DET // 2, counter, counter - DET).astype(np.float64)
    chirp = np.exp(-1j * RATE * frequency**2 / DET)
    step = fourier.conj() @ (chirp[:, None] * fourier)
    step = (step + step.T) / 2
    out = []
    for matrix in (step, step.conj(), fourier, fourier.conj()):
        block = real_block(matrix).astype(np.float32)
        high = block.astype(jnp.bfloat16)
        low = (block - high.astype(np.float32)).astype(jnp.bfloat16)
        out += [high, low]
    return np.stack(out)


STEP, STEP_BACK, FAR, FAR_BACK = range(4)
CONJ = {STEP: STEP_BACK, STEP_BACK: STEP, FAR: FAR_BACK, FAR_BACK: FAR}


def halves(x):
    high = x.astype(BF16)
    return high, (x - high.astype(F32)).astype(BF16)


def rows(m):
    return slice(m * DET, (m + 1) * DET)


def right_product(mats, which, real, imag):
    rh, rl = halves(real)
    ih, il = halves(imag)
    lhs = jnp.concatenate([rh, ih, rl, il, rh, ih], axis=1)
    high, low = mats[2 * which], mats[2 * which + 1]
    rhs = jnp.concatenate([high, high, low], axis=0)
    return jnp.dot(lhs, rhs, preferred_element_type=F32)


def left_product(mats, which, stacked):
    conj = CONJ[which]
    high, low = mats[2 * conj], mats[2 * conj + 1]
    main = jnp.dot(jnp.concatenate([high, low], axis=0), stacked[: 2 * DET], preferred_element_type=F32)
    rest = jnp.dot(high, stacked[2 * DET :], preferred_element_type=F32)
    return main[: 2 * DET] + main[2 * DET :] + rest


def two_sided(mats, which, fetch, deliver, mid):
    for m in range(LOCAL):
        real, imag = fetch(m)
        out = right_product(mats, which, real, imag)
        rh, rl = halves(out[:, :DET])
        ih, il = halves(out[:, DET:])
        for part, value in enumerate((rh, ih, rl, il)):
            mid[rows(part), rows(m)] = value
    for pair in range(LOCAL // 2):
        out = left_product(mats, which, mid[:, pair * 2 * DET : (pair + 1) * 2 * DET])
        for k in range(2):
            deliver(2 * pair + k, out[:DET, rows(k)], out[DET:, rows(k)])

MESH = pl.DeviceIdType.MESH
HALF = DET // 2
BLOCK = HALF // 2


def lane_low(shape):
    return lax.broadcasted_iota(jnp.int32, shape, len(shape) - 1) < HALF


def turned(x):
    return pltpu.roll(x, HALF, x.ndim - 1)


def packed_edges(strip):
    first, second = strip[:BLOCK], strip[BLOCK:]
    low = lane_low(first.shape)
    left_edge = jnp.where(low, first, turned(second))
    right_edge = jnp.where(low, turned(first), second)
    return left_edge, right_edge


def unpacked_sides(from_left, from_right):
    low = lane_low(from_left.shape)
    first = jnp.where(low, from_right, turned(from_left))
    second = jnp.where(low, turned(from_right), from_left)
    return first, second


def packed_sides(strip):
    half = strip.shape[0] // 2
    upper, lower = strip[:half], strip[half:]
    low = lane_low(upper.shape)
    return jnp.where(low, turned(upper), lower), jnp.where(low, upper, turned(lower))


def unpacked_halves(from_left, from_right):
    low = lane_low(from_left.shape)
    return jnp.where(low, from_left, turned(from_right)), jnp.where(low, turned(from_left), from_right)


LEFT, RIGHT, UP, DOWN, UP_CORNER, DOWN_CORNER = range(6)


def kernel(
    pos_ref, obj, probe_in, measured_in, mats_in, out,
    probe, measured, mats, pk, rs, rl, vt, cr, ext, window, psi, far, part, others, mid, pulled, term, collected, joint, parts, middle, vp, hp, cp, gv, gh, gc,
    load, halo_send, halo_recv, cross_send, cross_recv, relay_send, relay_recv, mode_send, mode_recv, collect_send, collect_recv, joint_send, joint_recv, partner_send, partner_recv, grad_send, grad_recv,
):
    mode, ty, tx = lax.axis_index("mode"), lax.axis_index("ty"), lax.axis_index("tx")
    modes, tys, txs = lax.axis_size("mode"), lax.axis_size("ty"), lax.axis_size("tx")
    has = {LEFT: tx > 0, RIGHT: tx < txs - 1, UP: ty > 0, DOWN: ty < tys - 1}
    has[UP_CORNER], has[DOWN_CORNER] = has[UP], has[DOWN]
    cross_right, cross_left = tx == txs // 2 - 1, tx == txs // 2
    mirror = modes - 1 - mode
    left_mode = jnp.where(cross_left, mirror, mode)
    right_mode = jnp.where(cross_right, mirror, mode)
    target = {
        LEFT: {"mode": left_mode, "ty": ty, "tx": tx - 1},
        RIGHT: {"mode": right_mode, "ty": ty, "tx": tx + 1},
        UP: {"mode": mode, "ty": ty - 1, "tx": tx},
        DOWN: {"mode": mode, "ty": ty + 1, "tx": tx},
    }
    crossing = {LEFT: cross_left, RIGHT: cross_right}
    relay_tx = {LEFT: txs - 1, RIGHT: 0}
    relaying = {LEFT: tx == relay_tx[LEFT], RIGHT: tx == relay_tx[RIGHT]}
    landing_tx = {LEFT: txs // 2 - 1, RIGHT: txs // 2}
    direct = {LEFT: {"mode": mode, "ty": ty, "tx": tx - 1}, RIGHT: {"mode": mode, "ty": ty, "tx": tx + 1}}

    def peer(step):
        return {"mode": lax.rem(mode + step, modes), "ty": ty, "tx": tx}

    loads = [pltpu.make_async_copy(src, dst, load.at[i]) for i, (src, dst) in enumerate(((probe_in, probe), (mats_in, mats), (measured_in, measured)))]
    for copy in loads:
        copy.start()

    for side in (LEFT, RIGHT):

        @pl.when(jnp.logical_not(has[side]))
        def _():
            rs[:, side] = jnp.zeros_like(rs[:, side])
            gh[side] = jnp.zeros_like(gh[side])
            gc[:, side] = jnp.zeros_like(gc[:, side])

    for side in (UP, DOWN):

        @pl.when(jnp.logical_not(has[side]))
        def _():
            vt[:, side - UP] = jnp.zeros_like(vt[:, side - UP])
            cr[:, side - UP] = jnp.zeros_like(cr[:, side - UP])
            gv[side - UP] = jnp.zeros_like(gv[side - UP])
            gc[side - UP] = jnp.zeros_like(gc[side - UP])

    for s in range(SLICES):
        for c in range(2):
            for b in range(2):
                left_edge, right_edge = packed_edges(obj[s, c, b * HALF : (b + 1) * HALF])
                pk[s, LEFT, c, b * BLOCK : (b + 1) * BLOCK] = left_edge
                pk[s, RIGHT, c, b * BLOCK : (b + 1) * BLOCK] = right_edge

    barrier = pltpu.get_barrier_semaphore()
    count = jnp.int32(modes - 1)
    for side in (LEFT, RIGHT, UP, DOWN):
        count = count + has[side].astype(jnp.int32)

        @pl.when(has[side])
        def _():
            pl.semaphore_signal(barrier, inc=1, device_id=target[side], device_id_type=MESH)

    for side, cross in ((LEFT, cross_left), (RIGHT, cross_right)):
        far_pair = jnp.logical_and(cross, has[side])
        count = count + far_pair.astype(jnp.int32)

        @pl.when(far_pair)
        def _():
            pl.semaphore_signal(barrier, inc=1, device_id=direct[side], device_id_type=MESH)

    for side in (LEFT, RIGHT):
        from_relay, from_landing = crossing[side], relaying[side]
        count = count + from_relay.astype(jnp.int32) + from_landing.astype(jnp.int32)

        @pl.when(relaying[side])
        def _():
            sender = {"mode": mode, "ty": ty, "tx": landing_tx[1 - side]}
            pl.semaphore_signal(barrier, inc=1, device_id=sender, device_id_type=MESH)

        @pl.when(tx == landing_tx[side])
        def _():
            relay = {"mode": mirror, "ty": ty, "tx": relay_tx[side]}
            pl.semaphore_signal(barrier, inc=1, device_id=relay, device_id_type=MESH)

    for step in range(1, modes):
        pl.semaphore_signal(barrier, inc=1, device_id=peer(step), device_id_type=MESH)
    pl.semaphore_wait(barrier, count)

    opposite = {LEFT: RIGHT, RIGHT: LEFT, UP: DOWN, DOWN: UP, UP_CORNER: DOWN_CORNER, DOWN_CORNER: UP_CORNER}

    def landing(s, kind):
        if kind in (LEFT, RIGHT):
            return rs.at[s, kind]
        if kind in (UP, DOWN):
            return vt.at[s, kind - UP]
        return cr.at[s, kind - UP_CORNER]

    def source(s, kind):
        if kind in (LEFT, RIGHT):
            return pk.at[s, kind]
        if kind in (UP, DOWN):
            return obj.at[s, :, (kind - UP) * HALF : (kind - UP + 1) * HALF]
        return rs.at[s, :, :, (kind - UP_CORNER) * BLOCK : (kind - UP_CORNER + 1) * BLOCK]

    def halo_copy(s, kind):
        return pltpu.make_async_remote_copy(
            src_ref=source(s, kind),
            dst_ref=landing(s, opposite[kind]),
            send_sem=halo_send.at[s, kind],
            recv_sem=halo_recv.at[s, opposite[kind]],
            device_id=target[kind if kind < UP_CORNER else kind - 2],
            device_id_type=MESH,
        )

    def straight_copy(s, kind):
        return pltpu.make_async_remote_copy(
            src_ref=pk.at[s, kind, 0],
            dst_ref=rs.at[s, opposite[kind], 0],
            send_sem=cross_send.at[s, 0],
            recv_sem=cross_recv.at[s, 0],
            device_id=target[kind],
            device_id_type=MESH,
        )

    def detour_copy(s, kind):
        return pltpu.make_async_remote_copy(
            src_ref=pk.at[s, kind, 1],
            dst_ref=rl.at[s],
            send_sem=cross_send.at[s, 1],
            recv_sem=relay_recv.at[s],
            device_id={"mode": mode, "ty": ty, "tx": relay_tx[kind]},
            device_id_type=MESH,
        )

    def onward_copy(s, kind):
        return pltpu.make_async_remote_copy(
            src_ref=rl.at[s],
            dst_ref=rs.at[s, opposite[kind], 1],
            send_sem=relay_send.at[s],
            recv_sem=cross_recv.at[s, 1],
            device_id={"mode": mirror, "ty": ty, "tx": landing_tx[kind]},
            device_id_type=MESH,
        )

    def near(kind):
        return jnp.logical_and(has[kind], jnp.logical_not(crossing[kind])) if kind in crossing else has[kind]

    def start_halo(s, kind):
        @pl.when(near(kind))
        def _():
            halo_copy(s, kind).start()

        if kind in crossing:

            @pl.when(crossing[kind])
            def _():
                straight_copy(s, kind).start()
                detour_copy(s, kind).start()

    def await_halo(s, kind):
        @pl.when(near(kind))
        def _():
            halo_copy(s, opposite[kind]).wait_recv()

        if kind in crossing:

            @pl.when(crossing[kind])
            def _():
                straight_copy(s, opposite[kind]).wait_recv()
                onward_copy(s, opposite[kind]).wait_recv()

    def relay(s):
        for kind in (LEFT, RIGHT):

            @pl.when(relaying[kind])
            def _():
                detour_copy(s, kind).wait_recv()
                onward_copy(s, kind).start()

    for s in range(SLICES):
        for kind in (LEFT, RIGHT, UP, DOWN):
            start_halo(s, kind)

    def relay_corners(s):
        await_halo(s, LEFT)
        await_halo(s, RIGHT)
        start_halo(s, UP_CORNER)
        start_halo(s, DOWN_CORNER)

    row, col = pos_ref[0], pos_ref[1]
    here, there = (lax.broadcasted_iota(jnp.int32, (DET, 2 * DET), d) for d in range(2))
    pick_rows = jnp.where(there == here + row, 1.0, 0.0).astype(BF16)
    offset = here + (col + 2 * DET - HALF)
    offset = jnp.where(offset >= 2 * DET, offset - 2 * DET, offset)
    pick_cols = jnp.where(there == offset, 1.0, 0.0).astype(BF16)
    here, there = (lax.broadcasted_iota(jnp.int32, (2 * DET, DET), d) for d in range(2))
    put_rows = jnp.where(here == there + row, 1.0, 0.0).astype(BF16)
    offset = there + (col + 2 * DET - HALF)
    offset = jnp.where(offset >= 2 * DET, offset - 2 * DET, offset)
    put_cols = jnp.where(here == offset, 1.0, 0.0).astype(BF16)

    def twice(x, axis):
        return jnp.concatenate([x, x], axis=axis)

    def both(x, axis):
        return jnp.concatenate(halves(x), axis=axis)

    def dot(x, y):
        return jnp.dot(x, y, preferred_element_type=F32)

    def build_window(s):
        for kind in (UP, DOWN, UP_CORNER, DOWN_CORNER):
            await_halo(s, kind)
        for c in range(2):
            for side in range(2):
                at = side * 3 * HALF
                ext[c, at : at + HALF, :DET] = vt[s, side, c]
                first, second = unpacked_sides(cr[s, side, LEFT, c], cr[s, side, RIGHT, c])
                ext[c, at : at + BLOCK, DET:] = first
                ext[c, at + BLOCK : at + HALF, DET:] = second
            ext[c, HALF : 3 * HALF, :DET] = obj[s, c]
            for b in range(2):
                block = slice(b * BLOCK, (b + 1) * BLOCK)
                first, second = unpacked_sides(rs[s, LEFT, c, block], rs[s, RIGHT, c, block])
                at = HALF + b * HALF
                ext[c, at : at + BLOCK, DET:] = first
                ext[c, at + BLOCK : at + HALF, DET:] = second
            band = dot(twice(pick_rows, 1), both(ext[c], 0))
            window[s, c] = dot(both(band, 1), twice(put_cols, 0))

    relay_corners(0)
    relay(0)
    for s in range(SLICES):
        if s + 1 < SLICES:
            relay_corners(s + 1)
        for ahead in range(2 * s, min(2 * s + 2, SLICES)):
            if ahead:
                relay(ahead)
        build_window(s)
        if s == 0:
            for copy in loads:
                copy.wait()

        def fetch(m):
            if s == 0:
                real, imag = probe[m, 0], probe[m, 1]
            else:
                real, imag = psi[s - 1, 0, rows(m)], psi[s - 1, 1, rows(m)]
            wr, wi = window[s, 0], window[s, 1]
            return real * wr - imag * wi, real * wi + imag * wr

        def deliver(m, real, imag):
            if s + 1 < SLICES:
                psi[s, 0, rows(m)] = real
                psi[s, 1, rows(m)] = imag
            else:
                far[0, rows(m)] = real
                far[1, rows(m)] = imag
                power = real * real + imag * imag
                part[...] = power if m == 0 else part[...] + power

        two_sided(mats, STEP if s + 1 < SLICES else FAR, fetch, deliver, mid)

    first, last = mode == 0, mode == modes - 1
    inner, lower = jnp.logical_not(jnp.logical_or(first, last)), mode < modes // 2

    def mode_copy(step):
        return pltpu.make_async_remote_copy(
            src_ref=part,
            dst_ref=others.at[step - 1],
            send_sem=mode_send.at[step - 1],
            recv_sem=mode_recv.at[step - 1],
            device_id=peer(step),
            device_id_type=MESH,
        )

    for step in range(1, modes):
        mode_copy(step).start()
    whole = part[...]
    for step in range(1, modes):
        mode_copy(step).wait_recv()
        whole = whole + others[step - 1]
    weight = 1.0 - measured[0, 0, 0] / jnp.maximum(jnp.sqrt(whole), 1.0)

    outer, collector = jnp.logical_or(first, last), jnp.where(lower, 1, 2)

    def far_slice(low_pair, i):
        return SLICES - 1 - i if low_pair else 1 - i

    def piece(q):
        return q // 2, pl.ds(q % 2 * HALF, HALF)

    def collect_copy(low_pair, i, q):
        return pltpu.make_async_remote_copy(
            src_ref=term.at[(far_slice(low_pair, i), *piece(q))],
            dst_ref=collected.at[(i, *piece(q))],
            send_sem=collect_send.at[i, q],
            recv_sem=collect_recv.at[i, q],
            device_id={"mode": collector, "ty": ty, "tx": tx},
            device_id_type=MESH,
        )

    def pair_sum_copy(low_pair, i, q):
        return pltpu.make_async_remote_copy(
            src_ref=joint.at[(i, *piece(q))],
            dst_ref=parts.at[(1, *piece(q))],
            send_sem=joint_send.at[i, q],
            recv_sem=joint_recv.at[q],
            device_id={"mode": far_slice(low_pair, i), "ty": ty, "tx": tx},
            device_id_type=MESH,
        )

    def partner_copy(owner):
        return pltpu.make_async_remote_copy(
            src_ref=term.at[owner],
            dst_ref=parts.at[0],
            send_sem=partner_send,
            recv_sem=partner_recv,
            device_id={"mode": owner, "ty": ty, "tx": tx},
            device_id_type=MESH,
        )

    def send_far(low_pair, i):
        @pl.when(first if low_pair else last)
        def _():
            for q in range(4):
                collect_copy(low_pair, i, q).start()

    def send_partner(owner):
        @pl.when(mode == (owner ^ 1))
        def _():
            partner_copy(owner).start()

    def join(low_pair, i):
        s = far_slice(low_pair, i)
        for q in range(4):
            collect_copy(low_pair, i, q).wait_recv()
            at = piece(q)
            joint[(i, *at)] = collected[(i, *at)] + term[(s, *at)]
            pair_sum_copy(low_pair, i, q).start()

    for s in reversed(range(SLICES)):

        def fetch(m):
            if s == SLICES - 1:
                return weight * far[0, rows(m)], weight * far[1, rows(m)]
            return pulled[0, rows(m)], pulled[1, rows(m)]

        def deliver(m, real, imag):
            if s == 0:
                pr, pi = probe[m, 0], probe[m, 1]
            else:
                pr, pi = psi[s - 1, 0, rows(m)], psi[s - 1, 1, rows(m)]
            tr, ti = pr * real + pi * imag, pr * imag - pi * real
            term[s, 0] = tr if m == 0 else term[s, 0] + tr
            term[s, 1] = ti if m == 0 else term[s, 1] + ti
            if s > 0:
                wr, wi = window[s, 0], window[s, 1]
                pulled[0, rows(m)] = wr * real + wi * imag
                pulled[1, rows(m)] = wr * imag - wi * real

        two_sided(mats, FAR_BACK if s == SLICES - 1 else STEP_BACK, fetch, deliver, mid)

        if s == 3:
            send_far(True, 0)
            send_partner(3)
        elif s == 2:
            send_far(True, 1)
        elif s == 1:
            send_partner(1)
        else:
            send_far(False, 1)
            send_partner(0)
            send_far(False, 0)
            send_partner(2)

    for low_pair in (True, False):

        @pl.when(mode == (1 if low_pair else 2))
        def _():
            join(low_pair, 0 if low_pair else 1)
            join(low_pair, 1 if low_pair else 0)

    partner_copy(0).wait_recv()
    for q in range(4):
        pair_sum_copy(True, 0, q).wait_recv()
    for c in range(2):
        mine = term[mode, c]
        mine = mine + parts[0, c] + parts[1, c]
        tall = dot(twice(put_rows, 1), both(mine, 0))
        placed = dot(both(tall, 1), twice(pick_cols, 0))
        middle[c] = placed[HALF : 3 * HALF, :DET]
        for v in range(2):
            at = 3 * v * HALF
            vp[v, c] = placed[at : at + HALF, :DET]
            cp[v, LEFT, c], cp[v, RIGHT, c] = packed_sides(placed[at : at + HALF, DET:])
        hp[LEFT, c], hp[RIGHT, c] = packed_sides(placed[HALF : 3 * HALF, DET:])

    def grad_has(v, h):
        if v is None:
            return has[h]
        return has[UP + v] if h is None else jnp.logical_and(has[UP + v], has[h])

    def grad_copy(v, h):
        if v is None:
            src, dst, i = hp.at[h], gh.at[1 - h], h
        elif h is None:
            src, dst, i = vp.at[v], gv.at[1 - v], 2 + v
        else:
            src, dst, i = cp.at[v, h], gc.at[1 - v, 1 - h], 4 + 2 * v + h
        return pltpu.make_async_remote_copy(
            src_ref=src,
            dst_ref=dst,
            send_sem=grad_send.at[i],
            recv_sem=grad_recv.at[i],
            device_id={"mode": mode, "ty": ty if v is None else ty + 2 * v - 1, "tx": tx if h is None else tx + 2 * h - 1},
            device_id_type=MESH,
        )

    directions = [(None, 0), (None, 1), (0, 0), (0, 1), (1, 0), (1, 1), (0, None), (1, None)]
    for v, h in directions:

        @pl.when(grad_has(v, h))
        def _():
            grad_copy(v, h).start()

    for v, h in reversed(directions):
        @pl.when(grad_has(v, h))
        def _():
            grad_copy(v if v is None else 1 - v, h if h is None else 1 - h).wait_recv()

    for c in range(2):
        for v in range(2):
            half = slice(v * HALF, (v + 1) * HALF)
            sides = unpacked_halves(gh[LEFT, c], gh[RIGHT, c])[v]
            corners = jnp.concatenate(unpacked_halves(gc[v, LEFT, c], gc[v, RIGHT, c]), axis=0)
            out[0, c, half] = middle[c, half] + gv[v, c] + (sides + corners)

    for v, h in directions:

        @pl.when(grad_has(v, h))
        def _():
            grad_copy(v, h).wait_send()

    for kind in range(6):

        @pl.when(near(kind))
        def _():
            for s in range(SLICES):
                halo_copy(s, kind).wait_send()

    for kind in (LEFT, RIGHT):

        @pl.when(crossing[kind])
        def _():
            for s in range(SLICES):
                straight_copy(s, kind).wait_send()
                detour_copy(s, kind).wait_send()

        @pl.when(relaying[kind])
        def _():
            for s in range(SLICES):
                onward_copy(s, kind).wait_send()

    for step in range(1, modes):
        mode_copy(step).wait_send()

    partner_copy(0).wait_send()
    for i in range(2):
        for q in range(4):

            @pl.when(outer)
            def _():
                collect_copy(True, i, q).wait_send()

            @pl.when(inner)
            def _():
                pair_sum_copy(True, i, q).wait_send()


VMEM = pl.BlockSpec(memory_space=pltpu.VMEM)
SMEM = pl.BlockSpec(memory_space=pltpu.SMEM)
ANY = pl.BlockSpec(memory_space=pl.ANY)


def body(object_slices, probe_modes, positions, measured):
    mats = jnp.asarray(tables())
    modes = lax.axis_size("mode")
    dma = pltpu.SemaphoreType.DMA
    wave = (LOCAL * DET, DET)
    scratch = dict(
        probe=(LOCAL, 2, DET, DET),
        measured=(1, 1, 1, DET, DET),
        mats=(8, 2 * DET, 2 * DET),
        pk=(SLICES, 2, 2, HALF, DET),
        rs=(SLICES, 2, 2, HALF, DET),
        rl=(SLICES, HALF, DET),
        vt=(SLICES, 2, 2, HALF, DET),
        cr=(SLICES, 2, 2, 2, BLOCK, DET),
        ext=(2, 2 * DET, 2 * DET),
        window=(SLICES, 2, DET, DET),
        psi=(SLICES - 1, 2, *wave),
        far=(2, *wave),
        part=(DET, DET),
        others=(modes - 1, DET, DET),
        mid=(4 * DET, LOCAL * DET),
        pulled=(2, *wave),
        term=(SLICES, 2, DET, DET),
        collected=(2, 2, DET, DET),
        joint=(2, 2, DET, DET),
        parts=(2, 2, DET, DET),
        middle=(2, DET, DET),
        vp=(2, 2, HALF, DET),
        hp=(2, 2, HALF, DET),
        cp=(2, 2, 2, BLOCK, DET),
        gv=(2, 2, HALF, DET),
        gh=(2, 2, HALF, DET),
        gc=(2, 2, 2, BLOCK, DET),
    )
    return pl.pallas_call(
        kernel,
        out_shape=jax.ShapeDtypeStruct((1, 2, DET, DET), F32),
        in_specs=[SMEM, VMEM, ANY, ANY, ANY],
        out_specs=VMEM,
        scratch_shapes=[pltpu.VMEM(shape, BF16 if name in ("mid", "mats") else F32) for name, shape in scratch.items()]
        + [dma((3,))]
        + [dma((SLICES, 6)), dma((SLICES, 6))]
        + [dma((SLICES, 2)), dma((SLICES, 2)), dma((SLICES,)), dma((SLICES,))]
        + [dma((modes - 1,)), dma((modes - 1,))]
        + [dma((2, 4)), dma((2, 4)), dma((2, 4)), dma((4,)), dma, dma]
        + [dma((8,)), dma((8,))],
        compiler_params=pltpu.CompilerParams(collective_id=0, has_side_effects=True),
        name="ptycho",
    )(positions.reshape(2), object_slices, probe_modes, measured, mats)


def solution(mesh):
    return jax.shard_map(
        body,
        mesh=mesh,
        in_specs=(
            P(None, None, "ty", "tx"),
            P("mode", None, None, None),
            P("ty", "tx", None, None),
            P("ty", "tx", None, None, None),
        ),
        out_specs=P("mode", None, "ty", "tx"),
        check_vma=False,
    )
```

```python
import functools

import numpy as np
import jax
import jax.numpy as jnp
from jax import lax
from jax.experimental import pallas as pl
from jax.experimental.pallas import tpu as pltpu
from jax.sharding import PartitionSpec as P

DET = 128
SLICES = 4
MARGIN = 64
LOCAL = 4
RATE = 0.3
F32 = jnp.float32
BF16 = jnp.bfloat16


def real_block(matrix):
    return np.block([[matrix.real, matrix.imag], [-matrix.imag, matrix.real]])


def tables():
    counter = np.arange(DET)
    fourier = np.exp(-2j * np.pi * (np.outer(counter, counter) % DET) / DET) / np.sqrt(DET)
    frequency = np.where(counter < DET // 2, counter, counter - DET).astype(np.float64)
    chirp = np.exp(-1j * RATE * frequency**2 / DET)
    step = fourier.conj() @ (chirp[:, None] * fourier)
    step = (step + step.T) / 2
    out = []
    for matrix in (step, step.conj(), fourier, fourier.conj()):
        block = real_block(matrix).astype(np.float32)
        high = block.astype(jnp.bfloat16)
        low = (block - high.astype(np.float32)).astype(jnp.bfloat16)
        out += [high, low]
    return np.stack(out)


STEP, STEP_BACK, FAR, FAR_BACK = range(4)
CONJ = {STEP: STEP_BACK, STEP_BACK: STEP, FAR: FAR_BACK, FAR_BACK: FAR}


def halves(x):
    high = x.astype(BF16)
    return high, (x - high.astype(F32)).astype(BF16)


def rows(m):
    return slice(m * DET, (m + 1) * DET)


def right_product(mats, which, real, imag):
    rh, rl = halves(real)
    ih, il = halves(imag)
    lhs = jnp.concatenate([rh, ih, rl, il, rh, ih], axis=1)
    high, low = mats[2 * which], mats[2 * which + 1]
    rhs = jnp.concatenate([high, high, low], axis=0)
    return jnp.dot(lhs, rhs, preferred_element_type=F32)


def left_product(mats, which, stacked):
    conj = CONJ[which]
    high, low = mats[2 * conj], mats[2 * conj + 1]
    main = jnp.dot(jnp.concatenate([high, low], axis=0), stacked[: 2 * DET], preferred_element_type=F32)
    rest = jnp.dot(high, stacked[2 * DET :], preferred_element_type=F32)
    return main[: 2 * DET] + main[2 * DET :] + rest


def two_sided(mats, which, fetch, deliver, mid):
    for m in range(LOCAL):
        real, imag = fetch(m)
        out = right_product(mats, which, real, imag)
        rh, rl = halves(out[:, :DET])
        ih, il = halves(out[:, DET:])
        for part, value in enumerate((rh, ih, rl, il)):
            mid[rows(part), rows(m)] = value
    for pair in range(LOCAL // 2):
        out = left_product(mats, which, mid[:, pair * 2 * DET : (pair + 1) * 2 * DET])
        for k in range(2):
            deliver(2 * pair + k, out[:DET, rows(k)], out[DET:, rows(k)])

MESH = pl.DeviceIdType.MESH
HALF = DET // 2
BLOCK = HALF // 2
EXTRA = 8
STRAIGHT = ((0, slice(0, HALF)), (1, slice(0, EXTRA)))


def lane_low(shape):
    return lax.broadcasted_iota(jnp.int32, shape, len(shape) - 1) < HALF


def turned(x):
    return pltpu.roll(x, HALF, x.ndim - 1)


def packed_edges(strip):
    first, second = strip[:BLOCK], strip[BLOCK:]
    low = lane_low(first.shape)
    left_edge = jnp.where(low, first, turned(second))
    right_edge = jnp.where(low, turned(first), second)
    return left_edge, right_edge


def unpacked_sides(from_left, from_right):
    low = lane_low(from_left.shape)
    first = jnp.where(low, from_right, turned(from_left))
    second = jnp.where(low, turned(from_right), from_left)
    return first, second


def packed_sides(strip):
    half = strip.shape[0] // 2
    upper, lower = strip[:half], strip[half:]
    low = lane_low(upper.shape)
    return jnp.where(low, turned(upper), lower), jnp.where(low, upper, turned(lower))


def unpacked_halves(from_left, from_right):
    low = lane_low(from_left.shape)
    return jnp.where(low, from_left, turned(from_right)), jnp.where(low, turned(from_left), from_right)


LEFT, RIGHT, UP, DOWN, UP_CORNER, DOWN_CORNER = range(6)


def kernel(
    pos_ref, obj_in, probe_in, measured_in, mats_in, out,
    obj, probe, measured, mats, pk, rs, rl, vt, cr, ext, window, psi, far, part, others, mid, pulled, term, collected, joint, parts, middle, vp, hp, cp, gv, gh, gc,
    load, halo_send, halo_recv, cross_send, cross_recv, relay_send, relay_recv, mode_send, mode_recv, collect_send, collect_recv, joint_send, joint_recv, partner_send, partner_recv, grad_send, grad_recv,
):
    mode, ty, tx = lax.axis_index("mode"), lax.axis_index("ty"), lax.axis_index("tx")
    modes, tys, txs = lax.axis_size("mode"), lax.axis_size("ty"), lax.axis_size("tx")
    has = {LEFT: tx > 0, RIGHT: tx < txs - 1, UP: ty > 0, DOWN: ty < tys - 1}
    has[UP_CORNER], has[DOWN_CORNER] = has[UP], has[DOWN]
    cross_right, cross_left = tx == txs // 2 - 1, tx == txs // 2
    mirror = modes - 1 - mode
    left_mode = jnp.where(cross_left, mirror, mode)
    right_mode = jnp.where(cross_right, mirror, mode)
    target = {
        LEFT: {"mode": left_mode, "ty": ty, "tx": tx - 1},
        RIGHT: {"mode": right_mode, "ty": ty, "tx": tx + 1},
        UP: {"mode": mode, "ty": ty - 1, "tx": tx},
        DOWN: {"mode": mode, "ty": ty + 1, "tx": tx},
    }
    crossing = {LEFT: cross_left, RIGHT: cross_right}
    relay_tx = {LEFT: txs - 1, RIGHT: 0}
    relaying = {LEFT: tx == relay_tx[LEFT], RIGHT: tx == relay_tx[RIGHT]}
    landing_tx = {LEFT: txs // 2 - 1, RIGHT: txs // 2}
    direct = {LEFT: {"mode": mode, "ty": ty, "tx": tx - 1}, RIGHT: {"mode": mode, "ty": ty, "tx": tx + 1}}

    def peer(step):
        return {"mode": lax.rem(mode + step, modes), "ty": ty, "tx": tx}

    barrier = pltpu.get_barrier_semaphore()
    count = jnp.int32(modes - 1)
    for side in (LEFT, RIGHT, UP, DOWN):
        count = count + has[side].astype(jnp.int32)

        @pl.when(has[side])
        def _():
            pl.semaphore_signal(barrier, inc=1, device_id=target[side], device_id_type=MESH)

    for side, cross in ((LEFT, cross_left), (RIGHT, cross_right)):
        far_pair = jnp.logical_and(cross, has[side])
        count = count + far_pair.astype(jnp.int32)

        @pl.when(far_pair)
        def _():
            pl.semaphore_signal(barrier, inc=1, device_id=direct[side], device_id_type=MESH)

    for side in (LEFT, RIGHT):
        from_relay, from_landing = crossing[side], relaying[side]
        count = count + from_relay.astype(jnp.int32) + from_landing.astype(jnp.int32)

        @pl.when(relaying[side])
        def _():
            sender = {"mode": mode, "ty": ty, "tx": landing_tx[1 - side]}
            pl.semaphore_signal(barrier, inc=1, device_id=sender, device_id_type=MESH)

        @pl.when(tx == landing_tx[side])
        def _():
            relay = {"mode": mirror, "ty": ty, "tx": relay_tx[side]}
            pl.semaphore_signal(barrier, inc=1, device_id=relay, device_id_type=MESH)

    for step in range(1, modes):
        pl.semaphore_signal(barrier, inc=1, device_id=peer(step), device_id_type=MESH)
    object_loads = [pltpu.make_async_copy(obj_in.at[s], obj.at[s], load.at[3 + s]) for s in range(SLICES)]
    loads = [pltpu.make_async_copy(src, dst, load.at[i]) for i, (src, dst) in enumerate(((probe_in, probe), (mats_in, mats), (measured_in, measured)))]
    for copy in object_loads + loads:
        copy.start()

    for side in (LEFT, RIGHT):

        @pl.when(jnp.logical_not(has[side]))
        def _():
            rs[:, side] = jnp.zeros_like(rs[:, side])
            gh[side] = jnp.zeros_like(gh[side])
            gc[:, side] = jnp.zeros_like(gc[:, side])

    for side in (UP, DOWN):

        @pl.when(jnp.logical_not(has[side]))
        def _():
            vt[:, side - UP] = jnp.zeros_like(vt[:, side - UP])
            cr[:, side - UP] = jnp.zeros_like(cr[:, side - UP])
            gv[side - UP] = jnp.zeros_like(gv[side - UP])
            gc[side - UP] = jnp.zeros_like(gc[side - UP])

    def pack(s):
        object_loads[s].wait()
        for c in range(2):
            for b in range(2):
                left_edge, right_edge = packed_edges(obj[s, c, b * HALF : (b + 1) * HALF])
                pk[s, LEFT, c, b * BLOCK : (b + 1) * BLOCK] = left_edge
                pk[s, RIGHT, c, b * BLOCK : (b + 1) * BLOCK] = right_edge

    pack(0)
    pl.semaphore_wait(barrier, count)

    opposite = {LEFT: RIGHT, RIGHT: LEFT, UP: DOWN, DOWN: UP, UP_CORNER: DOWN_CORNER, DOWN_CORNER: UP_CORNER}

    def landing(s, kind):
        if kind in (LEFT, RIGHT):
            return rs.at[s, kind]
        if kind in (UP, DOWN):
            return vt.at[s, kind - UP]
        return cr.at[s, kind - UP_CORNER]

    def source(s, kind):
        if kind in (LEFT, RIGHT):
            return pk.at[s, kind]
        if kind in (UP, DOWN):
            return obj.at[s, :, (kind - UP) * HALF : (kind - UP + 1) * HALF]
        return rs.at[s, :, :, (kind - UP_CORNER) * BLOCK : (kind - UP_CORNER + 1) * BLOCK]

    def halo_copy(s, kind):
        return pltpu.make_async_remote_copy(
            src_ref=source(s, kind),
            dst_ref=landing(s, opposite[kind]),
            send_sem=halo_send.at[s, kind],
            recv_sem=halo_recv.at[s, opposite[kind]],
            device_id=target[kind if kind < UP_CORNER else kind - 2],
            device_id_type=MESH,
        )

    def straight_copy(s, kind, i):
        return pltpu.make_async_remote_copy(
            src_ref=pk.at[(s, kind, *STRAIGHT[i])],
            dst_ref=rs.at[(s, opposite[kind], *STRAIGHT[i])],
            send_sem=cross_send.at[s, 2 * i],
            recv_sem=cross_recv.at[s, 2 * i],
            device_id=target[kind],
            device_id_type=MESH,
        )

    def detour_copy(s, kind):
        return pltpu.make_async_remote_copy(
            src_ref=pk.at[s, kind, 1, EXTRA:],
            dst_ref=rl.at[s],
            send_sem=cross_send.at[s, 1],
            recv_sem=relay_recv.at[s],
            device_id={"mode": mode, "ty": ty, "tx": relay_tx[kind]},
            device_id_type=MESH,
        )

    def onward_copy(s, kind):
        return pltpu.make_async_remote_copy(
            src_ref=rl.at[s],
            dst_ref=rs.at[s, opposite[kind], 1, EXTRA:],
            send_sem=relay_send.at[s],
            recv_sem=cross_recv.at[s, 1],
            device_id={"mode": mirror, "ty": ty, "tx": landing_tx[kind]},
            device_id_type=MESH,
        )

    def near(kind):
        return jnp.logical_and(has[kind], jnp.logical_not(crossing[kind])) if kind in crossing else has[kind]

    def start_halo(s, kind):
        @pl.when(near(kind))
        def _():
            halo_copy(s, kind).start()

        if kind in crossing:

            @pl.when(crossing[kind])
            def _():
                straight_copy(s, kind, 0).start()
                straight_copy(s, kind, 1).start()
                detour_copy(s, kind).start()

    def await_halo(s, kind):
        @pl.when(near(kind))
        def _():
            halo_copy(s, opposite[kind]).wait_recv()

        if kind in crossing:

            @pl.when(crossing[kind])
            def _():
                straight_copy(s, opposite[kind], 0).wait_recv()
                straight_copy(s, opposite[kind], 1).wait_recv()
                onward_copy(s, opposite[kind]).wait_recv()

    def relay(s):
        for kind in (LEFT, RIGHT):

            @pl.when(relaying[kind])
            def _():
                detour_copy(s, kind).wait_recv()
                onward_copy(s, kind).start()

    for s in range(SLICES):
        if s + 1 < SLICES:
            pack(s + 1)
        for kind in (RIGHT, LEFT, UP, DOWN):
            start_halo(s, kind)

    def relay_corners(s):
        await_halo(s, LEFT)
        await_halo(s, RIGHT)
        start_halo(s, UP_CORNER)
        start_halo(s, DOWN_CORNER)

    row, col = pos_ref[0], pos_ref[1]
    here, there = (lax.broadcasted_iota(jnp.int32, (DET, 2 * DET), d) for d in range(2))
    pick_rows = jnp.where(there == here + row, 1.0, 0.0).astype(BF16)
    offset = here + (col + 2 * DET - HALF)
    offset = jnp.where(offset >= 2 * DET, offset - 2 * DET, offset)
    pick_cols = jnp.where(there == offset, 1.0, 0.0).astype(BF16)
    here, there = (lax.broadcasted_iota(jnp.int32, (2 * DET, DET), d) for d in range(2))
    put_rows = jnp.where(here == there + row, 1.0, 0.0).astype(BF16)
    offset = there + (col + 2 * DET - HALF)
    offset = jnp.where(offset >= 2 * DET, offset - 2 * DET, offset)
    put_cols = jnp.where(here == offset, 1.0, 0.0).astype(BF16)

    def twice(x, axis):
        return jnp.concatenate([x, x], axis=axis)

    def both(x, axis):
        return jnp.concatenate(halves(x), axis=axis)

    def dot(x, y):
        return jnp.dot(x, y, preferred_element_type=F32)

    def build_window(s):
        for kind in (UP, DOWN, UP_CORNER, DOWN_CORNER):
            await_halo(s, kind)
        for c in range(2):
            for side in range(2):
                at = side * 3 * HALF
                ext[c, at : at + HALF, :DET] = vt[s, side, c]
                first, second = unpacked_sides(cr[s, side, LEFT, c], cr[s, side, RIGHT, c])
                ext[c, at : at + BLOCK, DET:] = first
                ext[c, at + BLOCK : at + HALF, DET:] = second
            ext[c, HALF : 3 * HALF, :DET] = obj[s, c]
            for b in range(2):
                block = slice(b * BLOCK, (b + 1) * BLOCK)
                first, second = unpacked_sides(rs[s, LEFT, c, block], rs[s, RIGHT, c, block])
                at = HALF + b * HALF
                ext[c, at : at + BLOCK, DET:] = first
                ext[c, at + BLOCK : at + HALF, DET:] = second
            band = dot(twice(pick_rows, 1), both(ext[c], 0))
            window[s, c] = dot(both(band, 1), twice(put_cols, 0))

    relay(0)
    relay_corners(0)
    for s in range(SLICES):
        if s + 1 < SLICES:
            relay_corners(s + 1)
        if s == 0:
            for ahead in range(1, SLICES):
                relay(ahead)
        build_window(s)
        if s == 0:
            for copy in loads:
                copy.wait()

        def fetch(m):
            if s == 0:
                real, imag = probe[m, 0], probe[m, 1]
            else:
                real, imag = psi[s - 1, 0, rows(m)], psi[s - 1, 1, rows(m)]
            wr, wi = window[s, 0], window[s, 1]
            return real * wr - imag * wi, real * wi + imag * wr

        def deliver(m, real, imag):
            if s + 1 < SLICES:
                psi[s, 0, rows(m)] = real
                psi[s, 1, rows(m)] = imag
            else:
                far[0, rows(m)] = real
                far[1, rows(m)] = imag
                power = real * real + imag * imag
                part[...] = power if m == 0 else part[...] + power

        two_sided(mats, STEP if s + 1 < SLICES else FAR, fetch, deliver, mid)

    first, last = mode == 0, mode == modes - 1
    inner, lower = jnp.logical_not(jnp.logical_or(first, last)), mode < modes // 2

    def mode_copy(step):
        return pltpu.make_async_remote_copy(
            src_ref=part,
            dst_ref=others.at[step - 1],
            send_sem=mode_send.at[step - 1],
            recv_sem=mode_recv.at[step - 1],
            device_id=peer(step),
            device_id_type=MESH,
        )

    for step in range(1, modes):
        mode_copy(step).start()
    whole = part[...]
    for step in range(1, modes):
        mode_copy(step).wait_recv()
        whole = whole + others[step - 1]
    weight = 1.0 - measured[0, 0, 0] / jnp.maximum(jnp.sqrt(whole), 1.0)

    outer, collector = jnp.logical_or(first, last), jnp.where(lower, 1, 2)

    def far_slice(low_pair, i):
        return SLICES - 1 - i if low_pair else 1 - i

    def piece(q):
        return q // 2, pl.ds(q % 2 * HALF, HALF)

    def collect_copy(low_pair, i, q):
        return pltpu.make_async_remote_copy(
            src_ref=term.at[(far_slice(low_pair, i), *piece(q))],
            dst_ref=collected.at[(i, *piece(q))],
            send_sem=collect_send.at[i, q],
            recv_sem=collect_recv.at[i, q],
            device_id={"mode": collector, "ty": ty, "tx": tx},
            device_id_type=MESH,
        )

    def pair_sum_copy(low_pair, i, q):
        return pltpu.make_async_remote_copy(
            src_ref=joint.at[(i, *piece(q))],
            dst_ref=parts.at[(1, *piece(q))],
            send_sem=joint_send.at[i, q],
            recv_sem=joint_recv.at[q],
            device_id={"mode": far_slice(low_pair, i), "ty": ty, "tx": tx},
            device_id_type=MESH,
        )

    def partner_copy(owner):
        return pltpu.make_async_remote_copy(
            src_ref=term.at[owner],
            dst_ref=parts.at[0],
            send_sem=partner_send,
            recv_sem=partner_recv,
            device_id={"mode": owner, "ty": ty, "tx": tx},
            device_id_type=MESH,
        )

    def send_far(low_pair, i, pieces=(0, 1, 2, 3)):
        @pl.when(first if low_pair else last)
        def _():
            for q in pieces:
                collect_copy(low_pair, i, q).start()

    def send_partner(owner):
        @pl.when(mode == (owner ^ 1))
        def _():
            partner_copy(owner).start()

    def join(low_pair, i, pieces=(0, 1, 2, 3)):
        s = far_slice(low_pair, i)
        for q in pieces:
            collect_copy(low_pair, i, q).wait_recv()
            at = piece(q)
            joint[(i, *at)] = collected[(i, *at)] + term[(s, *at)]
            pair_sum_copy(low_pair, i, q).start()

    for s in reversed(range(SLICES)):

        def fetch(m):
            if s == SLICES - 1:
                return weight * far[0, rows(m)], weight * far[1, rows(m)]
            return pulled[0, rows(m)], pulled[1, rows(m)]

        def deliver(m, real, imag):
            if s == 0:
                pr, pi = probe[m, 0], probe[m, 1]
            else:
                pr, pi = psi[s - 1, 0, rows(m)], psi[s - 1, 1, rows(m)]
            tr, ti = pr * real + pi * imag, pr * imag - pi * real
            term[s, 0] = tr if m == 0 else term[s, 0] + tr
            term[s, 1] = ti if m == 0 else term[s, 1] + ti
            if s > 0:
                wr, wi = window[s, 0], window[s, 1]
                pulled[0, rows(m)] = wr * real + wi * imag
                pulled[1, rows(m)] = wr * imag - wi * real

        two_sided(mats, FAR_BACK if s == SLICES - 1 else STEP_BACK, fetch, deliver, mid)

        if s == 3:
            send_far(True, 0)
            send_partner(3)
        elif s == 2:
            send_far(True, 1)
        elif s == 1:
            send_partner(1)
            send_far(False, 0, (0, 1))
        else:
            send_far(False, 1)
            send_partner(0)
            send_far(False, 0, (2, 3))
            send_partner(2)

    for low_pair in (True, False):

        @pl.when(mode == (1 if low_pair else 2))
        def _():
            join(low_pair, 0, (0, 1))
            if low_pair:
                join(low_pair, 0, (2, 3))
                join(low_pair, 1)
            else:
                join(low_pair, 1)
                join(low_pair, 0, (2, 3))

    partner_copy(0).wait_recv()
    for q in range(4):
        pair_sum_copy(True, 0, q).wait_recv()
    for c in range(2):
        mine = term[mode, c]
        mine = mine + parts[0, c] + parts[1, c]
        tall = dot(twice(put_rows, 1), both(mine, 0))
        placed = dot(both(tall, 1), twice(pick_cols, 0))
        middle[c] = placed[HALF : 3 * HALF, :DET]
        for v in range(2):
            at = 3 * v * HALF
            vp[v, c] = placed[at : at + HALF, :DET]
            cp[v, LEFT, c], cp[v, RIGHT, c] = packed_sides(placed[at : at + HALF, DET:])
        hp[LEFT, c], hp[RIGHT, c] = packed_sides(placed[HALF : 3 * HALF, DET:])

    def grad_has(v, h):
        if v is None:
            return has[h]
        return has[UP + v] if h is None else jnp.logical_and(has[UP + v], has[h])

    def grad_copy(v, h):
        if v is None:
            src, dst, i = hp.at[h], gh.at[1 - h], h
        elif h is None:
            src, dst, i = vp.at[v], gv.at[1 - v], 2 + v
        else:
            src, dst, i = cp.at[v, h], gc.at[1 - v, 1 - h], 4 + 2 * v + h
        return pltpu.make_async_remote_copy(
            src_ref=src,
            dst_ref=dst,
            send_sem=grad_send.at[i],
            recv_sem=grad_recv.at[i],
            device_id={"mode": mode, "ty": ty if v is None else ty + 2 * v - 1, "tx": tx if h is None else tx + 2 * h - 1},
            device_id_type=MESH,
        )

    directions = [(None, 1), (0, 1), (1, 1), (None, 0), (0, 0), (1, 0), (0, None), (1, None)]
    for v, h in directions:

        @pl.when(grad_has(v, h))
        def _():
            grad_copy(v, h).start()

    for v, h in reversed(directions):
        @pl.when(grad_has(v, h))
        def _():
            grad_copy(v if v is None else 1 - v, h if h is None else 1 - h).wait_recv()

    for c in range(2):
        for v in range(2):
            half = slice(v * HALF, (v + 1) * HALF)
            sides = unpacked_halves(gh[LEFT, c], gh[RIGHT, c])[v]
            corners = jnp.concatenate(unpacked_halves(gc[v, LEFT, c], gc[v, RIGHT, c]), axis=0)
            out[0, c, half] = middle[c, half] + gv[v, c] + (sides + corners)

    for v, h in directions:

        @pl.when(grad_has(v, h))
        def _():
            grad_copy(v, h).wait_send()

    for kind in range(6):

        @pl.when(near(kind))
        def _():
            for s in range(SLICES):
                halo_copy(s, kind).wait_send()

    for kind in (LEFT, RIGHT):

        @pl.when(crossing[kind])
        def _():
            for s in range(SLICES):
                straight_copy(s, kind, 0).wait_send()
                straight_copy(s, kind, 1).wait_send()
                detour_copy(s, kind).wait_send()

        @pl.when(relaying[kind])
        def _():
            for s in range(SLICES):
                onward_copy(s, kind).wait_send()

    for step in range(1, modes):
        mode_copy(step).wait_send()

    partner_copy(0).wait_send()
    for i in range(2):
        for q in range(4):

            @pl.when(outer)
            def _():
                collect_copy(True, i, q).wait_send()

            @pl.when(inner)
            def _():
                pair_sum_copy(True, i, q).wait_send()


VMEM = pl.BlockSpec(memory_space=pltpu.VMEM)
SMEM = pl.BlockSpec(memory_space=pltpu.SMEM)
ANY = pl.BlockSpec(memory_space=pl.ANY)


def body(object_slices, probe_modes, positions, measured):
    mats = jnp.asarray(tables())
    modes = lax.axis_size("mode")
    dma = pltpu.SemaphoreType.DMA
    wave = (LOCAL * DET, DET)
    scratch = dict(
        obj=(SLICES, 2, DET, DET),
        probe=(LOCAL, 2, DET, DET),
        measured=(1, 1, 1, DET, DET),
        mats=(8, 2 * DET, 2 * DET),
        pk=(SLICES, 2, 2, HALF, DET),
        rs=(SLICES, 2, 2, HALF, DET),
        rl=(SLICES, HALF - EXTRA, DET),
        vt=(SLICES, 2, 2, HALF, DET),
        cr=(SLICES, 2, 2, 2, BLOCK, DET),
        ext=(2, 2 * DET, 2 * DET),
        window=(SLICES, 2, DET, DET),
        psi=(SLICES - 1, 2, *wave),
        far=(2, *wave),
        part=(DET, DET),
        others=(modes - 1, DET, DET),
        mid=(4 * DET, LOCAL * DET),
        pulled=(2, *wave),
        term=(SLICES, 2, DET, DET),
        collected=(2, 2, DET, DET),
        joint=(2, 2, DET, DET),
        parts=(2, 2, DET, DET),
        middle=(2, DET, DET),
        vp=(2, 2, HALF, DET),
        hp=(2, 2, HALF, DET),
        cp=(2, 2, 2, BLOCK, DET),
        gv=(2, 2, HALF, DET),
        gh=(2, 2, HALF, DET),
        gc=(2, 2, 2, BLOCK, DET),
    )
    return pl.pallas_call(
        kernel,
        out_shape=jax.ShapeDtypeStruct((1, 2, DET, DET), F32),
        in_specs=[SMEM, ANY, ANY, ANY, ANY],
        out_specs=VMEM,
        scratch_shapes=[pltpu.VMEM(shape, BF16 if name in ("mid", "mats") else F32) for name, shape in scratch.items()]
        + [dma((3 + SLICES,))]
        + [dma((SLICES, 6)), dma((SLICES, 6))]
        + [dma((SLICES, 3)), dma((SLICES, 3)), dma((SLICES,)), dma((SLICES,))]
        + [dma((modes - 1,)), dma((modes - 1,))]
        + [dma((2, 4)), dma((2, 4)), dma((2, 4)), dma((4,)), dma, dma]
        + [dma((8,)), dma((8,))],
        compiler_params=pltpu.CompilerParams(collective_id=0, has_side_effects=True),
        name="ptycho",
    )(positions.reshape(2), object_slices, probe_modes, measured, mats)


def solution(mesh):
    return jax.shard_map(
        body,
        mesh=mesh,
        in_specs=(
            P(None, None, "ty", "tx"),
            P("mode", None, None, None),
            P("ty", "tx", None, None),
            P("ty", "tx", None, None, None),
        ),
        out_specs=P("mode", None, "ty", "tx"),
        check_vma=False,
    )
```

```python
import functools

import numpy as np
import jax
import jax.numpy as jnp
from jax import lax
from jax.experimental import pallas as pl
from jax.experimental.pallas import tpu as pltpu
from jax.sharding import PartitionSpec as P

DET = 128
SLICES = 4
MARGIN = 64
LOCAL = 4
RATE = 0.3
F32 = jnp.float32
BF16 = jnp.bfloat16


def real_block(matrix):
    return np.block([[matrix.real, matrix.imag], [-matrix.imag, matrix.real]])


def tables():
    counter = np.arange(DET)
    fourier = np.exp(-2j * np.pi * (np.outer(counter, counter) % DET) / DET) / np.sqrt(DET)
    frequency = np.where(counter < DET // 2, counter, counter - DET).astype(np.float64)
    chirp = np.exp(-1j * RATE * frequency**2 / DET)
    step = fourier.conj() @ (chirp[:, None] * fourier)
    step = (step + step.T) / 2
    out = []
    for matrix in (step, step.conj(), fourier, fourier.conj()):
        block = real_block(matrix).astype(np.float32)
        high = block.astype(jnp.bfloat16)
        low = (block - high.astype(np.float32)).astype(jnp.bfloat16)
        out += [high, low]
    return np.stack(out)


STEP, STEP_BACK, FAR, FAR_BACK = range(4)
CONJ = {STEP: STEP_BACK, STEP_BACK: STEP, FAR: FAR_BACK, FAR_BACK: FAR}


def halves(x):
    high = x.astype(BF16)
    return high, (x - high.astype(F32)).astype(BF16)


def rows(m):
    return slice(m * DET, (m + 1) * DET)


def right_product(mats, which, real, imag):
    rh, rl = halves(real)
    ih, il = halves(imag)
    lhs = jnp.concatenate([rh, ih, rl, il, rh, ih], axis=1)
    high, low = mats[2 * which], mats[2 * which + 1]
    rhs = jnp.concatenate([high, high, low], axis=0)
    return jnp.dot(lhs, rhs, preferred_element_type=F32)


def left_product(mats, which, stacked):
    conj = CONJ[which]
    high, low = mats[2 * conj], mats[2 * conj + 1]
    main = jnp.dot(jnp.concatenate([high, low], axis=0), stacked[: 2 * DET], preferred_element_type=F32)
    rest = jnp.dot(high, stacked[2 * DET :], preferred_element_type=F32)
    return main[: 2 * DET] + main[2 * DET :] + rest


def two_sided(mats, which, fetch, deliver, mid):
    for m in range(LOCAL):
        real, imag = fetch(m)
        out = right_product(mats, which, real, imag)
        rh, rl = halves(out[:, :DET])
        ih, il = halves(out[:, DET:])
        for part, value in enumerate((rh, ih, rl, il)):
            mid[rows(part), rows(m)] = value
    for pair in range(LOCAL // 2):
        out = left_product(mats, which, mid[:, pair * 2 * DET : (pair + 1) * 2 * DET])
        for k in range(2):
            deliver(2 * pair + k, out[:DET, rows(k)], out[DET:, rows(k)])

MESH = pl.DeviceIdType.MESH
HALF = DET // 2
BLOCK = HALF // 2
EXTRA = 16
STRAIGHT = ((0, slice(0, HALF)), (1, slice(0, EXTRA)))


def lane_low(shape):
    return lax.broadcasted_iota(jnp.int32, shape, len(shape) - 1) < HALF


def turned(x):
    return pltpu.roll(x, HALF, x.ndim - 1)


def packed_edges(strip):
    first, second = strip[:BLOCK], strip[BLOCK:]
    low = lane_low(first.shape)
    left_edge = jnp.where(low, first, turned(second))
    right_edge = jnp.where(low, turned(first), second)
    return left_edge, right_edge


def unpacked_sides(from_left, from_right):
    low = lane_low(from_left.shape)
    first = jnp.where(low, from_right, turned(from_left))
    second = jnp.where(low, turned(from_right), from_left)
    return first, second


def packed_sides(strip):
    half = strip.shape[0] // 2
    upper, lower = strip[:half], strip[half:]
    low = lane_low(upper.shape)
    return jnp.where(low, turned(upper), lower), jnp.where(low, upper, turned(lower))


def unpacked_halves(from_left, from_right):
    low = lane_low(from_left.shape)
    return jnp.where(low, from_left, turned(from_right)), jnp.where(low, turned(from_left), from_right)


LEFT, RIGHT, UP, DOWN, UP_CORNER, DOWN_CORNER = range(6)


def kernel(
    pos_ref, obj_in, probe_in, measured_in, mats_in, out,
    obj, probe, measured, mats, pk, rs, rl, vt, cr, ext, window, psi, far, part, others, mid, pulled, term, collected, joint, parts, middle, vp, hp, cp, gv, gh, gc,
    load, halo_send, halo_recv, cross_send, cross_recv, relay_send, relay_recv, mode_send, mode_recv, collect_send, collect_recv, joint_send, joint_recv, partner_send, partner_recv, grad_send, grad_recv,
):
    mode, ty, tx = lax.axis_index("mode"), lax.axis_index("ty"), lax.axis_index("tx")
    modes, tys, txs = lax.axis_size("mode"), lax.axis_size("ty"), lax.axis_size("tx")
    has = {LEFT: tx > 0, RIGHT: tx < txs - 1, UP: ty > 0, DOWN: ty < tys - 1}
    has[UP_CORNER], has[DOWN_CORNER] = has[UP], has[DOWN]
    cross_right, cross_left = tx == txs // 2 - 1, tx == txs // 2
    mirror = modes - 1 - mode
    left_mode = jnp.where(cross_left, mirror, mode)
    right_mode = jnp.where(cross_right, mirror, mode)
    target = {
        LEFT: {"mode": left_mode, "ty": ty, "tx": tx - 1},
        RIGHT: {"mode": right_mode, "ty": ty, "tx": tx + 1},
        UP: {"mode": mode, "ty": ty - 1, "tx": tx},
        DOWN: {"mode": mode, "ty": ty + 1, "tx": tx},
    }
    crossing = {LEFT: cross_left, RIGHT: cross_right}
    relay_tx = {LEFT: txs - 1, RIGHT: 0}
    relaying = {LEFT: tx == relay_tx[LEFT], RIGHT: tx == relay_tx[RIGHT]}
    landing_tx = {LEFT: txs // 2 - 1, RIGHT: txs // 2}
    direct = {LEFT: {"mode": mode, "ty": ty, "tx": tx - 1}, RIGHT: {"mode": mode, "ty": ty, "tx": tx + 1}}

    def peer(step):
        return {"mode": lax.rem(mode + step, modes), "ty": ty, "tx": tx}

    barrier = pltpu.get_barrier_semaphore()
    count = jnp.int32(modes - 1)
    for side in (LEFT, RIGHT, UP, DOWN):
        count = count + has[side].astype(jnp.int32)

        @pl.when(has[side])
        def _():
            pl.semaphore_signal(barrier, inc=1, device_id=target[side], device_id_type=MESH)

    for side, cross in ((LEFT, cross_left), (RIGHT, cross_right)):
        far_pair = jnp.logical_and(cross, has[side])
        count = count + far_pair.astype(jnp.int32)

        @pl.when(far_pair)
        def _():
            pl.semaphore_signal(barrier, inc=1, device_id=direct[side], device_id_type=MESH)

    for side in (LEFT, RIGHT):
        from_relay, from_landing = crossing[side], relaying[side]
        count = count + from_relay.astype(jnp.int32) + from_landing.astype(jnp.int32)

        @pl.when(relaying[side])
        def _():
            sender = {"mode": mode, "ty": ty, "tx": landing_tx[1 - side]}
            pl.semaphore_signal(barrier, inc=1, device_id=sender, device_id_type=MESH)

        @pl.when(tx == landing_tx[side])
        def _():
            relay = {"mode": mirror, "ty": ty, "tx": relay_tx[side]}
            pl.semaphore_signal(barrier, inc=1, device_id=relay, device_id_type=MESH)

    for step in range(1, modes):
        pl.semaphore_signal(barrier, inc=1, device_id=peer(step), device_id_type=MESH)
    object_loads = [pltpu.make_async_copy(obj_in.at[s], obj.at[s], load.at[3 + s]) for s in range(SLICES)]
    loads = [pltpu.make_async_copy(src, dst, load.at[i]) for i, (src, dst) in enumerate(((probe_in, probe), (mats_in, mats), (measured_in, measured)))]
    for copy in object_loads + loads:
        copy.start()

    for side in (LEFT, RIGHT):

        @pl.when(jnp.logical_not(has[side]))
        def _():
            rs[:, side] = jnp.zeros_like(rs[:, side])
            gh[side] = jnp.zeros_like(gh[side])
            gc[:, side] = jnp.zeros_like(gc[:, side])

    for side in (UP, DOWN):

        @pl.when(jnp.logical_not(has[side]))
        def _():
            vt[:, side - UP] = jnp.zeros_like(vt[:, side - UP])
            cr[:, side - UP] = jnp.zeros_like(cr[:, side - UP])
            gv[side - UP] = jnp.zeros_like(gv[side - UP])
            gc[side - UP] = jnp.zeros_like(gc[side - UP])

    def pack(s):
        object_loads[s].wait()
        for c in range(2):
            for b in range(2):
                left_edge, right_edge = packed_edges(obj[s, c, b * HALF : (b + 1) * HALF])
                pk[s, LEFT, c, b * BLOCK : (b + 1) * BLOCK] = left_edge
                pk[s, RIGHT, c, b * BLOCK : (b + 1) * BLOCK] = right_edge

    pack(0)
    pl.semaphore_wait(barrier, count)

    opposite = {LEFT: RIGHT, RIGHT: LEFT, UP: DOWN, DOWN: UP, UP_CORNER: DOWN_CORNER, DOWN_CORNER: UP_CORNER}

    def landing(s, kind):
        if kind in (LEFT, RIGHT):
            return rs.at[s, kind]
        if kind in (UP, DOWN):
            return vt.at[s, kind - UP]
        return cr.at[s, kind - UP_CORNER]

    def source(s, kind):
        if kind in (LEFT, RIGHT):
            return pk.at[s, kind]
        if kind in (UP, DOWN):
            return obj.at[s, :, (kind - UP) * HALF : (kind - UP + 1) * HALF]
        return rs.at[s, :, :, (kind - UP_CORNER) * BLOCK : (kind - UP_CORNER + 1) * BLOCK]

    def halo_copy(s, kind):
        return pltpu.make_async_remote_copy(
            src_ref=source(s, kind),
            dst_ref=landing(s, opposite[kind]),
            send_sem=halo_send.at[s, kind],
            recv_sem=halo_recv.at[s, opposite[kind]],
            device_id=target[kind if kind < UP_CORNER else kind - 2],
            device_id_type=MESH,
        )

    def straight_copy(s, kind, i):
        return pltpu.make_async_remote_copy(
            src_ref=pk.at[(s, kind, *STRAIGHT[i])],
            dst_ref=rs.at[(s, opposite[kind], *STRAIGHT[i])],
            send_sem=cross_send.at[s, 2 * i],
            recv_sem=cross_recv.at[s, 2 * i],
            device_id=target[kind],
            device_id_type=MESH,
        )

    def detour_copy(s, kind):
        return pltpu.make_async_remote_copy(
            src_ref=pk.at[s, kind, 1, EXTRA:],
            dst_ref=rl.at[s],
            send_sem=cross_send.at[s, 1],
            recv_sem=relay_recv.at[s],
            device_id={"mode": mode, "ty": ty, "tx": relay_tx[kind]},
            device_id_type=MESH,
        )

    def onward_copy(s, kind):
        return pltpu.make_async_remote_copy(
            src_ref=rl.at[s],
            dst_ref=rs.at[s, opposite[kind], 1, EXTRA:],
            send_sem=relay_send.at[s],
            recv_sem=cross_recv.at[s, 1],
            device_id={"mode": mirror, "ty": ty, "tx": landing_tx[kind]},
            device_id_type=MESH,
        )

    def near(kind):
        return jnp.logical_and(has[kind], jnp.logical_not(crossing[kind])) if kind in crossing else has[kind]

    def start_halo(s, kind):
        @pl.when(near(kind))
        def _():
            halo_copy(s, kind).start()

        if kind in crossing:

            @pl.when(crossing[kind])
            def _():
                straight_copy(s, kind, 0).start()
                straight_copy(s, kind, 1).start()
                detour_copy(s, kind).start()

    def await_halo(s, kind):
        @pl.when(near(kind))
        def _():
            halo_copy(s, opposite[kind]).wait_recv()

        if kind in crossing:

            @pl.when(crossing[kind])
            def _():
                straight_copy(s, opposite[kind], 0).wait_recv()
                straight_copy(s, opposite[kind], 1).wait_recv()
                onward_copy(s, opposite[kind]).wait_recv()

    def relay(s):
        for kind in (LEFT, RIGHT):

            @pl.when(relaying[kind])
            def _():
                detour_copy(s, kind).wait_recv()
                onward_copy(s, kind).start()

    for s in range(SLICES):
        if s + 1 < SLICES:
            pack(s + 1)
        for kind in (RIGHT, LEFT, UP, DOWN):
            start_halo(s, kind)

    def relay_corners(s):
        await_halo(s, LEFT)
        await_halo(s, RIGHT)
        start_halo(s, UP_CORNER)
        start_halo(s, DOWN_CORNER)

    row, col = pos_ref[0], pos_ref[1]
    here, there = (lax.broadcasted_iota(jnp.int32, (DET, 2 * DET), d) for d in range(2))
    pick_rows = jnp.where(there == here + row, 1.0, 0.0).astype(BF16)
    offset = here + (col + 2 * DET - HALF)
    offset = jnp.where(offset >= 2 * DET, offset - 2 * DET, offset)
    pick_cols = jnp.where(there == offset, 1.0, 0.0).astype(BF16)
    here, there = (lax.broadcasted_iota(jnp.int32, (2 * DET, DET), d) for d in range(2))
    put_rows = jnp.where(here == there + row, 1.0, 0.0).astype(BF16)
    offset = there + (col + 2 * DET - HALF)
    offset = jnp.where(offset >= 2 * DET, offset - 2 * DET, offset)
    put_cols = jnp.where(here == offset, 1.0, 0.0).astype(BF16)

    def twice(x, axis):
        return jnp.concatenate([x, x], axis=axis)

    def both(x, axis):
        return jnp.concatenate(halves(x), axis=axis)

    def dot(x, y):
        return jnp.dot(x, y, preferred_element_type=F32)

    def build_window(s):
        for kind in (UP, DOWN, UP_CORNER, DOWN_CORNER):
            await_halo(s, kind)
        for c in range(2):
            for side in range(2):
                at = side * 3 * HALF
                ext[c, at : at + HALF, :DET] = vt[s, side, c]
                first, second = unpacked_sides(cr[s, side, LEFT, c], cr[s, side, RIGHT, c])
                ext[c, at : at + BLOCK, DET:] = first
                ext[c, at + BLOCK : at + HALF, DET:] = second
            ext[c, HALF : 3 * HALF, :DET] = obj[s, c]
            for b in range(2):
                block = slice(b * BLOCK, (b + 1) * BLOCK)
                first, second = unpacked_sides(rs[s, LEFT, c, block], rs[s, RIGHT, c, block])
                at = HALF + b * HALF
                ext[c, at : at + BLOCK, DET:] = first
                ext[c, at + BLOCK : at + HALF, DET:] = second
            band = dot(twice(pick_rows, 1), both(ext[c], 0))
            window[s, c] = dot(both(band, 1), twice(put_cols, 0))

    relay(0)
    relay_corners(0)
    for s in range(SLICES):
        if s + 1 < SLICES:
            relay_corners(s + 1)
        if s == 0:
            for ahead in range(1, SLICES):
                relay(ahead)
        build_window(s)
        if s == 0:
            for copy in loads:
                copy.wait()

        def fetch(m):
            if s == 0:
                real, imag = probe[m, 0], probe[m, 1]
            else:
                real, imag = psi[s - 1, 0, rows(m)], psi[s - 1, 1, rows(m)]
            wr, wi = window[s, 0], window[s, 1]
            return real * wr - imag * wi, real * wi + imag * wr

        def deliver(m, real, imag):
            if s + 1 < SLICES:
                psi[s, 0, rows(m)] = real
                psi[s, 1, rows(m)] = imag
            else:
                far[0, rows(m)] = real
                far[1, rows(m)] = imag
                power = real * real + imag * imag
                part[...] = power if m == 0 else part[...] + power

        two_sided(mats, STEP if s + 1 < SLICES else FAR, fetch, deliver, mid)

    first, last = mode == 0, mode == modes - 1
    inner, lower = jnp.logical_not(jnp.logical_or(first, last)), mode < modes // 2

    def mode_copy(step):
        return pltpu.make_async_remote_copy(
            src_ref=part,
            dst_ref=others.at[step - 1],
            send_sem=mode_send.at[step - 1],
            recv_sem=mode_recv.at[step - 1],
            device_id=peer(step),
            device_id_type=MESH,
        )

    for step in range(1, modes):
        mode_copy(step).start()
    whole = part[...]
    for step in range(1, modes):
        mode_copy(step).wait_recv()
        whole = whole + others[step - 1]
    weight = 1.0 - measured[0, 0, 0] / jnp.maximum(jnp.sqrt(whole), 1.0)

    outer, collector = jnp.logical_or(first, last), jnp.where(lower, 1, 2)

    def far_slice(low_pair, i):
        return SLICES - 1 - i if low_pair else 1 - i

    def piece(q):
        return q // 2, pl.ds(q % 2 * HALF, HALF)

    def collect_copy(low_pair, i, q):
        return pltpu.make_async_remote_copy(
            src_ref=term.at[(far_slice(low_pair, i), *piece(q))],
            dst_ref=collected.at[(i, *piece(q))],
            send_sem=collect_send.at[i, q],
            recv_sem=collect_recv.at[i, q],
            device_id={"mode": collector, "ty": ty, "tx": tx},
            device_id_type=MESH,
        )

    def pair_sum_copy(low_pair, i, q):
        return pltpu.make_async_remote_copy(
            src_ref=joint.at[(i, *piece(q))],
            dst_ref=parts.at[(1, *piece(q))],
            send_sem=joint_send.at[i, q],
            recv_sem=joint_recv.at[q],
            device_id={"mode": far_slice(low_pair, i), "ty": ty, "tx": tx},
            device_id_type=MESH,
        )

    def partner_copy(owner, c):
        return pltpu.make_async_remote_copy(
            src_ref=term.at[owner, c],
            dst_ref=parts.at[0, c],
            send_sem=partner_send.at[c],
            recv_sem=partner_recv.at[c],
            device_id={"mode": owner, "ty": ty, "tx": tx},
            device_id_type=MESH,
        )

    def send_far(low_pair, i, pieces=(0, 1, 2, 3)):
        @pl.when(first if low_pair else last)
        def _():
            for q in pieces:
                collect_copy(low_pair, i, q).start()

    def send_partner(owner):
        @pl.when(mode == (owner ^ 1))
        def _():
            for c in range(2):
                partner_copy(owner, c).start()

    def join(low_pair, i, pieces=(0, 1, 2, 3)):
        s = far_slice(low_pair, i)
        for q in pieces:
            collect_copy(low_pair, i, q).wait_recv()
            at = piece(q)
            joint[(i, *at)] = collected[(i, *at)] + term[(s, *at)]
            pair_sum_copy(low_pair, i, q).start()

    for s in reversed(range(SLICES)):

        def fetch(m):
            if s == SLICES - 1:
                return weight * far[0, rows(m)], weight * far[1, rows(m)]
            return pulled[0, rows(m)], pulled[1, rows(m)]

        def deliver(m, real, imag):
            if s == 0:
                pr, pi = probe[m, 0], probe[m, 1]
            else:
                pr, pi = psi[s - 1, 0, rows(m)], psi[s - 1, 1, rows(m)]
            tr, ti = pr * real + pi * imag, pr * imag - pi * real
            term[s, 0] = tr if m == 0 else term[s, 0] + tr
            term[s, 1] = ti if m == 0 else term[s, 1] + ti
            if s > 0:
                wr, wi = window[s, 0], window[s, 1]
                pulled[0, rows(m)] = wr * real + wi * imag
                pulled[1, rows(m)] = wr * imag - wi * real

        two_sided(mats, FAR_BACK if s == SLICES - 1 else STEP_BACK, fetch, deliver, mid)

        if s == 3:
            send_far(True, 0)
            send_partner(3)
        elif s == 2:
            send_far(True, 1)
        elif s == 1:
            send_partner(1)
            send_far(False, 0, (0, 1))
        else:
            send_far(False, 1)
            send_partner(0)
            send_far(False, 0, (2, 3))
            send_partner(2)

    for low_pair in (True, False):

        @pl.when(mode == (1 if low_pair else 2))
        def _():
            join(low_pair, 0, (0, 1))
            if low_pair:
                join(low_pair, 0, (2, 3))
                join(low_pair, 1)
            else:
                join(low_pair, 1)
                join(low_pair, 0, (2, 3))

    def place(c):
        partner_copy(0, c).wait_recv()
        for q in range(2 * c, 2 * c + 2):
            pair_sum_copy(True, 0, q).wait_recv()
        mine = term[mode, c] + parts[0, c] + parts[1, c]
        tall = dot(twice(put_rows, 1), both(mine, 0))
        placed = dot(both(tall, 1), twice(pick_cols, 0))
        middle[c] = placed[HALF : 3 * HALF, :DET]
        for v in range(2):
            at = 3 * v * HALF
            vp[v, c] = placed[at : at + HALF, :DET]
            cp[v, LEFT, c], cp[v, RIGHT, c] = packed_sides(placed[at : at + HALF, DET:])
        hp[LEFT, c], hp[RIGHT, c] = packed_sides(placed[HALF : 3 * HALF, DET:])

    def grad_has(v, h):
        if v is None:
            return has[h]
        return has[UP + v] if h is None else jnp.logical_and(has[UP + v], has[h])

    def grad_copy(v, h, c):
        if v is None:
            src, dst, i = hp.at[h, c], gh.at[1 - h, c], h
        elif h is None:
            src, dst, i = vp.at[v, c], gv.at[1 - v, c], 2 + v
        else:
            src, dst, i = cp.at[v, h, c], gc.at[1 - v, 1 - h, c], 4 + 2 * v + h
        return pltpu.make_async_remote_copy(
            src_ref=src,
            dst_ref=dst,
            send_sem=grad_send.at[i, c],
            recv_sem=grad_recv.at[i, c],
            device_id={"mode": mode, "ty": ty if v is None else ty + 2 * v - 1, "tx": tx if h is None else tx + 2 * h - 1},
            device_id_type=MESH,
        )

    directions = [(None, 1), (0, 1), (1, 1), (None, 0), (0, 0), (1, 0), (0, None), (1, None)]
    for c in range(2):
        place(c)
        for v, h in directions:

            @pl.when(grad_has(v, h))
            def _():
                grad_copy(v, h, c).start()

    for v, h in reversed(directions):
        @pl.when(grad_has(v, h))
        def _():
            for c in range(2):
                grad_copy(v if v is None else 1 - v, h if h is None else 1 - h, c).wait_recv()

    for c in range(2):
        for v in range(2):
            half = slice(v * HALF, (v + 1) * HALF)
            sides = unpacked_halves(gh[LEFT, c], gh[RIGHT, c])[v]
            corners = jnp.concatenate(unpacked_halves(gc[v, LEFT, c], gc[v, RIGHT, c]), axis=0)
            out[0, c, half] = middle[c, half] + gv[v, c] + (sides + corners)

    for v, h in directions:

        @pl.when(grad_has(v, h))
        def _():
            for c in range(2):
                grad_copy(v, h, c).wait_send()

    for kind in range(6):

        @pl.when(near(kind))
        def _():
            for s in range(SLICES):
                halo_copy(s, kind).wait_send()

    for kind in (LEFT, RIGHT):

        @pl.when(crossing[kind])
        def _():
            for s in range(SLICES):
                straight_copy(s, kind, 0).wait_send()
                straight_copy(s, kind, 1).wait_send()
                detour_copy(s, kind).wait_send()

        @pl.when(relaying[kind])
        def _():
            for s in range(SLICES):
                onward_copy(s, kind).wait_send()

    for step in range(1, modes):
        mode_copy(step).wait_send()

    for c in range(2):
        partner_copy(0, c).wait_send()
    for i in range(2):
        for q in range(4):

            @pl.when(outer)
            def _():
                collect_copy(True, i, q).wait_send()

            @pl.when(inner)
            def _():
                pair_sum_copy(True, i, q).wait_send()


VMEM = pl.BlockSpec(memory_space=pltpu.VMEM)
SMEM = pl.BlockSpec(memory_space=pltpu.SMEM)
ANY = pl.BlockSpec(memory_space=pl.ANY)


def body(object_slices, probe_modes, positions, measured):
    mats = jnp.asarray(tables())
    modes = lax.axis_size("mode")
    dma = pltpu.SemaphoreType.DMA
    wave = (LOCAL * DET, DET)
    scratch = dict(
        obj=(SLICES, 2, DET, DET),
        probe=(LOCAL, 2, DET, DET),
        measured=(1, 1, 1, DET, DET),
        mats=(8, 2 * DET, 2 * DET),
        pk=(SLICES, 2, 2, HALF, DET),
        rs=(SLICES, 2, 2, HALF, DET),
        rl=(SLICES, HALF - EXTRA, DET),
        vt=(SLICES, 2, 2, HALF, DET),
        cr=(SLICES, 2, 2, 2, BLOCK, DET),
        ext=(2, 2 * DET, 2 * DET),
        window=(SLICES, 2, DET, DET),
        psi=(SLICES - 1, 2, *wave),
        far=(2, *wave),
        part=(DET, DET),
        others=(modes - 1, DET, DET),
        mid=(4 * DET, LOCAL * DET),
        pulled=(2, *wave),
        term=(SLICES, 2, DET, DET),
        collected=(2, 2, DET, DET),
        joint=(2, 2, DET, DET),
        parts=(2, 2, DET, DET),
        middle=(2, DET, DET),
        vp=(2, 2, HALF, DET),
        hp=(2, 2, HALF, DET),
        cp=(2, 2, 2, BLOCK, DET),
        gv=(2, 2, HALF, DET),
        gh=(2, 2, HALF, DET),
        gc=(2, 2, 2, BLOCK, DET),
    )
    return pl.pallas_call(
        kernel,
        out_shape=jax.ShapeDtypeStruct((1, 2, DET, DET), F32),
        in_specs=[SMEM, ANY, ANY, ANY, ANY],
        out_specs=VMEM,
        scratch_shapes=[pltpu.VMEM(shape, BF16 if name in ("mid", "mats") else F32) for name, shape in scratch.items()]
        + [dma((3 + SLICES,))]
        + [dma((SLICES, 6)), dma((SLICES, 6))]
        + [dma((SLICES, 3)), dma((SLICES, 3)), dma((SLICES,)), dma((SLICES,))]
        + [dma((modes - 1,)), dma((modes - 1,))]
        + [dma((2, 4)), dma((2, 4)), dma((2, 4)), dma((4,)), dma((2,)), dma((2,))]
        + [dma((8, 2)), dma((8, 2))],
        compiler_params=pltpu.CompilerParams(collective_id=0, has_side_effects=True),
        name="ptycho",
    )(positions.reshape(2), object_slices, probe_modes, measured, mats)


def solution(mesh):
    return jax.shard_map(
        body,
        mesh=mesh,
        in_specs=(
            P(None, None, "ty", "tx"),
            P("mode", None, None, None),
            P("ty", "tx", None, None),
            P("ty", "tx", None, None, None),
        ),
        out_specs=P("mode", None, "ty", "tx"),
        check_vma=False,
    )
```

```python
import functools

import numpy as np
import jax
import jax.numpy as jnp
from jax import lax
from jax.experimental import pallas as pl
from jax.experimental.pallas import tpu as pltpu
from jax.sharding import PartitionSpec as P

DET = 128
SLICES = 4
MARGIN = 64
LOCAL = 4
RATE = 0.3
F32 = jnp.float32
BF16 = jnp.bfloat16


def real_block(matrix):
    return np.block([[matrix.real, matrix.imag], [-matrix.imag, matrix.real]])


def tables():
    counter = np.arange(DET)
    fourier = np.exp(-2j * np.pi * (np.outer(counter, counter) % DET) / DET) / np.sqrt(DET)
    frequency = np.where(counter < DET // 2, counter, counter - DET).astype(np.float64)
    chirp = np.exp(-1j * RATE * frequency**2 / DET)
    step = fourier.conj() @ (chirp[:, None] * fourier)
    step = (step + step.T) / 2
    out = []
    for matrix in (step, step.conj(), fourier, fourier.conj()):
        block = real_block(matrix).astype(np.float32)
        high = block.astype(jnp.bfloat16)
        low = (block - high.astype(np.float32)).astype(jnp.bfloat16)
        out += [high, low]
    return np.stack(out)


STEP, STEP_BACK, FAR, FAR_BACK = range(4)
CONJ = {STEP: STEP_BACK, STEP_BACK: STEP, FAR: FAR_BACK, FAR_BACK: FAR}


def halves(x):
    high = x.astype(BF16)
    return high, (x - high.astype(F32)).astype(BF16)


def rows(m):
    return slice(m * DET, (m + 1) * DET)


def right_product(mats, which, real, imag):
    rh, rl = halves(real)
    ih, il = halves(imag)
    lhs = jnp.concatenate([rh, ih, rl, il, rh, ih], axis=1)
    high, low = mats[2 * which], mats[2 * which + 1]
    rhs = jnp.concatenate([high, high, low], axis=0)
    return jnp.dot(lhs, rhs, preferred_element_type=F32)


def left_product(mats, which, stacked):
    conj = CONJ[which]
    high, low = mats[2 * conj], mats[2 * conj + 1]
    main = jnp.dot(jnp.concatenate([high, low], axis=0), stacked[: 2 * DET], preferred_element_type=F32)
    rest = jnp.dot(high, stacked[2 * DET :], preferred_element_type=F32)
    return main[: 2 * DET] + main[2 * DET :] + rest


def two_sided(mats, which, fetch, deliver, mid):
    for m in range(LOCAL):
        real, imag = fetch(m)
        out = right_product(mats, which, real, imag)
        rh, rl = halves(out[:, :DET])
        ih, il = halves(out[:, DET:])
        for part, value in enumerate((rh, ih, rl, il)):
            mid[rows(part), rows(m)] = value
    for pair in range(LOCAL // 2):
        out = left_product(mats, which, mid[:, pair * 2 * DET : (pair + 1) * 2 * DET])
        for k in range(2):
            deliver(2 * pair + k, out[:DET, rows(k)], out[DET:, rows(k)])

MESH = pl.DeviceIdType.MESH
HALF = DET // 2
BLOCK = HALF // 2
EXTRA = 16
STRAIGHT = ((0, slice(0, HALF)), (1, slice(0, EXTRA)))


def lane_low(shape):
    return lax.broadcasted_iota(jnp.int32, shape, len(shape) - 1) < HALF


def turned(x):
    return pltpu.roll(x, HALF, x.ndim - 1)


def packed_edges(strip):
    first, second = strip[:BLOCK], strip[BLOCK:]
    low = lane_low(first.shape)
    left_edge = jnp.where(low, first, turned(second))
    right_edge = jnp.where(low, turned(first), second)
    return left_edge, right_edge


def unpacked_sides(from_left, from_right):
    low = lane_low(from_left.shape)
    first = jnp.where(low, from_right, turned(from_left))
    second = jnp.where(low, turned(from_right), from_left)
    return first, second


def packed_sides(strip):
    half = strip.shape[0] // 2
    upper, lower = strip[:half], strip[half:]
    low = lane_low(upper.shape)
    return jnp.where(low, turned(upper), lower), jnp.where(low, upper, turned(lower))


def unpacked_halves(from_left, from_right):
    low = lane_low(from_left.shape)
    return jnp.where(low, from_left, turned(from_right)), jnp.where(low, turned(from_left), from_right)


LEFT, RIGHT, UP, DOWN, UP_CORNER, DOWN_CORNER = range(6)


def kernel(
    pos_ref, obj_in, probe_in, measured_in, mats_in, out,
    obj, probe, measured, mats, pk, rs, rl, vt, cr, ext, window, psi, far, part, others, mid, pulled, term, collected, joint, parts, middle, vp, hp, cp, gv, gh, gc,
    load, halo_send, halo_recv, cross_send, cross_recv, relay_send, relay_recv, mode_send, mode_recv, collect_send, collect_recv, joint_send, joint_recv, partner_send, partner_recv, grad_send, grad_recv,
):
    mode, ty, tx = lax.axis_index("mode"), lax.axis_index("ty"), lax.axis_index("tx")
    modes, tys, txs = lax.axis_size("mode"), lax.axis_size("ty"), lax.axis_size("tx")
    has = {LEFT: tx > 0, RIGHT: tx < txs - 1, UP: ty > 0, DOWN: ty < tys - 1}
    has[UP_CORNER], has[DOWN_CORNER] = has[UP], has[DOWN]
    cross_right, cross_left = tx == txs // 2 - 1, tx == txs // 2
    mirror = modes - 1 - mode
    left_mode = jnp.where(cross_left, mirror, mode)
    right_mode = jnp.where(cross_right, mirror, mode)
    target = {
        LEFT: {"mode": left_mode, "ty": ty, "tx": tx - 1},
        RIGHT: {"mode": right_mode, "ty": ty, "tx": tx + 1},
        UP: {"mode": mode, "ty": ty - 1, "tx": tx},
        DOWN: {"mode": mode, "ty": ty + 1, "tx": tx},
    }
    crossing = {LEFT: cross_left, RIGHT: cross_right}
    relay_tx = {LEFT: txs - 1, RIGHT: 0}
    relaying = {LEFT: tx == relay_tx[LEFT], RIGHT: tx == relay_tx[RIGHT]}
    landing_tx = {LEFT: txs // 2 - 1, RIGHT: txs // 2}
    direct = {LEFT: {"mode": mode, "ty": ty, "tx": tx - 1}, RIGHT: {"mode": mode, "ty": ty, "tx": tx + 1}}

    def peer(step):
        return {"mode": lax.rem(mode + step, modes), "ty": ty, "tx": tx}

    barrier = pltpu.get_barrier_semaphore()
    count = jnp.int32(modes - 1)
    for side in (LEFT, RIGHT, UP, DOWN):
        count = count + has[side].astype(jnp.int32)

        @pl.when(has[side])
        def _():
            pl.semaphore_signal(barrier, inc=1, device_id=target[side], device_id_type=MESH)

    for side, cross in ((LEFT, cross_left), (RIGHT, cross_right)):
        far_pair = jnp.logical_and(cross, has[side])
        count = count + far_pair.astype(jnp.int32)

        @pl.when(far_pair)
        def _():
            pl.semaphore_signal(barrier, inc=1, device_id=direct[side], device_id_type=MESH)

    for side in (LEFT, RIGHT):
        from_relay, from_landing = crossing[side], relaying[side]
        count = count + from_relay.astype(jnp.int32) + from_landing.astype(jnp.int32)

        @pl.when(relaying[side])
        def _():
            sender = {"mode": mode, "ty": ty, "tx": landing_tx[1 - side]}
            pl.semaphore_signal(barrier, inc=1, device_id=sender, device_id_type=MESH)

        @pl.when(tx == landing_tx[side])
        def _():
            relay = {"mode": mirror, "ty": ty, "tx": relay_tx[side]}
            pl.semaphore_signal(barrier, inc=1, device_id=relay, device_id_type=MESH)

    for step in range(1, modes):
        pl.semaphore_signal(barrier, inc=1, device_id=peer(step), device_id_type=MESH)
    object_loads = [pltpu.make_async_copy(obj_in.at[s], obj.at[s], load.at[3 + s]) for s in range(SLICES)]
    loads = [pltpu.make_async_copy(src, dst, load.at[i]) for i, (src, dst) in enumerate(((probe_in, probe), (mats_in, mats), (measured_in, measured)))]
    for copy in object_loads + loads:
        copy.start()

    for side in (LEFT, RIGHT):

        @pl.when(jnp.logical_not(has[side]))
        def _():
            rs[:, side] = jnp.zeros_like(rs[:, side])
            gh[side] = jnp.zeros_like(gh[side])
            gc[:, side] = jnp.zeros_like(gc[:, side])

    for side in (UP, DOWN):

        @pl.when(jnp.logical_not(has[side]))
        def _():
            vt[:, side - UP] = jnp.zeros_like(vt[:, side - UP])
            cr[:, side - UP] = jnp.zeros_like(cr[:, side - UP])
            gv[side - UP] = jnp.zeros_like(gv[side - UP])
            gc[side - UP] = jnp.zeros_like(gc[side - UP])

    def pack(s):
        object_loads[s].wait()
        for c in range(2):
            for b in range(2):
                left_edge, right_edge = packed_edges(obj[s, c, b * HALF : (b + 1) * HALF])
                pk[s, LEFT, c, b * BLOCK : (b + 1) * BLOCK] = left_edge
                pk[s, RIGHT, c, b * BLOCK : (b + 1) * BLOCK] = right_edge

    pack(0)
    pl.semaphore_wait(barrier, count)

    opposite = {LEFT: RIGHT, RIGHT: LEFT, UP: DOWN, DOWN: UP, UP_CORNER: DOWN_CORNER, DOWN_CORNER: UP_CORNER}

    def landing(s, kind):
        if kind in (LEFT, RIGHT):
            return rs.at[s, kind]
        if kind in (UP, DOWN):
            return vt.at[s, kind - UP]
        return cr.at[s, kind - UP_CORNER]

    def source(s, kind):
        if kind in (LEFT, RIGHT):
            return pk.at[s, kind]
        if kind in (UP, DOWN):
            return obj.at[s, :, (kind - UP) * HALF : (kind - UP + 1) * HALF]
        return rs.at[s, :, :, (kind - UP_CORNER) * BLOCK : (kind - UP_CORNER + 1) * BLOCK]

    def halo_copy(s, kind):
        return pltpu.make_async_remote_copy(
            src_ref=source(s, kind),
            dst_ref=landing(s, opposite[kind]),
            send_sem=halo_send.at[s, kind],
            recv_sem=halo_recv.at[s, opposite[kind]],
            device_id=target[kind if kind < UP_CORNER else kind - 2],
            device_id_type=MESH,
        )

    def straight_copy(s, kind, i):
        return pltpu.make_async_remote_copy(
            src_ref=pk.at[(s, kind, *STRAIGHT[i])],
            dst_ref=rs.at[(s, opposite[kind], *STRAIGHT[i])],
            send_sem=cross_send.at[s, 2 * i],
            recv_sem=cross_recv.at[s, 2 * i],
            device_id=target[kind],
            device_id_type=MESH,
        )

    def detour_copy(s, kind):
        return pltpu.make_async_remote_copy(
            src_ref=pk.at[s, kind, 1, EXTRA:],
            dst_ref=rl.at[s],
            send_sem=cross_send.at[s, 1],
            recv_sem=relay_recv.at[s],
            device_id={"mode": mode, "ty": ty, "tx": relay_tx[kind]},
            device_id_type=MESH,
        )

    def onward_copy(s, kind):
        return pltpu.make_async_remote_copy(
            src_ref=rl.at[s],
            dst_ref=rs.at[s, opposite[kind], 1, EXTRA:],
            send_sem=relay_send.at[s],
            recv_sem=cross_recv.at[s, 1],
            device_id={"mode": mirror, "ty": ty, "tx": landing_tx[kind]},
            device_id_type=MESH,
        )

    def near(kind):
        return jnp.logical_and(has[kind], jnp.logical_not(crossing[kind])) if kind in crossing else has[kind]

    def start_halo(s, kind):
        @pl.when(near(kind))
        def _():
            halo_copy(s, kind).start()

        if kind in crossing:

            @pl.when(crossing[kind])
            def _():
                straight_copy(s, kind, 0).start()
                straight_copy(s, kind, 1).start()
                detour_copy(s, kind).start()

    def await_halo(s, kind):
        @pl.when(near(kind))
        def _():
            halo_copy(s, opposite[kind]).wait_recv()

        if kind in crossing:

            @pl.when(crossing[kind])
            def _():
                straight_copy(s, opposite[kind], 0).wait_recv()
                straight_copy(s, opposite[kind], 1).wait_recv()
                onward_copy(s, opposite[kind]).wait_recv()

    def relay(s):
        for kind in (LEFT, RIGHT):

            @pl.when(relaying[kind])
            def _():
                detour_copy(s, kind).wait_recv()
                onward_copy(s, kind).start()

    for s in range(SLICES):
        if s + 1 < SLICES:
            pack(s + 1)
        for kind in (RIGHT, LEFT, UP, DOWN):
            start_halo(s, kind)

    def relay_corners(s):
        await_halo(s, LEFT)
        await_halo(s, RIGHT)
        start_halo(s, UP_CORNER)
        start_halo(s, DOWN_CORNER)

    row, col = pos_ref[0], pos_ref[1]
    here, there = (lax.broadcasted_iota(jnp.int32, (DET, 2 * DET), d) for d in range(2))
    pick_rows = jnp.where(there == here + row, 1.0, 0.0).astype(BF16)
    offset = here + (col + 2 * DET - HALF)
    offset = jnp.where(offset >= 2 * DET, offset - 2 * DET, offset)
    pick_cols = jnp.where(there == offset, 1.0, 0.0).astype(BF16)
    here, there = (lax.broadcasted_iota(jnp.int32, (2 * DET, DET), d) for d in range(2))
    put_rows = jnp.where(here == there + row, 1.0, 0.0).astype(BF16)
    offset = there + (col + 2 * DET - HALF)
    offset = jnp.where(offset >= 2 * DET, offset - 2 * DET, offset)
    put_cols = jnp.where(here == offset, 1.0, 0.0).astype(BF16)

    def twice(x, axis):
        return jnp.concatenate([x, x], axis=axis)

    def both(x, axis):
        return jnp.concatenate(halves(x), axis=axis)

    def dot(x, y):
        return jnp.dot(x, y, preferred_element_type=F32)

    def build_window(s):
        for kind in (UP, DOWN, UP_CORNER, DOWN_CORNER):
            await_halo(s, kind)
        for c in range(2):
            for side in range(2):
                at = side * 3 * HALF
                ext[c, at : at + HALF, :DET] = vt[s, side, c]
                first, second = unpacked_sides(cr[s, side, LEFT, c], cr[s, side, RIGHT, c])
                ext[c, at : at + BLOCK, DET:] = first
                ext[c, at + BLOCK : at + HALF, DET:] = second
            ext[c, HALF : 3 * HALF, :DET] = obj[s, c]
            for b in range(2):
                block = slice(b * BLOCK, (b + 1) * BLOCK)
                first, second = unpacked_sides(rs[s, LEFT, c, block], rs[s, RIGHT, c, block])
                at = HALF + b * HALF
                ext[c, at : at + BLOCK, DET:] = first
                ext[c, at + BLOCK : at + HALF, DET:] = second
            band = dot(twice(pick_rows, 1), both(ext[c], 0))
            window[s, c] = dot(both(band, 1), twice(put_cols, 0))

    relay(0)
    relay_corners(0)
    for s in range(SLICES):
        if s + 1 < SLICES:
            relay_corners(s + 1)
        if s == 0:
            for ahead in range(1, SLICES):
                relay(ahead)
        build_window(s)
        if s == 0:
            for copy in loads:
                copy.wait()

        def fetch(m):
            if s == 0:
                real, imag = probe[m, 0], probe[m, 1]
            else:
                real, imag = psi[s - 1, 0, rows(m)], psi[s - 1, 1, rows(m)]
            wr, wi = window[s, 0], window[s, 1]
            return real * wr - imag * wi, real * wi + imag * wr

        def deliver(m, real, imag):
            if s + 1 < SLICES:
                psi[s, 0, rows(m)] = real
                psi[s, 1, rows(m)] = imag
            else:
                far[0, rows(m)] = real
                far[1, rows(m)] = imag
                power = real * real + imag * imag
                part[...] = power if m == 0 else part[...] + power

        two_sided(mats, STEP if s + 1 < SLICES else FAR, fetch, deliver, mid)

    first, last = mode == 0, mode == modes - 1
    inner, lower = jnp.logical_not(jnp.logical_or(first, last)), mode < modes // 2

    def mode_copy(step):
        return pltpu.make_async_remote_copy(
            src_ref=part,
            dst_ref=others.at[step - 1],
            send_sem=mode_send.at[step - 1],
            recv_sem=mode_recv.at[step - 1],
            device_id=peer(step),
            device_id_type=MESH,
        )

    for peer_mode in (jnp.where(lower, 3, 0), jnp.where(lower, 2, 1), mode + 1 - 2 * lax.rem(mode, 2)):
        mode_copy(lax.rem(peer_mode - mode + modes, modes)).start()
    whole = part[...]
    for step in range(1, modes):
        mode_copy(step).wait_recv()
        whole = whole + others[step - 1]
    weight = 1.0 - measured[0, 0, 0] / jnp.maximum(jnp.sqrt(whole), 1.0)

    outer, collector = jnp.logical_or(first, last), jnp.where(lower, 1, 2)

    def far_slice(low_pair, i):
        return SLICES - 1 - i if low_pair else 1 - i

    def piece(q):
        return q // 2, pl.ds(q % 2 * HALF, HALF)

    def collect_copy(low_pair, i, q):
        return pltpu.make_async_remote_copy(
            src_ref=term.at[(far_slice(low_pair, i), *piece(q))],
            dst_ref=collected.at[(i, *piece(q))],
            send_sem=collect_send.at[i, q],
            recv_sem=collect_recv.at[i, q],
            device_id={"mode": collector, "ty": ty, "tx": tx},
            device_id_type=MESH,
        )

    def pair_sum_copy(low_pair, i, q):
        return pltpu.make_async_remote_copy(
            src_ref=joint.at[(i, *piece(q))],
            dst_ref=parts.at[(1, *piece(q))],
            send_sem=joint_send.at[i, q],
            recv_sem=joint_recv.at[q],
            device_id={"mode": far_slice(low_pair, i), "ty": ty, "tx": tx},
            device_id_type=MESH,
        )

    def partner_copy(owner, c):
        return pltpu.make_async_remote_copy(
            src_ref=term.at[owner, c],
            dst_ref=parts.at[0, c],
            send_sem=partner_send.at[c],
            recv_sem=partner_recv.at[c],
            device_id={"mode": owner, "ty": ty, "tx": tx},
            device_id_type=MESH,
        )

    def send_far(low_pair, i, pieces=(0, 1, 2, 3)):
        @pl.when(first if low_pair else last)
        def _():
            for q in pieces:
                collect_copy(low_pair, i, q).start()

    def send_partner(owner):
        @pl.when(mode == (owner ^ 1))
        def _():
            for c in range(2):
                partner_copy(owner, c).start()

    def join(low_pair, i, pieces=(0, 1, 2, 3)):
        s = far_slice(low_pair, i)
        for q in pieces:
            collect_copy(low_pair, i, q).wait_recv()
            at = piece(q)
            joint[(i, *at)] = collected[(i, *at)] + term[(s, *at)]
            pair_sum_copy(low_pair, i, q).start()

    for s in reversed(range(SLICES)):

        def fetch(m):
            if s == SLICES - 1:
                return weight * far[0, rows(m)], weight * far[1, rows(m)]
            return pulled[0, rows(m)], pulled[1, rows(m)]

        def deliver(m, real, imag):
            if s == 0:
                pr, pi = probe[m, 0], probe[m, 1]
            else:
                pr, pi = psi[s - 1, 0, rows(m)], psi[s - 1, 1, rows(m)]
            tr, ti = pr * real + pi * imag, pr * imag - pi * real
            term[s, 0] = tr if m == 0 else term[s, 0] + tr
            term[s, 1] = ti if m == 0 else term[s, 1] + ti
            if s > 0:
                wr, wi = window[s, 0], window[s, 1]
                pulled[0, rows(m)] = wr * real + wi * imag
                pulled[1, rows(m)] = wr * imag - wi * real

        two_sided(mats, FAR_BACK if s == SLICES - 1 else STEP_BACK, fetch, deliver, mid)

        if s == 3:
            send_far(True, 0)
            send_partner(3)
        elif s == 2:
            send_far(True, 1)
        elif s == 1:
            send_partner(1)
            send_far(False, 0, (0, 1))
        else:
            send_far(False, 1)
            send_partner(0)
            send_far(False, 0, (2, 3))
            send_partner(2)

    for low_pair in (True, False):

        @pl.when(mode == (1 if low_pair else 2))
        def _():
            join(low_pair, 0, (0, 1))
            if low_pair:
                join(low_pair, 0, (2, 3))
                join(low_pair, 1)
            else:
                join(low_pair, 1)
                join(low_pair, 0, (2, 3))

    def place(c):
        partner_copy(0, c).wait_recv()
        for q in range(2 * c, 2 * c + 2):
            pair_sum_copy(True, 0, q).wait_recv()
        mine = term[mode, c] + parts[0, c] + parts[1, c]
        tall = dot(twice(put_rows, 1), both(mine, 0))
        placed = dot(both(tall, 1), twice(pick_cols, 0))
        middle[c] = placed[HALF : 3 * HALF, :DET]
        for v in range(2):
            at = 3 * v * HALF
            vp[v, c] = placed[at : at + HALF, :DET]
            cp[v, LEFT, c], cp[v, RIGHT, c] = packed_sides(placed[at : at + HALF, DET:])
        hp[LEFT, c], hp[RIGHT, c] = packed_sides(placed[HALF : 3 * HALF, DET:])

    def grad_has(v, h):
        if v is None:
            return has[h]
        return has[UP + v] if h is None else jnp.logical_and(has[UP + v], has[h])

    def grad_copy(v, h, c):
        if v is None:
            src, dst, i = hp.at[h, c], gh.at[1 - h, c], h
        elif h is None:
            src, dst, i = vp.at[v, c], gv.at[1 - v, c], 2 + v
        else:
            src, dst, i = cp.at[v, h, c], gc.at[1 - v, 1 - h, c], 4 + 2 * v + h
        return pltpu.make_async_remote_copy(
            src_ref=src,
            dst_ref=dst,
            send_sem=grad_send.at[i, c],
            recv_sem=grad_recv.at[i, c],
            device_id={"mode": mode, "ty": ty if v is None else ty + 2 * v - 1, "tx": tx if h is None else tx + 2 * h - 1},
            device_id_type=MESH,
        )

    directions = [(None, 1), (0, 1), (1, 1), (None, 0), (0, 0), (1, 0), (0, None), (1, None)]
    for c in range(2):
        place(c)
        for v, h in directions:

            @pl.when(grad_has(v, h))
            def _():
                grad_copy(v, h, c).start()

    for v, h in reversed(directions):
        @pl.when(grad_has(v, h))
        def _():
            for c in range(2):
                grad_copy(v if v is None else 1 - v, h if h is None else 1 - h, c).wait_recv()

    for c in range(2):
        for v in range(2):
            half = slice(v * HALF, (v + 1) * HALF)
            sides = unpacked_halves(gh[LEFT, c], gh[RIGHT, c])[v]
            corners = jnp.concatenate(unpacked_halves(gc[v, LEFT, c], gc[v, RIGHT, c]), axis=0)
            out[0, c, half] = middle[c, half] + gv[v, c] + (sides + corners)

    for v, h in directions:

        @pl.when(grad_has(v, h))
        def _():
            for c in range(2):
                grad_copy(v, h, c).wait_send()

    for kind in range(6):

        @pl.when(near(kind))
        def _():
            for s in range(SLICES):
                halo_copy(s, kind).wait_send()

    for kind in (LEFT, RIGHT):

        @pl.when(crossing[kind])
        def _():
            for s in range(SLICES):
                straight_copy(s, kind, 0).wait_send()
                straight_copy(s, kind, 1).wait_send()
                detour_copy(s, kind).wait_send()

        @pl.when(relaying[kind])
        def _():
            for s in range(SLICES):
                onward_copy(s, kind).wait_send()

    for step in range(1, modes):
        mode_copy(step).wait_send()

    for c in range(2):
        partner_copy(0, c).wait_send()
    for i in range(2):
        for q in range(4):

            @pl.when(outer)
            def _():
                collect_copy(True, i, q).wait_send()

            @pl.when(inner)
            def _():
                pair_sum_copy(True, i, q).wait_send()


VMEM = pl.BlockSpec(memory_space=pltpu.VMEM)
SMEM = pl.BlockSpec(memory_space=pltpu.SMEM)
ANY = pl.BlockSpec(memory_space=pl.ANY)


def body(object_slices, probe_modes, positions, measured):
    mats = jnp.asarray(tables())
    modes = lax.axis_size("mode")
    dma = pltpu.SemaphoreType.DMA
    wave = (LOCAL * DET, DET)
    scratch = dict(
        obj=(SLICES, 2, DET, DET),
        probe=(LOCAL, 2, DET, DET),
        measured=(1, 1, 1, DET, DET),
        mats=(8, 2 * DET, 2 * DET),
        pk=(SLICES, 2, 2, HALF, DET),
        rs=(SLICES, 2, 2, HALF, DET),
        rl=(SLICES, HALF - EXTRA, DET),
        vt=(SLICES, 2, 2, HALF, DET),
        cr=(SLICES, 2, 2, 2, BLOCK, DET),
        ext=(2, 2 * DET, 2 * DET),
        window=(SLICES, 2, DET, DET),
        psi=(SLICES - 1, 2, *wave),
        far=(2, *wave),
        part=(DET, DET),
        others=(modes - 1, DET, DET),
        mid=(4 * DET, LOCAL * DET),
        pulled=(2, *wave),
        term=(SLICES, 2, DET, DET),
        collected=(2, 2, DET, DET),
        joint=(2, 2, DET, DET),
        parts=(2, 2, DET, DET),
        middle=(2, DET, DET),
        vp=(2, 2, HALF, DET),
        hp=(2, 2, HALF, DET),
        cp=(2, 2, 2, BLOCK, DET),
        gv=(2, 2, HALF, DET),
        gh=(2, 2, HALF, DET),
        gc=(2, 2, 2, BLOCK, DET),
    )
    return pl.pallas_call(
        kernel,
        out_shape=jax.ShapeDtypeStruct((1, 2, DET, DET), F32),
        in_specs=[SMEM, ANY, ANY, ANY, ANY],
        out_specs=VMEM,
        scratch_shapes=[pltpu.VMEM(shape, BF16 if name in ("mid", "mats") else F32) for name, shape in scratch.items()]
        + [dma((3 + SLICES,))]
        + [dma((SLICES, 6)), dma((SLICES, 6))]
        + [dma((SLICES, 3)), dma((SLICES, 3)), dma((SLICES,)), dma((SLICES,))]
        + [dma((modes - 1,)), dma((modes - 1,))]
        + [dma((2, 4)), dma((2, 4)), dma((2, 4)), dma((4,)), dma((2,)), dma((2,))]
        + [dma((8, 2)), dma((8, 2))],
        compiler_params=pltpu.CompilerParams(collective_id=0, has_side_effects=True),
        name="ptycho",
    )(positions.reshape(2), object_slices, probe_modes, measured, mats)


def solution(mesh):
    return jax.shard_map(
        body,
        mesh=mesh,
        in_specs=(
            P(None, None, "ty", "tx"),
            P("mode", None, None, None),
            P("ty", "tx", None, None),
            P("ty", "tx", None, None, None),
        ),
        out_specs=P("mode", None, "ty", "tx"),
        check_vma=False,
    )
```

```python
import functools

import numpy as np
import jax
import jax.numpy as jnp
from jax import lax
from jax.experimental import pallas as pl
from jax.experimental.pallas import tpu as pltpu
from jax.sharding import PartitionSpec as P

DET = 128
SLICES = 4
MARGIN = 64
LOCAL = 4
RATE = 0.3
F32 = jnp.float32
BF16 = jnp.bfloat16


def real_block(matrix):
    return np.block([[matrix.real, matrix.imag], [-matrix.imag, matrix.real]])


def tables():
    counter = np.arange(DET)
    fourier = np.exp(-2j * np.pi * (np.outer(counter, counter) % DET) / DET) / np.sqrt(DET)
    frequency = np.where(counter < DET // 2, counter, counter - DET).astype(np.float64)
    chirp = np.exp(-1j * RATE * frequency**2 / DET)
    step = fourier.conj() @ (chirp[:, None] * fourier)
    step = (step + step.T) / 2
    out = []
    for matrix in (step, step.conj(), fourier, fourier.conj()):
        block = real_block(matrix).astype(np.float32)
        high = block.astype(jnp.bfloat16)
        low = (block - high.astype(np.float32)).astype(jnp.bfloat16)
        out += [high, low]
    return np.stack(out)


STEP, STEP_BACK, FAR, FAR_BACK = range(4)
CONJ = {STEP: STEP_BACK, STEP_BACK: STEP, FAR: FAR_BACK, FAR_BACK: FAR}


def halves(x):
    high = x.astype(BF16)
    return high, (x - high.astype(F32)).astype(BF16)


def rows(m):
    return slice(m * DET, (m + 1) * DET)


def right_product(mats, which, real, imag):
    rh, rl = halves(real)
    ih, il = halves(imag)
    lhs = jnp.concatenate([rh, ih, rl, il, rh, ih], axis=1)
    high, low = mats[2 * which], mats[2 * which + 1]
    rhs = jnp.concatenate([high, high, low], axis=0)
    return jnp.dot(lhs, rhs, preferred_element_type=F32)


def left_product(mats, which, stacked):
    conj = CONJ[which]
    high, low = mats[2 * conj], mats[2 * conj + 1]
    main = jnp.dot(jnp.concatenate([high, low], axis=0), stacked[: 2 * DET], preferred_element_type=F32)
    rest = jnp.dot(high, stacked[2 * DET :], preferred_element_type=F32)
    return main[: 2 * DET] + main[2 * DET :] + rest


def two_sided(mats, which, fetch, deliver, mid):
    kept = []
    for pair in range(LOCAL // 2):
        got = [fetch(m) for m in (2 * pair, 2 * pair + 1)]
        real = jnp.concatenate([g[0] for g in got], axis=0)
        imag = jnp.concatenate([g[1] for g in got], axis=0)
        out = right_product(mats, which, real, imag)
        re = jnp.concatenate([out[:DET, :DET], out[DET:, :DET]], axis=1)
        im = jnp.concatenate([out[:DET, DET:], out[DET:, DET:]], axis=1)
        stack = jnp.concatenate([re, im], axis=0)
        high, low = halves(stack)
        kept.append(jnp.concatenate([high, low], axis=0))
    for pair in range(LOCAL // 2):
        out = left_product(mats, which, kept[pair])
        for k in range(2):
            deliver(2 * pair + k, out[:DET, rows(k)], out[DET:, rows(k)])


MESH = pl.DeviceIdType.MESH
HALF = DET // 2
BLOCK = HALF // 2
EXTRA = 16
STRAIGHT = ((0, slice(0, HALF)), (1, slice(0, EXTRA)))


def lane_low(shape):
    return lax.broadcasted_iota(jnp.int32, shape, len(shape) - 1) < HALF


def turned(x):
    return pltpu.roll(x, HALF, x.ndim - 1)


def packed_edges(strip):
    first, second = strip[:BLOCK], strip[BLOCK:]
    low = lane_low(first.shape)
    left_edge = jnp.where(low, first, turned(second))
    right_edge = jnp.where(low, turned(first), second)
    return left_edge, right_edge


def unpacked_sides(from_left, from_right):
    low = lane_low(from_left.shape)
    first = jnp.where(low, from_right, turned(from_left))
    second = jnp.where(low, turned(from_right), from_left)
    return first, second


def packed_sides(strip):
    half = strip.shape[0] // 2
    upper, lower = strip[:half], strip[half:]
    low = lane_low(upper.shape)
    return jnp.where(low, turned(upper), lower), jnp.where(low, upper, turned(lower))


def unpacked_halves(from_left, from_right):
    low = lane_low(from_left.shape)
    return jnp.where(low, from_left, turned(from_right)), jnp.where(low, turned(from_left), from_right)


LEFT, RIGHT, UP, DOWN, UP_CORNER, DOWN_CORNER = range(6)


def kernel(
    pos_ref, obj_in, probe_in, measured_in, mats_in, out,
    obj, probe, measured, mats, pk, rs, rl, vt, cr, ext, window, psi, far, part, others, mid, pulled, term, collected, joint, parts, middle, vp, hp, cp, gv, gh, gc,
    load, halo_send, halo_recv, cross_send, cross_recv, relay_send, relay_recv, mode_send, mode_recv, collect_send, collect_recv, joint_send, joint_recv, partner_send, partner_recv, grad_send, grad_recv,
):
    mode, ty, tx = lax.axis_index("mode"), lax.axis_index("ty"), lax.axis_index("tx")
    modes, tys, txs = lax.axis_size("mode"), lax.axis_size("ty"), lax.axis_size("tx")
    has = {LEFT: tx > 0, RIGHT: tx < txs - 1, UP: ty > 0, DOWN: ty < tys - 1}
    has[UP_CORNER], has[DOWN_CORNER] = has[UP], has[DOWN]
    cross_right, cross_left = tx == txs // 2 - 1, tx == txs // 2
    mirror = modes - 1 - mode
    left_mode = jnp.where(cross_left, mirror, mode)
    right_mode = jnp.where(cross_right, mirror, mode)
    target = {
        LEFT: {"mode": left_mode, "ty": ty, "tx": tx - 1},
        RIGHT: {"mode": right_mode, "ty": ty, "tx": tx + 1},
        UP: {"mode": mode, "ty": ty - 1, "tx": tx},
        DOWN: {"mode": mode, "ty": ty + 1, "tx": tx},
    }
    crossing = {LEFT: cross_left, RIGHT: cross_right}
    relay_tx = {LEFT: txs - 1, RIGHT: 0}
    relaying = {LEFT: tx == relay_tx[LEFT], RIGHT: tx == relay_tx[RIGHT]}
    landing_tx = {LEFT: txs // 2 - 1, RIGHT: txs // 2}
    direct = {LEFT: {"mode": mode, "ty": ty, "tx": tx - 1}, RIGHT: {"mode": mode, "ty": ty, "tx": tx + 1}}

    def peer(step):
        return {"mode": lax.rem(mode + step, modes), "ty": ty, "tx": tx}

    barrier = pltpu.get_barrier_semaphore()
    count = jnp.int32(modes - 1)
    for side in (LEFT, RIGHT, UP, DOWN):
        count = count + has[side].astype(jnp.int32)

        @pl.when(has[side])
        def _():
            pl.semaphore_signal(barrier, inc=1, device_id=target[side], device_id_type=MESH)

    for side, cross in ((LEFT, cross_left), (RIGHT, cross_right)):
        far_pair = jnp.logical_and(cross, has[side])
        count = count + far_pair.astype(jnp.int32)

        @pl.when(far_pair)
        def _():
            pl.semaphore_signal(barrier, inc=1, device_id=direct[side], device_id_type=MESH)

    for side in (LEFT, RIGHT):
        from_relay, from_landing = crossing[side], relaying[side]
        count = count + from_relay.astype(jnp.int32) + from_landing.astype(jnp.int32)

        @pl.when(relaying[side])
        def _():
            sender = {"mode": mode, "ty": ty, "tx": landing_tx[1 - side]}
            pl.semaphore_signal(barrier, inc=1, device_id=sender, device_id_type=MESH)

        @pl.when(tx == landing_tx[side])
        def _():
            relay = {"mode": mirror, "ty": ty, "tx": relay_tx[side]}
            pl.semaphore_signal(barrier, inc=1, device_id=relay, device_id_type=MESH)

    for step in range(1, modes):
        pl.semaphore_signal(barrier, inc=1, device_id=peer(step), device_id_type=MESH)
    object_loads = [pltpu.make_async_copy(obj_in.at[s], obj.at[s], load.at[3 + s]) for s in range(SLICES)]
    loads = [pltpu.make_async_copy(src, dst, load.at[i]) for i, (src, dst) in enumerate(((probe_in, probe), (mats_in, mats), (measured_in, measured)))]
    for copy in object_loads + loads:
        copy.start()

    for side in (LEFT, RIGHT):

        @pl.when(jnp.logical_not(has[side]))
        def _():
            rs[:, side] = jnp.zeros_like(rs[:, side])
            gh[side] = jnp.zeros_like(gh[side])
            gc[:, side] = jnp.zeros_like(gc[:, side])

    for side in (UP, DOWN):

        @pl.when(jnp.logical_not(has[side]))
        def _():
            vt[:, side - UP] = jnp.zeros_like(vt[:, side - UP])
            cr[:, side - UP] = jnp.zeros_like(cr[:, side - UP])
            gv[side - UP] = jnp.zeros_like(gv[side - UP])
            gc[side - UP] = jnp.zeros_like(gc[side - UP])

    def pack(s):
        object_loads[s].wait()
        for c in range(2):
            for b in range(2):
                left_edge, right_edge = packed_edges(obj[s, c, b * HALF : (b + 1) * HALF])
                pk[s, LEFT, c, b * BLOCK : (b + 1) * BLOCK] = left_edge
                pk[s, RIGHT, c, b * BLOCK : (b + 1) * BLOCK] = right_edge

    pack(0)
    pl.semaphore_wait(barrier, count)

    opposite = {LEFT: RIGHT, RIGHT: LEFT, UP: DOWN, DOWN: UP, UP_CORNER: DOWN_CORNER, DOWN_CORNER: UP_CORNER}

    def landing(s, kind):
        if kind in (LEFT, RIGHT):
            return rs.at[s, kind]
        if kind in (UP, DOWN):
            return vt.at[s, kind - UP]
        return cr.at[s, kind - UP_CORNER]

    def source(s, kind):
        if kind in (LEFT, RIGHT):
            return pk.at[s, kind]
        if kind in (UP, DOWN):
            return obj.at[s, :, (kind - UP) * HALF : (kind - UP + 1) * HALF]
        return rs.at[s, :, :, (kind - UP_CORNER) * BLOCK : (kind - UP_CORNER + 1) * BLOCK]

    def halo_copy(s, kind):
        return pltpu.make_async_remote_copy(
            src_ref=source(s, kind),
            dst_ref=landing(s, opposite[kind]),
            send_sem=halo_send.at[s, kind],
            recv_sem=halo_recv.at[s, opposite[kind]],
            device_id=target[kind if kind < UP_CORNER else kind - 2],
            device_id_type=MESH,
        )

    def straight_copy(s, kind, i):
        return pltpu.make_async_remote_copy(
            src_ref=pk.at[(s, kind, *STRAIGHT[i])],
            dst_ref=rs.at[(s, opposite[kind], *STRAIGHT[i])],
            send_sem=cross_send.at[s, 2 * i],
            recv_sem=cross_recv.at[s, 2 * i],
            device_id=target[kind],
            device_id_type=MESH,
        )

    def detour_copy(s, kind):
        return pltpu.make_async_remote_copy(
            src_ref=pk.at[s, kind, 1, EXTRA:],
            dst_ref=rl.at[s],
            send_sem=cross_send.at[s, 1],
            recv_sem=relay_recv.at[s],
            device_id={"mode": mode, "ty": ty, "tx": relay_tx[kind]},
            device_id_type=MESH,
        )

    def onward_copy(s, kind):
        return pltpu.make_async_remote_copy(
            src_ref=rl.at[s],
            dst_ref=rs.at[s, opposite[kind], 1, EXTRA:],
            send_sem=relay_send.at[s],
            recv_sem=cross_recv.at[s, 1],
            device_id={"mode": mirror, "ty": ty, "tx": landing_tx[kind]},
            device_id_type=MESH,
        )

    def near(kind):
        return jnp.logical_and(has[kind], jnp.logical_not(crossing[kind])) if kind in crossing else has[kind]

    def start_halo(s, kind):
        @pl.when(near(kind))
        def _():
            halo_copy(s, kind).start()

        if kind in crossing:

            @pl.when(crossing[kind])
            def _():
                straight_copy(s, kind, 0).start()
                straight_copy(s, kind, 1).start()
                detour_copy(s, kind).start()

    def await_halo(s, kind):
        @pl.when(near(kind))
        def _():
            halo_copy(s, opposite[kind]).wait_recv()

        if kind in crossing:

            @pl.when(crossing[kind])
            def _():
                straight_copy(s, opposite[kind], 0).wait_recv()
                straight_copy(s, opposite[kind], 1).wait_recv()
                onward_copy(s, opposite[kind]).wait_recv()

    def relay(s):
        for kind in (LEFT, RIGHT):

            @pl.when(relaying[kind])
            def _():
                detour_copy(s, kind).wait_recv()
                onward_copy(s, kind).start()

    for s in range(SLICES):
        if s + 1 < SLICES:
            pack(s + 1)
        for kind in (RIGHT, LEFT, UP, DOWN):
            start_halo(s, kind)

    def relay_corners(s):
        await_halo(s, LEFT)
        await_halo(s, RIGHT)
        start_halo(s, UP_CORNER)
        start_halo(s, DOWN_CORNER)

    row, col = pos_ref[0], pos_ref[1]
    here, there = (lax.broadcasted_iota(jnp.int32, (DET, 2 * DET), d) for d in range(2))
    pick_rows = jnp.where(there == here + row, 1.0, 0.0).astype(BF16)
    offset = here + (col + 2 * DET - HALF)
    offset = jnp.where(offset >= 2 * DET, offset - 2 * DET, offset)
    pick_cols = jnp.where(there == offset, 1.0, 0.0).astype(BF16)
    here, there = (lax.broadcasted_iota(jnp.int32, (2 * DET, DET), d) for d in range(2))
    put_rows = jnp.where(here == there + row, 1.0, 0.0).astype(BF16)
    offset = there + (col + 2 * DET - HALF)
    offset = jnp.where(offset >= 2 * DET, offset - 2 * DET, offset)
    put_cols = jnp.where(here == offset, 1.0, 0.0).astype(BF16)

    def twice(x, axis):
        return jnp.concatenate([x, x], axis=axis)

    def both(x, axis):
        return jnp.concatenate(halves(x), axis=axis)

    def dot(x, y):
        return jnp.dot(x, y, preferred_element_type=F32)

    def build_window(s):
        for kind in (UP, DOWN, UP_CORNER, DOWN_CORNER):
            await_halo(s, kind)
        for c in range(2):
            for side in range(2):
                at = side * 3 * HALF
                ext[c, at : at + HALF, :DET] = vt[s, side, c]
                first, second = unpacked_sides(cr[s, side, LEFT, c], cr[s, side, RIGHT, c])
                ext[c, at : at + BLOCK, DET:] = first
                ext[c, at + BLOCK : at + HALF, DET:] = second
            ext[c, HALF : 3 * HALF, :DET] = obj[s, c]
            for b in range(2):
                block = slice(b * BLOCK, (b + 1) * BLOCK)
                first, second = unpacked_sides(rs[s, LEFT, c, block], rs[s, RIGHT, c, block])
                at = HALF + b * HALF
                ext[c, at : at + BLOCK, DET:] = first
                ext[c, at + BLOCK : at + HALF, DET:] = second
            band = dot(twice(pick_rows, 1), both(ext[c], 0))
            window[s, c] = dot(both(band, 1), twice(put_cols, 0))

    relay(0)
    relay_corners(0)
    for s in range(SLICES):
        if s + 1 < SLICES:
            relay_corners(s + 1)
        if s == 0:
            for ahead in range(1, SLICES):
                relay(ahead)
        build_window(s)
        if s == 0:
            for copy in loads:
                copy.wait()

        def fetch(m):
            if s == 0:
                real, imag = probe[m, 0], probe[m, 1]
            else:
                real, imag = psi[s - 1, 0, rows(m)], psi[s - 1, 1, rows(m)]
            wr, wi = window[s, 0], window[s, 1]
            return real * wr - imag * wi, real * wi + imag * wr

        def deliver(m, real, imag):
            if s + 1 < SLICES:
                psi[s, 0, rows(m)] = real
                psi[s, 1, rows(m)] = imag
            else:
                far[0, rows(m)] = real
                far[1, rows(m)] = imag
                power = real * real + imag * imag
                part[...] = power if m == 0 else part[...] + power

        two_sided(mats, STEP if s + 1 < SLICES else FAR, fetch, deliver, mid)

    first, last = mode == 0, mode == modes - 1
    inner, lower = jnp.logical_not(jnp.logical_or(first, last)), mode < modes // 2

    def mode_copy(step):
        return pltpu.make_async_remote_copy(
            src_ref=part,
            dst_ref=others.at[step - 1],
            send_sem=mode_send.at[step - 1],
            recv_sem=mode_recv.at[step - 1],
            device_id=peer(step),
            device_id_type=MESH,
        )

    for peer_mode in (jnp.where(lower, 3, 0), jnp.where(lower, 2, 1), mode + 1 - 2 * lax.rem(mode, 2)):
        mode_copy(lax.rem(peer_mode - mode + modes, modes)).start()
    whole = part[...]
    for step in range(1, modes):
        mode_copy(step).wait_recv()
        whole = whole + others[step - 1]
    weight = 1.0 - measured[0, 0, 0] / jnp.maximum(jnp.sqrt(whole), 1.0)

    outer, collector = jnp.logical_or(first, last), jnp.where(lower, 1, 2)

    def far_slice(low_pair, i):
        return SLICES - 1 - i if low_pair else 1 - i

    def piece(q):
        return q // 2, pl.ds(q % 2 * HALF, HALF)

    def collect_copy(low_pair, i, q):
        return pltpu.make_async_remote_copy(
            src_ref=term.at[(far_slice(low_pair, i), *piece(q))],
            dst_ref=collected.at[(i, *piece(q))],
            send_sem=collect_send.at[i, q],
            recv_sem=collect_recv.at[i, q],
            device_id={"mode": collector, "ty": ty, "tx": tx},
            device_id_type=MESH,
        )

    def pair_sum_copy(low_pair, i, q):
        return pltpu.make_async_remote_copy(
            src_ref=joint.at[(i, *piece(q))],
            dst_ref=parts.at[(1, *piece(q))],
            send_sem=joint_send.at[i, q],
            recv_sem=joint_recv.at[q],
            device_id={"mode": far_slice(low_pair, i), "ty": ty, "tx": tx},
            device_id_type=MESH,
        )

    def partner_copy(owner, c):
        return pltpu.make_async_remote_copy(
            src_ref=term.at[owner, c],
            dst_ref=parts.at[0, c],
            send_sem=partner_send.at[c],
            recv_sem=partner_recv.at[c],
            device_id={"mode": owner, "ty": ty, "tx": tx},
            device_id_type=MESH,
        )

    def send_far(low_pair, i, pieces=(0, 1, 2, 3)):
        @pl.when(first if low_pair else last)
        def _():
            for q in pieces:
                collect_copy(low_pair, i, q).start()

    def send_partner(owner):
        @pl.when(mode == (owner ^ 1))
        def _():
            for c in range(2):
                partner_copy(owner, c).start()

    def join(low_pair, i, pieces=(0, 1, 2, 3)):
        s = far_slice(low_pair, i)
        for q in pieces:
            collect_copy(low_pair, i, q).wait_recv()
            at = piece(q)
            joint[(i, *at)] = collected[(i, *at)] + term[(s, *at)]
            pair_sum_copy(low_pair, i, q).start()

    for s in reversed(range(SLICES)):

        def fetch(m):
            if s == SLICES - 1:
                return weight * far[0, rows(m)], weight * far[1, rows(m)]
            return pulled[0, rows(m)], pulled[1, rows(m)]

        def deliver(m, real, imag):
            if s == 0:
                pr, pi = probe[m, 0], probe[m, 1]
            else:
                pr, pi = psi[s - 1, 0, rows(m)], psi[s - 1, 1, rows(m)]
            tr, ti = pr * real + pi * imag, pr * imag - pi * real
            term[s, 0] = tr if m == 0 else term[s, 0] + tr
            term[s, 1] = ti if m == 0 else term[s, 1] + ti
            if s > 0:
                wr, wi = window[s, 0], window[s, 1]
                pulled[0, rows(m)] = wr * real + wi * imag
                pulled[1, rows(m)] = wr * imag - wi * real

        two_sided(mats, FAR_BACK if s == SLICES - 1 else STEP_BACK, fetch, deliver, mid)

        if s == 3:
            send_far(True, 0)
            send_partner(3)
        elif s == 2:
            send_far(True, 1)
        elif s == 1:
            send_partner(1)
            send_far(False, 0, (0, 1))
        else:
            send_far(False, 1)
            send_partner(0)
            send_far(False, 0, (2, 3))
            send_partner(2)

    for low_pair in (True, False):

        @pl.when(mode == (1 if low_pair else 2))
        def _():
            join(low_pair, 0, (0, 1))
            if low_pair:
                join(low_pair, 0, (2, 3))
                join(low_pair, 1)
            else:
                join(low_pair, 1)
                join(low_pair, 0, (2, 3))

    def place(c):
        partner_copy(0, c).wait_recv()
        for q in range(2 * c, 2 * c + 2):
            pair_sum_copy(True, 0, q).wait_recv()
        mine = term[mode, c] + parts[0, c] + parts[1, c]
        tall = dot(twice(put_rows, 1), both(mine, 0))
        placed = dot(both(tall, 1), twice(pick_cols, 0))
        middle[c] = placed[HALF : 3 * HALF, :DET]
        for v in range(2):
            at = 3 * v * HALF
            vp[v, c] = placed[at : at + HALF, :DET]
            cp[v, LEFT, c], cp[v, RIGHT, c] = packed_sides(placed[at : at + HALF, DET:])
        hp[LEFT, c], hp[RIGHT, c] = packed_sides(placed[HALF : 3 * HALF, DET:])

    def grad_has(v, h):
        if v is None:
            return has[h]
        return has[UP + v] if h is None else jnp.logical_and(has[UP + v], has[h])

    def grad_copy(v, h, c):
        if v is None:
            src, dst, i = hp.at[h, c], gh.at[1 - h, c], h
        elif h is None:
            src, dst, i = vp.at[v, c], gv.at[1 - v, c], 2 + v
        else:
            src, dst, i = cp.at[v, h, c], gc.at[1 - v, 1 - h, c], 4 + 2 * v + h
        return pltpu.make_async_remote_copy(
            src_ref=src,
            dst_ref=dst,
            send_sem=grad_send.at[i, c],
            recv_sem=grad_recv.at[i, c],
            device_id={"mode": mode, "ty": ty if v is None else ty + 2 * v - 1, "tx": tx if h is None else tx + 2 * h - 1},
            device_id_type=MESH,
        )

    directions = [(None, 1), (0, 1), (1, 1), (None, 0), (0, 0), (1, 0), (0, None), (1, None)]
    for c in range(2):
        place(c)
        for v, h in directions:

            @pl.when(grad_has(v, h))
            def _():
                grad_copy(v, h, c).start()

    for v, h in reversed(directions):
        @pl.when(grad_has(v, h))
        def _():
            for c in range(2):
                grad_copy(v if v is None else 1 - v, h if h is None else 1 - h, c).wait_recv()

    for c in range(2):
        for v in range(2):
            half = slice(v * HALF, (v + 1) * HALF)
            sides = unpacked_halves(gh[LEFT, c], gh[RIGHT, c])[v]
            corners = jnp.concatenate(unpacked_halves(gc[v, LEFT, c], gc[v, RIGHT, c]), axis=0)
            out[0, c, half] = middle[c, half] + gv[v, c] + (sides + corners)

    for v, h in directions:

        @pl.when(grad_has(v, h))
        def _():
            for c in range(2):
                grad_copy(v, h, c).wait_send()

    for kind in range(6):

        @pl.when(near(kind))
        def _():
            for s in range(SLICES):
                halo_copy(s, kind).wait_send()

    for kind in (LEFT, RIGHT):

        @pl.when(crossing[kind])
        def _():
            for s in range(SLICES):
                straight_copy(s, kind, 0).wait_send()
                straight_copy(s, kind, 1).wait_send()
                detour_copy(s, kind).wait_send()

        @pl.when(relaying[kind])
        def _():
            for s in range(SLICES):
                onward_copy(s, kind).wait_send()

    for step in range(1, modes):
        mode_copy(step).wait_send()

    for c in range(2):
        partner_copy(0, c).wait_send()
    for i in range(2):
        for q in range(4):

            @pl.when(outer)
            def _():
                collect_copy(True, i, q).wait_send()

            @pl.when(inner)
            def _():
                pair_sum_copy(True, i, q).wait_send()


VMEM = pl.BlockSpec(memory_space=pltpu.VMEM)
SMEM = pl.BlockSpec(memory_space=pltpu.SMEM)
ANY = pl.BlockSpec(memory_space=pl.ANY)


def body(object_slices, probe_modes, positions, measured):
    mats = jnp.asarray(tables())
    modes = lax.axis_size("mode")
    dma = pltpu.SemaphoreType.DMA
    wave = (LOCAL * DET, DET)
    scratch = dict(
        obj=(SLICES, 2, DET, DET),
        probe=(LOCAL, 2, DET, DET),
        measured=(1, 1, 1, DET, DET),
        mats=(8, 2 * DET, 2 * DET),
        pk=(SLICES, 2, 2, HALF, DET),
        rs=(SLICES, 2, 2, HALF, DET),
        rl=(SLICES, HALF - EXTRA, DET),
        vt=(SLICES, 2, 2, HALF, DET),
        cr=(SLICES, 2, 2, 2, BLOCK, DET),
        ext=(2, 2 * DET, 2 * DET),
        window=(SLICES, 2, DET, DET),
        psi=(SLICES - 1, 2, *wave),
        far=(2, *wave),
        part=(DET, DET),
        others=(modes - 1, DET, DET),
        mid=(4 * DET, LOCAL * DET),
        pulled=(2, *wave),
        term=(SLICES, 2, DET, DET),
        collected=(2, 2, DET, DET),
        joint=(2, 2, DET, DET),
        parts=(2, 2, DET, DET),
        middle=(2, DET, DET),
        vp=(2, 2, HALF, DET),
        hp=(2, 2, HALF, DET),
        cp=(2, 2, 2, BLOCK, DET),
        gv=(2, 2, HALF, DET),
        gh=(2, 2, HALF, DET),
        gc=(2, 2, 2, BLOCK, DET),
    )
    return pl.pallas_call(
        kernel,
        out_shape=jax.ShapeDtypeStruct((1, 2, DET, DET), F32),
        in_specs=[SMEM, ANY, ANY, ANY, ANY],
        out_specs=VMEM,
        scratch_shapes=[pltpu.VMEM(shape, BF16 if name in ("mid", "mats") else F32) for name, shape in scratch.items()]
        + [dma((3 + SLICES,))]
        + [dma((SLICES, 6)), dma((SLICES, 6))]
        + [dma((SLICES, 3)), dma((SLICES, 3)), dma((SLICES,)), dma((SLICES,))]
        + [dma((modes - 1,)), dma((modes - 1,))]
        + [dma((2, 4)), dma((2, 4)), dma((2, 4)), dma((4,)), dma((2,)), dma((2,))]
        + [dma((8, 2)), dma((8, 2))],
        compiler_params=pltpu.CompilerParams(collective_id=0, has_side_effects=True, vmem_limit_bytes=55000 * 1024),
        name="ptycho",
    )(positions.reshape(2), object_slices, probe_modes, measured, mats)


def solution(mesh):
    return jax.shard_map(
        body,
        mesh=mesh,
        in_specs=(
            P(None, None, "ty", "tx"),
            P("mode", None, None, None),
            P("ty", "tx", None, None),
            P("ty", "tx", None, None, None),
        ),
        out_specs=P("mode", None, "ty", "tx"),
        check_vma=False,
    )
```

```python
import functools

import numpy as np
import jax
import jax.numpy as jnp
from jax import lax
from jax.experimental import pallas as pl
from jax.experimental.pallas import tpu as pltpu
from jax.sharding import PartitionSpec as P

DET = 128
SLICES = 4
MARGIN = 64
LOCAL = 4
RATE = 0.3
F32 = jnp.float32
BF16 = jnp.bfloat16


def real_block(matrix):
    return np.block([[matrix.real, matrix.imag], [-matrix.imag, matrix.real]])


def tables():
    counter = np.arange(DET)
    fourier = np.exp(-2j * np.pi * (np.outer(counter, counter) % DET) / DET) / np.sqrt(DET)
    frequency = np.where(counter < DET // 2, counter, counter - DET).astype(np.float64)
    chirp = np.exp(-1j * RATE * frequency**2 / DET)
    step = fourier.conj() @ (chirp[:, None] * fourier)
    step = (step + step.T) / 2
    out = []
    for matrix in (step, step.conj(), fourier, fourier.conj()):
        block = real_block(matrix).astype(np.float32)
        high = block.astype(jnp.bfloat16)
        low = (block - high.astype(np.float32)).astype(jnp.bfloat16)
        out += [high, low]
    return np.stack(out)


STEP, STEP_BACK, FAR, FAR_BACK = range(4)
CONJ = {STEP: STEP_BACK, STEP_BACK: STEP, FAR: FAR_BACK, FAR_BACK: FAR}


def halves(x):
    high = x.astype(BF16)
    return high, (x - high.astype(F32)).astype(BF16)


def rows(m):
    return slice(m * DET, (m + 1) * DET)


def right_product(mats, which, real, imag):
    rh, rl = halves(real)
    ih, il = halves(imag)
    lhs = jnp.concatenate([rh, ih, rl, il, rh, ih], axis=1)
    high, low = mats[2 * which], mats[2 * which + 1]
    rhs = jnp.concatenate([high, high, low], axis=0)
    return jnp.dot(lhs, rhs, preferred_element_type=F32)


def left_product(mats, which, stacked):
    conj = CONJ[which]
    high, low = mats[2 * conj], mats[2 * conj + 1]
    main = jnp.dot(jnp.concatenate([high, low], axis=0), stacked[: 2 * DET], preferred_element_type=F32)
    rest = jnp.dot(high, stacked[2 * DET :], preferred_element_type=F32)
    return main[: 2 * DET] + main[2 * DET :] + rest


def two_sided(mats, which, fetch, deliver, mid):
    for m in range(LOCAL):
        real, imag = fetch(m)
        out = right_product(mats, which, real, imag)
        rh, rl = halves(out[:, :DET])
        ih, il = halves(out[:, DET:])
        for part, value in enumerate((rh, ih, rl, il)):
            mid[rows(part), rows(m)] = value
    for pair in range(LOCAL // 2):
        out = left_product(mats, which, mid[:, pair * 2 * DET : (pair + 1) * 2 * DET])
        for k in range(2):
            deliver(2 * pair + k, out[:DET, rows(k)], out[DET:, rows(k)])

MESH = pl.DeviceIdType.MESH
HALF = DET // 2
BLOCK = HALF // 2
EXTRA = 16
STRAIGHT = ((0, slice(0, HALF)), (1, slice(0, EXTRA)))


def lane_low(shape):
    return lax.broadcasted_iota(jnp.int32, shape, len(shape) - 1) < HALF


def turned(x):
    return pltpu.roll(x, HALF, x.ndim - 1)


def packed_edges(strip):
    first, second = strip[:BLOCK], strip[BLOCK:]
    low = lane_low(first.shape)
    left_edge = jnp.where(low, first, turned(second))
    right_edge = jnp.where(low, turned(first), second)
    return left_edge, right_edge


def unpacked_sides(from_left, from_right):
    low = lane_low(from_left.shape)
    first = jnp.where(low, from_right, turned(from_left))
    second = jnp.where(low, turned(from_right), from_left)
    return first, second


def packed_sides(strip):
    half = strip.shape[0] // 2
    upper, lower = strip[:half], strip[half:]
    low = lane_low(upper.shape)
    return jnp.where(low, turned(upper), lower), jnp.where(low, upper, turned(lower))


def unpacked_halves(from_left, from_right):
    low = lane_low(from_left.shape)
    return jnp.where(low, from_left, turned(from_right)), jnp.where(low, turned(from_left), from_right)


LEFT, RIGHT, UP, DOWN, UP_CORNER, DOWN_CORNER = range(6)


def kernel(
    pos_ref, obj_in, probe_in, measured_in, mats_in, out,
    obj, probe, measured, mats, pk, rs, rl, vt, cr, ext, window, psi, far, part, others, mid, pulled, term, collected, joint, parts, middle, vp, hp, cp, gv, gh, gc,
    load, halo_send, halo_recv, cross_send, cross_recv, relay_send, relay_recv, mode_send, mode_recv, collect_send, collect_recv, joint_send, joint_recv, partner_send, partner_recv, grad_send, grad_recv,
):
    mode, ty, tx = lax.axis_index("mode"), lax.axis_index("ty"), lax.axis_index("tx")
    modes, tys, txs = lax.axis_size("mode"), lax.axis_size("ty"), lax.axis_size("tx")
    has = {LEFT: tx > 0, RIGHT: tx < txs - 1, UP: ty > 0, DOWN: ty < tys - 1}
    has[UP_CORNER], has[DOWN_CORNER] = has[UP], has[DOWN]
    cross_right, cross_left = tx == txs // 2 - 1, tx == txs // 2
    mirror = modes - 1 - mode
    left_mode = jnp.where(cross_left, mirror, mode)
    right_mode = jnp.where(cross_right, mirror, mode)
    target = {
        LEFT: {"mode": left_mode, "ty": ty, "tx": tx - 1},
        RIGHT: {"mode": right_mode, "ty": ty, "tx": tx + 1},
        UP: {"mode": mode, "ty": ty - 1, "tx": tx},
        DOWN: {"mode": mode, "ty": ty + 1, "tx": tx},
    }
    crossing = {LEFT: cross_left, RIGHT: cross_right}
    relay_tx = {LEFT: txs - 1, RIGHT: 0}
    relaying = {LEFT: tx == relay_tx[LEFT], RIGHT: tx == relay_tx[RIGHT]}
    landing_tx = {LEFT: txs // 2 - 1, RIGHT: txs // 2}
    direct = {LEFT: {"mode": mode, "ty": ty, "tx": tx - 1}, RIGHT: {"mode": mode, "ty": ty, "tx": tx + 1}}

    def peer(step):
        return {"mode": lax.rem(mode + step, modes), "ty": ty, "tx": tx}

    barrier = pltpu.get_barrier_semaphore()
    count = jnp.int32(modes - 1)
    for side in (LEFT, RIGHT, UP, DOWN):
        count = count + has[side].astype(jnp.int32)

        @pl.when(has[side])
        def _():
            pl.semaphore_signal(barrier, inc=1, device_id=target[side], device_id_type=MESH)

    for side, cross in ((LEFT, cross_left), (RIGHT, cross_right)):
        far_pair = jnp.logical_and(cross, has[side])
        count = count + far_pair.astype(jnp.int32)

        @pl.when(far_pair)
        def _():
            pl.semaphore_signal(barrier, inc=1, device_id=direct[side], device_id_type=MESH)

    for side in (LEFT, RIGHT):
        from_relay, from_landing = crossing[side], relaying[side]
        count = count + from_relay.astype(jnp.int32) + from_landing.astype(jnp.int32)

        @pl.when(relaying[side])
        def _():
            sender = {"mode": mode, "ty": ty, "tx": landing_tx[1 - side]}
            pl.semaphore_signal(barrier, inc=1, device_id=sender, device_id_type=MESH)

        @pl.when(tx == landing_tx[side])
        def _():
            relay = {"mode": mirror, "ty": ty, "tx": relay_tx[side]}
            pl.semaphore_signal(barrier, inc=1, device_id=relay, device_id_type=MESH)

    for step in range(1, modes):
        pl.semaphore_signal(barrier, inc=1, device_id=peer(step), device_id_type=MESH)
    object_loads = [pltpu.make_async_copy(obj_in.at[s], obj.at[s], load.at[3 + s]) for s in range(SLICES)]
    loads = [pltpu.make_async_copy(src, dst, load.at[i]) for i, (src, dst) in enumerate(((probe_in, probe), (mats_in, mats), (measured_in, measured)))]
    for copy in object_loads + loads:
        copy.start()

    for side in (LEFT, RIGHT):

        @pl.when(jnp.logical_not(has[side]))
        def _():
            rs[:, side] = jnp.zeros_like(rs[:, side])
            gh[side] = jnp.zeros_like(gh[side])
            gc[:, side] = jnp.zeros_like(gc[:, side])

    for side in (UP, DOWN):

        @pl.when(jnp.logical_not(has[side]))
        def _():
            vt[:, side - UP] = jnp.zeros_like(vt[:, side - UP])
            cr[:, side - UP] = jnp.zeros_like(cr[:, side - UP])
            gv[side - UP] = jnp.zeros_like(gv[side - UP])
            gc[side - UP] = jnp.zeros_like(gc[side - UP])

    def pack(s):
        object_loads[s].wait()
        for c in range(2):
            for b in range(2):
                left_edge, right_edge = packed_edges(obj[s, c, b * HALF : (b + 1) * HALF])
                pk[s, LEFT, c, b * BLOCK : (b + 1) * BLOCK] = left_edge
                pk[s, RIGHT, c, b * BLOCK : (b + 1) * BLOCK] = right_edge

    pack(0)
    pl.semaphore_wait(barrier, count)

    opposite = {LEFT: RIGHT, RIGHT: LEFT, UP: DOWN, DOWN: UP, UP_CORNER: DOWN_CORNER, DOWN_CORNER: UP_CORNER}

    def landing(s, kind):
        if kind in (LEFT, RIGHT):
            return rs.at[s, kind]
        if kind in (UP, DOWN):
            return vt.at[s, kind - UP]
        return cr.at[s, kind - UP_CORNER]

    def source(s, kind):
        if kind in (LEFT, RIGHT):
            return pk.at[s, kind]
        if kind in (UP, DOWN):
            return obj.at[s, :, (kind - UP) * HALF : (kind - UP + 1) * HALF]
        return rs.at[s, :, :, (kind - UP_CORNER) * BLOCK : (kind - UP_CORNER + 1) * BLOCK]

    def halo_copy(s, kind):
        return pltpu.make_async_remote_copy(
            src_ref=source(s, kind),
            dst_ref=landing(s, opposite[kind]),
            send_sem=halo_send.at[s, kind],
            recv_sem=halo_recv.at[s, opposite[kind]],
            device_id=target[kind if kind < UP_CORNER else kind - 2],
            device_id_type=MESH,
        )

    def straight_copy(s, kind, i):
        return pltpu.make_async_remote_copy(
            src_ref=pk.at[(s, kind, *STRAIGHT[i])],
            dst_ref=rs.at[(s, opposite[kind], *STRAIGHT[i])],
            send_sem=cross_send.at[s, 2 * i],
            recv_sem=cross_recv.at[s, 2 * i],
            device_id=target[kind],
            device_id_type=MESH,
        )

    def detour_copy(s, kind):
        return pltpu.make_async_remote_copy(
            src_ref=pk.at[s, kind, 1, EXTRA:],
            dst_ref=rl.at[s],
            send_sem=cross_send.at[s, 1],
            recv_sem=relay_recv.at[s],
            device_id={"mode": mode, "ty": ty, "tx": relay_tx[kind]},
            device_id_type=MESH,
        )

    def onward_copy(s, kind):
        return pltpu.make_async_remote_copy(
            src_ref=rl.at[s],
            dst_ref=rs.at[s, opposite[kind], 1, EXTRA:],
            send_sem=relay_send.at[s],
            recv_sem=cross_recv.at[s, 1],
            device_id={"mode": mirror, "ty": ty, "tx": landing_tx[kind]},
            device_id_type=MESH,
        )

    def near(kind):
        return jnp.logical_and(has[kind], jnp.logical_not(crossing[kind])) if kind in crossing else has[kind]

    def start_halo(s, kind):
        @pl.when(near(kind))
        def _():
            halo_copy(s, kind).start()

        if kind in crossing:

            @pl.when(crossing[kind])
            def _():
                straight_copy(s, kind, 0).start()
                straight_copy(s, kind, 1).start()
                detour_copy(s, kind).start()

    def await_halo(s, kind):
        @pl.when(near(kind))
        def _():
            halo_copy(s, opposite[kind]).wait_recv()

        if kind in crossing:

            @pl.when(crossing[kind])
            def _():
                straight_copy(s, opposite[kind], 0).wait_recv()
                straight_copy(s, opposite[kind], 1).wait_recv()
                onward_copy(s, opposite[kind]).wait_recv()

    def relay(s):
        for kind in (LEFT, RIGHT):

            @pl.when(relaying[kind])
            def _():
                detour_copy(s, kind).wait_recv()
                onward_copy(s, kind).start()

    for s in range(SLICES):
        if s + 1 < SLICES:
            pack(s + 1)
        for kind in (RIGHT, LEFT, UP, DOWN):
            start_halo(s, kind)

    def relay_corners(s):
        await_halo(s, LEFT)
        await_halo(s, RIGHT)
        start_halo(s, UP_CORNER)
        start_halo(s, DOWN_CORNER)

    row, col = pos_ref[0], pos_ref[1]
    here, there = (lax.broadcasted_iota(jnp.int32, (DET, 2 * DET), d) for d in range(2))
    pick_rows = jnp.where(there == here + row, 1.0, 0.0).astype(BF16)
    offset = here + (col + 2 * DET - HALF)
    offset = jnp.where(offset >= 2 * DET, offset - 2 * DET, offset)
    pick_cols = jnp.where(there == offset, 1.0, 0.0).astype(BF16)
    here, there = (lax.broadcasted_iota(jnp.int32, (2 * DET, DET), d) for d in range(2))
    put_rows = jnp.where(here == there + row, 1.0, 0.0).astype(BF16)
    offset = there + (col + 2 * DET - HALF)
    offset = jnp.where(offset >= 2 * DET, offset - 2 * DET, offset)
    put_cols = jnp.where(here == offset, 1.0, 0.0).astype(BF16)

    def twice(x, axis):
        return jnp.concatenate([x, x], axis=axis)

    def both(x, axis):
        return jnp.concatenate(halves(x), axis=axis)

    def dot(x, y):
        return jnp.dot(x, y, preferred_element_type=F32)

    def build_window(s):
        for kind in (UP, DOWN, UP_CORNER, DOWN_CORNER):
            await_halo(s, kind)
        for c in range(2):
            for side in range(2):
                at = side * 3 * HALF
                ext[c, at : at + HALF, :DET] = vt[s, side, c]
                first, second = unpacked_sides(cr[s, side, LEFT, c], cr[s, side, RIGHT, c])
                ext[c, at : at + BLOCK, DET:] = first
                ext[c, at + BLOCK : at + HALF, DET:] = second
            ext[c, HALF : 3 * HALF, :DET] = obj[s, c]
            for b in range(2):
                block = slice(b * BLOCK, (b + 1) * BLOCK)
                first, second = unpacked_sides(rs[s, LEFT, c, block], rs[s, RIGHT, c, block])
                at = HALF + b * HALF
                ext[c, at : at + BLOCK, DET:] = first
                ext[c, at + BLOCK : at + HALF, DET:] = second
            band = dot(twice(pick_rows, 1), both(ext[c], 0))
            window[s, c] = dot(both(band, 1), twice(put_cols, 0))

    relay(0)
    relay_corners(0)
    for s in range(SLICES):
        if s + 1 < SLICES:
            relay_corners(s + 1)
        if s == 0:
            for ahead in range(1, SLICES):
                relay(ahead)
        build_window(s)
        if s == 0:
            for copy in loads:
                copy.wait()

        def fetch(m):
            if s == 0:
                real, imag = probe[m, 0], probe[m, 1]
            else:
                real, imag = psi[s - 1, 0, rows(m)], psi[s - 1, 1, rows(m)]
            wr, wi = window[s, 0], window[s, 1]
            return real * wr - imag * wi, real * wi + imag * wr

        def deliver(m, real, imag):
            if s + 1 < SLICES:
                psi[s, 0, rows(m)] = real
                psi[s, 1, rows(m)] = imag
            else:
                far[0, rows(m)] = real
                far[1, rows(m)] = imag
                power = real * real + imag * imag
                part[...] = power if m == 0 else part[...] + power

        two_sided(mats, STEP if s + 1 < SLICES else FAR, fetch, deliver, mid)

    first, last = mode == 0, mode == modes - 1
    inner, lower = jnp.logical_not(jnp.logical_or(first, last)), mode < modes // 2

    def mode_copy(step):
        return pltpu.make_async_remote_copy(
            src_ref=part,
            dst_ref=others.at[step - 1],
            send_sem=mode_send.at[step - 1],
            recv_sem=mode_recv.at[step - 1],
            device_id=peer(step),
            device_id_type=MESH,
        )

    for peer_mode in (jnp.where(lower, 3, 0), jnp.where(lower, 2, 1), mode + 1 - 2 * lax.rem(mode, 2)):
        mode_copy(lax.rem(peer_mode - mode + modes, modes)).start()
    whole = part[...]
    for step in range(1, modes):
        mode_copy(step).wait_recv()
        whole = whole + others[step - 1]
    weight = 1.0 - measured[0, 0, 0] / jnp.maximum(jnp.sqrt(whole), 1.0)

    outer, collector = jnp.logical_or(first, last), jnp.where(lower, 1, 2)

    def far_slice(low_pair, i):
        return SLICES - 1 - i if low_pair else 1 - i

    def piece(q):
        return q // 2, pl.ds(q % 2 * HALF, HALF)

    def collect_copy(low_pair, i, q):
        return pltpu.make_async_remote_copy(
            src_ref=term.at[(far_slice(low_pair, i), *piece(q))],
            dst_ref=collected.at[(i, *piece(q))],
            send_sem=collect_send.at[i, q],
            recv_sem=collect_recv.at[i, q],
            device_id={"mode": collector, "ty": ty, "tx": tx},
            device_id_type=MESH,
        )

    def pair_sum_copy(low_pair, i, q):
        return pltpu.make_async_remote_copy(
            src_ref=joint.at[(i, *piece(q))],
            dst_ref=parts.at[(1, *piece(q))],
            send_sem=joint_send.at[i, q],
            recv_sem=joint_recv.at[q],
            device_id={"mode": far_slice(low_pair, i), "ty": ty, "tx": tx},
            device_id_type=MESH,
        )

    def partner_copy(owner, c):
        return pltpu.make_async_remote_copy(
            src_ref=term.at[owner, c],
            dst_ref=parts.at[0, c],
            send_sem=partner_send.at[c],
            recv_sem=partner_recv.at[c],
            device_id={"mode": owner, "ty": ty, "tx": tx},
            device_id_type=MESH,
        )

    def send_far(low_pair, i, pieces=(0, 1, 2, 3)):
        @pl.when(first if low_pair else last)
        def _():
            for q in pieces:
                collect_copy(low_pair, i, q).start()

    def send_partner(owner):
        @pl.when(mode == (owner ^ 1))
        def _():
            for c in range(2):
                partner_copy(owner, c).start()

    def join(low_pair, i, pieces=(0, 1, 2, 3)):
        s = far_slice(low_pair, i)
        for q in pieces:
            collect_copy(low_pair, i, q).wait_recv()
            at = piece(q)
            joint[(i, *at)] = collected[(i, *at)] + term[(s, *at)]
            pair_sum_copy(low_pair, i, q).start()

    for s in reversed(range(SLICES)):

        def fetch(m):
            if s == SLICES - 1:
                return weight * far[0, rows(m)], weight * far[1, rows(m)]
            return pulled[0, rows(m)], pulled[1, rows(m)]

        def deliver(m, real, imag):
            if s == 0:
                pr, pi = probe[m, 0], probe[m, 1]
            else:
                pr, pi = psi[s - 1, 0, rows(m)], psi[s - 1, 1, rows(m)]
            tr, ti = pr * real + pi * imag, pr * imag - pi * real
            term[s, 0] = tr if m == 0 else term[s, 0] + tr
            term[s, 1] = ti if m == 0 else term[s, 1] + ti
            if s > 0:
                wr, wi = window[s, 0], window[s, 1]
                pulled[0, rows(m)] = wr * real + wi * imag
                pulled[1, rows(m)] = wr * imag - wi * real

        two_sided(mats, FAR_BACK if s == SLICES - 1 else STEP_BACK, fetch, deliver, mid)

        if s == 3:
            send_far(True, 0)
            send_partner(3)
        elif s == 2:
            send_far(True, 1)
        elif s == 1:
            send_partner(1)
            send_far(False, 0, (0, 1))
        else:
            send_far(False, 1)
            send_partner(0)
            send_far(False, 0, (2, 3))
            send_partner(2)

    for low_pair in (True, False):

        @pl.when(mode == (1 if low_pair else 2))
        def _():
            join(low_pair, 0, (0, 1))
            if low_pair:
                join(low_pair, 0, (2, 3))
                join(low_pair, 1)
            else:
                join(low_pair, 1)
                join(low_pair, 0, (2, 3))

    def place(c):
        partner_copy(0, c).wait_recv()
        for q in range(2 * c, 2 * c + 2):
            pair_sum_copy(True, 0, q).wait_recv()
        mine = term[mode, c] + parts[0, c] + parts[1, c]
        tall = dot(twice(put_rows, 1), both(mine, 0))
        placed = dot(both(tall, 1), twice(pick_cols, 0))
        middle[c] = placed[HALF : 3 * HALF, :DET]
        for v in range(2):
            at = 3 * v * HALF
            vp[v, c] = placed[at : at + HALF, :DET]
            cp[v, LEFT, c], cp[v, RIGHT, c] = packed_sides(placed[at : at + HALF, DET:])
        hp[LEFT, c], hp[RIGHT, c] = packed_sides(placed[HALF : 3 * HALF, DET:])

    def grad_has(v, h):
        if v is None:
            return has[h]
        return has[UP + v] if h is None else jnp.logical_and(has[UP + v], has[h])

    def grad_copy(v, h, c):
        if v is None:
            src, dst, i = hp.at[h, c], gh.at[1 - h, c], h
        elif h is None:
            src, dst, i = vp.at[v, c], gv.at[1 - v, c], 2 + v
        else:
            src, dst, i = cp.at[v, h, c], gc.at[1 - v, 1 - h, c], 4 + 2 * v + h
        return pltpu.make_async_remote_copy(
            src_ref=src,
            dst_ref=dst,
            send_sem=grad_send.at[i, c],
            recv_sem=grad_recv.at[i, c],
            device_id={"mode": mode, "ty": ty if v is None else ty + 2 * v - 1, "tx": tx if h is None else tx + 2 * h - 1},
            device_id_type=MESH,
        )

    directions = [(None, 1), (0, 1), (1, 1), (None, 0), (0, 0), (1, 0), (0, None), (1, None)]
    for c in range(2):
        place(c)
        for early in (True, False):
            for v, h in directions:
                if h is None and early:
                    continue
                when = grad_has(v, h)
                if h is not None:
                    when = jnp.logical_and(when, crossing[h] if early else jnp.logical_not(crossing[h]))

                @pl.when(when)
                def _():
                    grad_copy(v, h, c).start()

    for v, h in reversed(directions):
        @pl.when(grad_has(v, h))
        def _():
            for c in range(2):
                grad_copy(v if v is None else 1 - v, h if h is None else 1 - h, c).wait_recv()

    for c in range(2):
        for v in range(2):
            half = slice(v * HALF, (v + 1) * HALF)
            sides = unpacked_halves(gh[LEFT, c], gh[RIGHT, c])[v]
            corners = jnp.concatenate(unpacked_halves(gc[v, LEFT, c], gc[v, RIGHT, c]), axis=0)
            out[0, c, half] = middle[c, half] + gv[v, c] + (sides + corners)

    for v, h in directions:

        @pl.when(grad_has(v, h))
        def _():
            for c in range(2):
                grad_copy(v, h, c).wait_send()

    for kind in range(6):

        @pl.when(near(kind))
        def _():
            for s in range(SLICES):
                halo_copy(s, kind).wait_send()

    for kind in (LEFT, RIGHT):

        @pl.when(crossing[kind])
        def _():
            for s in range(SLICES):
                straight_copy(s, kind, 0).wait_send()
                straight_copy(s, kind, 1).wait_send()
                detour_copy(s, kind).wait_send()

        @pl.when(relaying[kind])
        def _():
            for s in range(SLICES):
                onward_copy(s, kind).wait_send()

    for step in range(1, modes):
        mode_copy(step).wait_send()

    for c in range(2):
        partner_copy(0, c).wait_send()
    for i in range(2):
        for q in range(4):

            @pl.when(outer)
            def _():
                collect_copy(True, i, q).wait_send()

            @pl.when(inner)
            def _():
                pair_sum_copy(True, i, q).wait_send()


VMEM = pl.BlockSpec(memory_space=pltpu.VMEM)
SMEM = pl.BlockSpec(memory_space=pltpu.SMEM)
ANY = pl.BlockSpec(memory_space=pl.ANY)


def body(object_slices, probe_modes, positions, measured):
    mats = jnp.asarray(tables())
    modes = lax.axis_size("mode")
    dma = pltpu.SemaphoreType.DMA
    wave = (LOCAL * DET, DET)
    scratch = dict(
        obj=(SLICES, 2, DET, DET),
        probe=(LOCAL, 2, DET, DET),
        measured=(1, 1, 1, DET, DET),
        mats=(8, 2 * DET, 2 * DET),
        pk=(SLICES, 2, 2, HALF, DET),
        rs=(SLICES, 2, 2, HALF, DET),
        rl=(SLICES, HALF - EXTRA, DET),
        vt=(SLICES, 2, 2, HALF, DET),
        cr=(SLICES, 2, 2, 2, BLOCK, DET),
        ext=(2, 2 * DET, 2 * DET),
        window=(SLICES, 2, DET, DET),
        psi=(SLICES - 1, 2, *wave),
        far=(2, *wave),
        part=(DET, DET),
        others=(modes - 1, DET, DET),
        mid=(4 * DET, LOCAL * DET),
        pulled=(2, *wave),
        term=(SLICES, 2, DET, DET),
        collected=(2, 2, DET, DET),
        joint=(2, 2, DET, DET),
        parts=(2, 2, DET, DET),
        middle=(2, DET, DET),
        vp=(2, 2, HALF, DET),
        hp=(2, 2, HALF, DET),
        cp=(2, 2, 2, BLOCK, DET),
        gv=(2, 2, HALF, DET),
        gh=(2, 2, HALF, DET),
        gc=(2, 2, 2, BLOCK, DET),
    )
    return pl.pallas_call(
        kernel,
        out_shape=jax.ShapeDtypeStruct((1, 2, DET, DET), F32),
        in_specs=[SMEM, ANY, ANY, ANY, ANY],
        out_specs=VMEM,
        scratch_shapes=[pltpu.VMEM(shape, BF16 if name in ("mid", "mats") else F32) for name, shape in scratch.items()]
        + [dma((3 + SLICES,))]
        + [dma((SLICES, 6)), dma((SLICES, 6))]
        + [dma((SLICES, 3)), dma((SLICES, 3)), dma((SLICES,)), dma((SLICES,))]
        + [dma((modes - 1,)), dma((modes - 1,))]
        + [dma((2, 4)), dma((2, 4)), dma((2, 4)), dma((4,)), dma((2,)), dma((2,))]
        + [dma((8, 2)), dma((8, 2))],
        compiler_params=pltpu.CompilerParams(collective_id=0, has_side_effects=True),
        name="ptycho",
    )(positions.reshape(2), object_slices, probe_modes, measured, mats)


def solution(mesh):
    return jax.shard_map(
        body,
        mesh=mesh,
        in_specs=(
            P(None, None, "ty", "tx"),
            P("mode", None, None, None),
            P("ty", "tx", None, None),
            P("ty", "tx", None, None, None),
        ),
        out_specs=P("mode", None, "ty", "tx"),
        check_vma=False,
    )
```
